32 devices in a mesh: dp: 8 (over z, y), tensor: 4 (over x, core).
Axes of the slice: x: 2, y: 2, z: 4, core: 2. Of those that a mesh axis runs over, the one named last changes fastest.
Arguments:
- tokens: bfloat16 [8192, 1024], P(('dp', 'tensor')), may hold values from -16 to 16
- cotangent: bfloat16 [8192, 1024], P(('dp', 'tensor')), may hold values from -16 to 16
- gain_attn: float32 [1024], replicated, may hold values from 0.1 to 1.9
- bias_attn: float32 [1024], replicated, may hold values from -1.75 to 1.75
- gain_mlp: float32 [1024], replicated, may hold values from 0.1 to 1.9
- bias_mlp: float32 [1024], replicated, may hold values from -1.75 to 1.75
- qkv_weight: bfloat16 [1024, 3072], P(None, 'tensor'), may hold values from -0.1875 to 0.1875
- qkv_bias: float32 [3072], P('tensor'), may hold values from -1.75 to 1.75
- out_weight: bfloat16 [1024, 1024], P('tensor'), may hold values from -2.5 to 2.5
- out_bias: float32 [1024], replicated, may hold values from -1.75 to 1.75
- up_weight: bfloat16 [1024, 4096], P(None, 'tensor'), may hold values from -0.1875 to 0.1875
- up_bias: float32 [4096], P('tensor'), may hold values from -1.75 to 1.75
- down_weight: bfloat16 [4096, 1024], P('tensor'), may hold values from -0.09375 to 0.09375
- down_bias: float32 [1024], replicated, may hold values from -1.75 to 1.75
Outputs:
- mixed: bfloat16 [8192, 1024], P(('dp', 'tensor'))
- input_grad: float32 [8192, 1024], P(('dp', 'tensor'))
- gain_attn_grad: float32 [1024], replicated
- bias_attn_grad: float32 [1024], replicated
- gain_mlp_grad: float32 [1024], replicated
- bias_mlp_grad: float32 [1024], replicated
- qkv_weight_grad: float32 [1024, 3072], P(None, 'tensor')
- qkv_bias_grad: float32 [3072], P('tensor')
- out_weight_grad: float32 [1024, 1024], P('tensor')
- out_bias_grad: float32 [1024], replicated
- up_weight_grad: float32 [1024, 4096], P(None, 'tensor')
- up_bias_grad: float32 [4096], P('tensor')
- down_weight_grad: float32 [4096, 1024], P('tensor')
- down_bias_grad: float32 [1024], replicated
- statistics: float32 [3], replicated
The draws below stay inside these ranges and needn't reach their ends.
All inputs are finite; a program needn't handle non-finite values.
Results may differ from the reference program's by a relative error of at most 0.012.
The reference program's roundings to bfloat16 on the way count: a program that leaves them out, or rounds other values in their place, can miss the bound.
Values may be sent and summed in bfloat16 or wider, within the bound.
A program may use at most 192 MiB of HBM per device.

```python
import math
import jax
import jax.numpy as jnp
from jax import lax

D = 1024
HEADS = 16
HD = 64
FF = 4096
ROT = 16
SEQ = 1024
TOKENS = 8192
N_DP = 8


def rising_rows(key):
    key_main, key_row = jax.random.split(key)
    positions = jnp.arange(TOKENS, dtype=jnp.float32) / (TOKENS - 1)
    row_factor = jnp.exp(jax.random.uniform(key_row, (TOKENS, 1), jnp.float32, math.log(0.5), math.log(1.5)))
    base = jax.random.truncated_normal(key_main, -3.0, 3.0, (TOKENS, D), jnp.float32)
    rising = jnp.exp(positions * math.log(3.0))
    return base * (rising[:, None] * row_factor)


def draw_tokens(key, part):
    return rising_rows(jax.random.fold_in(key, 11)).astype(jnp.bfloat16)


def draw_cotangent(key, part):
    return rising_rows(jax.random.fold_in(key, 23)).astype(jnp.bfloat16)


def shard_levels(stream_key, dims, shards, least, high):
    def one(axis_at, shards_of):
        draws = jax.random.uniform(jax.random.fold_in(jax.random.fold_in(stream_key, 6), axis_at), (shards_of,), jnp.float32, least / len(shards), high / len(shards))
        return jnp.repeat(jnp.exp(draws), dims[axis_at] // shards_of).reshape((-1,) + (1,) * (len(dims) - axis_at - 1))

    loudness = one(*shards[0])
    for cut in shards[1:]:
        loudness = loudness * one(*cut)
    return loudness


def gaussian(rng, shape, width, reach, cuts=(), kind=jnp.bfloat16):
    array = jax.random.normal(rng, shape, jnp.float32) * width
    if len(cuts) > 0:
        array = shard_levels(rng, shape, cuts, -0.22, 0.18) * array
    return jnp.clip(array, min=-reach, max=reach).astype(kind)


def setup_inputs(seed: int = 0) -> dict:
    key_list = jax.random.split(jax.random.key(seed), 15)
    return {
        "tokens": draw_tokens(jax.random.fold_in(key_list[14], 71), 0),
        "cotangent": draw_cotangent(jax.random.fold_in(key_list[14], 71), 0),
        "gain_attn": jnp.clip(1.0 + 0.18 * jax.random.normal(key_list[2], (D,), jnp.float32), 0.1, 1.9),
        "bias_attn": gaussian(key_list[3], (D,), 0.3, 1.75, (), jnp.float32),
        "gain_mlp": jnp.clip(1.0 + 0.18 * jax.random.normal(key_list[4], (D,), jnp.float32), 0.1, 1.9),
        "bias_mlp": gaussian(key_list[5], (D,), 0.3, 1.75, (), jnp.float32),
        "qkv_weight": gaussian(key_list[6], (D, 3 * D), D ** -0.5, 0.1875, ((1, 4),)),
        "qkv_bias": gaussian(key_list[7], (3 * D,), 0.3, 1.75, ((0, 4),), jnp.float32),
        "out_weight": gaussian(key_list[8], (D, D), (max(1, 6 * D // SEQ)) ** -0.5, 2.5, ((0, 4),)),
        "out_bias": gaussian(key_list[9], (D,), 0.3, 1.75, (), jnp.float32),
        "up_weight": gaussian(key_list[10], (D, FF), D ** -0.5, 0.1875, ((1, 4),)),
        "up_bias": gaussian(key_list[11], (FF,), 0.3, 1.75, ((0, 4),), jnp.float32),
        "down_weight": gaussian(key_list[12], (FF, D), FF ** -0.5, 0.09375, ((0, 4),)),
        "down_bias": gaussian(key_list[13], (D,), 0.3, 1.75, (), jnp.float32),
    }


epsilon = 1e-05

@jax.custom_vjp
def low(v):
    return lax.optimization_barrier(v.astype(jnp.bfloat16)).astype(jnp.float32)

@jax.custom_vjp
def low_back(v):
    return v

def low_keep(v):
    return (low(v), None)

def low_pass(kept, grad):
    return (grad,)

def back_keep(v):
    return (v, None)

def back_low(kept, grad):
    return (low(grad),)
low.defvjp(low_keep, low_pass)
low_back.defvjp(back_keep, back_low)

def product(left, right):
    return jnp.dot(left, right, precision=lax.Precision.HIGHEST, preferred_element_type=jnp.float32)

def angle_tables(seq_len):
    positions = jnp.arange(seq_len, dtype=jnp.float32)
    inverse = 10000.0 ** (-(jnp.arange(ROT // 2, dtype=jnp.float32) * 2.0 / ROT))
    angles = positions[:, None] * inverse[None, :]
    cosine = jnp.concatenate([jnp.cos(angles), jnp.cos(angles)], axis=-1)[:, None, :]
    sine_part = jnp.concatenate([jnp.sin(angles), jnp.sin(angles)], axis=-1)[:, None, :]
    return (cosine, sine_part)

def rotate(field_in, cosine, sine_part):
    half_rot = ROT // 2
    first_half = field_in[..., :half_rot]
    second = field_in[..., half_rot:ROT]
    turned = jnp.concatenate([-second, first_half], axis=-1)
    return jnp.concatenate([field_in[..., :ROT] * cosine + turned * sine_part, field_in[..., ROT:]], axis=-1)

def attend(queries, keys_all, values_all):
    block_rows = min(512, SEQ)
    key_positions = jnp.arange(SEQ, dtype=jnp.int32)

    def one_block(number):
        offset = number * block_rows
        query_rows = lax.dynamic_slice_in_dim(queries, offset, block_rows, 0)
        scores = low_back(jnp.einsum('qhd,khd->hqk', query_rows, keys_all, precision=lax.Precision.HIGHEST) * HD ** (-0.5))
        allowed = key_positions[None, :] <= (offset + jnp.arange(block_rows, dtype=jnp.int32))[:, None]
        scores = jnp.where(allowed[None], scores, -1e+30)
        soft_rows = jax.nn.softmax(scores, axis=-1)
        return jnp.einsum('hqk,khd->qhd', low(soft_rows), values_all, precision=lax.Precision.HIGHEST)
    context_blocks = lax.map(jax.checkpoint(one_block), jnp.arange(SEQ // block_rows, dtype=jnp.int32))
    return context_blocks.reshape(SEQ, HEADS * HD)

def block_forward(inputs, gain_attn, bias_attn, gain_mlp, bias_mlp, qkv_weight, qkv_bias, out_weight, out_bias, up_weight, up_bias, down_weight, down_bias):
    average = lax.optimization_barrier(jnp.mean(inputs, axis=-1, keepdims=True))
    centred = inputs - average
    spread = lax.optimization_barrier(jnp.mean(centred * centred, axis=-1, keepdims=True))
    normed = centred * lax.rsqrt(spread + epsilon)
    attention_input = low(normed * gain_attn + bias_attn)
    feed_input = low(normed * gain_mlp + bias_mlp)
    projected = low_back(product(attention_input, qkv_weight) + qkv_bias).reshape(SEQ, HEADS, 3, HD)
    cosine, sine_part = angle_tables(SEQ)
    queries = low(rotate(projected[:, :, 0], cosine, sine_part))
    keys_all = low(rotate(projected[:, :, 1], cosine, sine_part))
    values_all = low(projected[:, :, 2])
    context = low_back(low(attend(queries, keys_all, values_all)))
    attention_out = low_back(product(context, out_weight) + out_bias)
    preact = low_back(product(feed_input, up_weight) + up_bias)
    hidden = low(jax.nn.gelu(preact, approximate=False))
    feed_out = low_back(product(hidden, down_weight) + down_bias)
    branch = attention_out + feed_out
    residual_out = inputs + branch
    return (residual_out, (jnp.sum(residual_out * residual_out), jnp.sum(branch * branch)))

def reference(tokens, cotangent, gain_attn, bias_attn, gain_mlp, bias_mlp, qkv_weight, qkv_bias, out_weight, out_bias, up_weight, up_bias, down_weight, down_bias):
    params = tuple((weight_array.astype(jnp.float32) for weight_array in (gain_attn, bias_attn, gain_mlp, bias_mlp, qkv_weight, qkv_bias, out_weight, out_bias, up_weight, up_bias, down_weight, down_bias)))
    inputs = tokens.astype(jnp.float32).reshape(N_DP, SEQ, D)
    incoming = cotangent.astype(jnp.float32).reshape(N_DP, SEQ, D)

    def per_sequence(carried, sequence_pair):
        grad_sums, square_sums = carried
        outputs, pullback, squares = jax.vjp(block_forward, sequence_pair[0], *params, has_aux=True)
        gradients = pullback(sequence_pair[1])
        grad_sums = tuple((left + right for left, right in zip(grad_sums, gradients[1:])))
        square_sums = square_sums + jnp.stack([squares[0], squares[1], jnp.sum(gradients[0] * gradients[0])])
        return ((grad_sums, square_sums), (outputs.astype(jnp.bfloat16), gradients[0]))
    initial = (tuple((jnp.zeros_like(weight_array) for weight_array in params)), jnp.zeros((3,), jnp.float32))
    (grad_sums, square_sums), (mixed_out, input_grad) = lax.scan(per_sequence, initial, (inputs, incoming))
    statistics = jnp.sqrt(square_sums / (TOKENS * D))
    return (mixed_out.reshape(TOKENS, D), input_grad.reshape(TOKENS, D), grad_sums[0], grad_sums[1], grad_sums[2], grad_sums[3], grad_sums[4], grad_sums[5], grad_sums[6], grad_sums[7], grad_sums[8], grad_sums[9], grad_sums[10], grad_sums[11], statistics)
```

```python
import functools
import math

import jax
import jax.numpy as jnp
import numpy as np
from jax import lax
from jax.experimental import pallas as pl
from jax.experimental.pallas import tpu as pltpu
from jax.sharding import PartitionSpec as P

HD = 64
ROT = 16
VMEM_LIMIT = 62 << 20


epsilon = 1e-05


def angle_tables(seq_len):
    positions = jnp.arange(seq_len, dtype=jnp.float32)
    inverse = 10000.0 ** (-(jnp.arange(ROT // 2, dtype=jnp.float32) * 2.0 / ROT))
    angles = positions[:, None] * inverse[None, :]
    cosine = jnp.concatenate([jnp.cos(angles), jnp.cos(angles)], axis=-1)[:, None, :]
    sine_part = jnp.concatenate([jnp.sin(angles), jnp.sin(angles)], axis=-1)[:, None, :]
    return (cosine, sine_part)


def rotate(field_in, cosine, sine_part):
    half_rot = ROT // 2
    first_half = field_in[..., :half_rot]
    second = field_in[..., half_rot:ROT]
    turned = jnp.concatenate([-second, first_half], axis=-1)
    return jnp.concatenate(
        [field_in[..., :ROT] * cosine + turned * sine_part, field_in[..., ROT:]], axis=-1
    )


def unrotate(grad_in, cosine, sine_part):
    half_rot = ROT // 2
    head_part = grad_in[..., :ROT]
    scaled = head_part * sine_part
    turned = jnp.concatenate([scaled[..., half_rot:], -scaled[..., :half_rot]], axis=-1)
    return jnp.concatenate([head_part * cosine + turned, grad_in[..., ROT:]], axis=-1)


def normalize(raw_rows):
    average = jnp.mean(raw_rows, axis=-1, keepdims=True)
    centred = raw_rows - average
    spread = jnp.mean(centred * centred, axis=-1, keepdims=True)
    inverse_root = lax.rsqrt(spread + epsilon)
    return (centred * inverse_root, inverse_root)


def against(left, right):
    return lax.dot_general(
        left, right, (((1,), (1,)), ((), ())), preferred_element_type=jnp.float32
    )


def per_device(
    tokens,
    cotangent,
    gain_attn,
    bias_attn,
    gain_mlp,
    bias_mlp,
    qkv_weight,
    qkv_bias,
    out_weight,
    out_bias,
    up_weight,
    up_bias,
    down_weight,
    down_bias,
):
    own_rows = tokens.shape[0]
    model_width = tokens.shape[1]
    heads_here = out_weight.shape[0] // HD
    score_scale = HD ** (-0.5)
    whole_rows = lax.all_gather(tokens, "tensor", axis=0, tiled=True)
    seq_len = whole_rows.shape[0]
    normed, _ = normalize(whole_rows.astype(jnp.float32))
    attention_input = (normed * gain_attn + bias_attn).astype(jnp.bfloat16)
    feed_input = (normed * gain_mlp + bias_mlp).astype(jnp.bfloat16)
    projected = jnp.dot(attention_input, qkv_weight, preferred_element_type=jnp.float32) + qkv_bias
    projected = projected.reshape(seq_len, heads_here, 3, HD)
    cosine, sine_part = angle_tables(seq_len)
    queries = rotate(projected[:, :, 0], cosine, sine_part).astype(jnp.bfloat16)
    keys_all = rotate(projected[:, :, 1], cosine, sine_part).astype(jnp.bfloat16)
    values_all = projected[:, :, 2].astype(jnp.bfloat16)
    preact = jnp.dot(feed_input, up_weight, preferred_element_type=jnp.float32) + up_bias
    hidden = jax.nn.gelu(preact, approximate=False).astype(jnp.bfloat16)
    block_rows = min(512, seq_len)
    block_total = seq_len // block_rows
    key_positions = jnp.arange(seq_len, dtype=jnp.int32)

    def causal_mask(offset):
        return key_positions[None, :] <= (offset + jnp.arange(block_rows, dtype=jnp.int32))[:, None]

    def forward_block(number):
        offset = number * block_rows
        query_rows = lax.dynamic_slice_in_dim(queries, offset, block_rows, 0)
        scores = (
            jnp.einsum("qhd,khd->hqk", query_rows, keys_all, preferred_element_type=jnp.float32)
            * score_scale
        )
        scores = jnp.where(causal_mask(offset)[None], scores, -1e30)
        highest = jnp.max(scores, axis=-1, keepdims=True)
        weights = jnp.exp(scores - highest)
        totals = jnp.sum(weights, axis=-1, keepdims=True)
        soft_rows = (weights / totals).astype(jnp.bfloat16)
        context_rows = jnp.einsum(
            "hqk,khd->qhd", soft_rows, values_all, preferred_element_type=jnp.float32
        ).astype(jnp.bfloat16)
        log_totals = (highest + jnp.log(totals))[:, :, 0].T
        return (context_rows, log_totals)

    context_blocks, log_blocks = lax.map(forward_block, jnp.arange(block_total, dtype=jnp.int32))
    context = context_blocks.reshape(seq_len, heads_here * HD)
    log_sums = log_blocks.reshape(seq_len, heads_here)
    context_rows = context
    branch = lax.psum_scatter(
        jnp.dot(context_rows, out_weight, preferred_element_type=jnp.float32)
        + jnp.dot(hidden, down_weight, preferred_element_type=jnp.float32),
        "tensor",
        scatter_dimension=0,
        tiled=True,
    )
    branch = branch + out_bias + down_bias
    residual_out = tokens.astype(jnp.float32) + branch
    mixed_out = residual_out.astype(jnp.bfloat16)
    forward_squares = jnp.stack([jnp.sum(residual_out * residual_out), jnp.sum(branch * branch)])
    forward_totals = lax.psum(forward_squares, ("dp", "tensor"))
    upstream = lax.all_gather(cotangent, "tensor", axis=0, tiled=True)
    out_weight_grad = jnp.einsum("sa,sd->ad", context, upstream, preferred_element_type=jnp.float32)
    down_weight_grad = jnp.einsum("sf,sd->fd", hidden, upstream, preferred_element_type=jnp.float32)
    context_grad = against(upstream, out_weight).astype(jnp.bfloat16)
    hidden_grad = against(upstream, down_weight)
    normal_cdf = 0.5 * (1.0 + lax.erf(preact * 0.5**0.5))
    density = jnp.exp(-0.5 * preact * preact) * (1.0 / math.sqrt(2.0 * math.pi))
    preact_grad = (hidden_grad * (normal_cdf + preact * density)).astype(jnp.bfloat16)
    context_grad3 = context_grad.reshape(seq_len, heads_here, HD)

    def backward_block(carried, number):
        key_grad, value_grad = carried
        offset = number * block_rows
        query_rows = lax.dynamic_slice_in_dim(queries, offset, block_rows, 0)
        grad_rows = lax.dynamic_slice_in_dim(context_grad3, offset, block_rows, 0)
        log_rows = lax.dynamic_slice_in_dim(log_sums, offset, block_rows, 0).T
        scores = (
            jnp.einsum("qhd,khd->hqk", query_rows, keys_all, preferred_element_type=jnp.float32)
            * score_scale
        )
        soft_full = jnp.exp(
            jnp.where(causal_mask(offset)[None], scores - log_rows[:, :, None], -1e30)
        )
        prob_grad = jnp.einsum(
            "qhd,khd->hqk", grad_rows, values_all, preferred_element_type=jnp.float32
        )
        deltas = jnp.sum(soft_full * prob_grad, axis=-1, keepdims=True)
        score_grad = (soft_full * (prob_grad - deltas)).astype(jnp.bfloat16)
        query_grad = (
            jnp.einsum("hqk,khd->qhd", score_grad, keys_all, preferred_element_type=jnp.float32)
            * score_scale
        )
        key_grad = (
            key_grad
            + jnp.einsum("hqk,qhd->khd", score_grad, query_rows, preferred_element_type=jnp.float32)
            * score_scale
        )
        value_grad = value_grad + jnp.einsum(
            "hqk,qhd->khd",
            soft_full.astype(jnp.bfloat16),
            grad_rows,
            preferred_element_type=jnp.float32,
        )
        return ((key_grad, value_grad), query_grad)

    empty = jnp.zeros((seq_len, heads_here, HD), jnp.float32)
    (key_grad, value_grad), query_blocks = lax.scan(
        backward_block, (empty, empty), jnp.arange(block_total, dtype=jnp.int32)
    )
    query_grad = unrotate(query_blocks.reshape(seq_len, heads_here, HD), cosine, sine_part)
    key_grad = unrotate(key_grad, cosine, sine_part)
    qkv_grad = (
        jnp.stack([query_grad, key_grad, value_grad], axis=2)
        .reshape(seq_len, 3 * heads_here * HD)
        .astype(jnp.bfloat16)
    )
    qkv_weight_grad = jnp.einsum(
        "sd,sc->dc", attention_input, qkv_grad, preferred_element_type=jnp.float32
    )
    qkv_bias_grad = jnp.sum(qkv_grad, axis=0, dtype=jnp.float32)
    up_weight_grad = jnp.einsum(
        "sd,sf->df", feed_input, preact_grad, preferred_element_type=jnp.float32
    )
    up_bias_grad = jnp.sum(preact_grad, axis=0, dtype=jnp.float32)
    own_normed, own_scale = normalize(tokens.astype(jnp.float32))
    attention_back = against(qkv_grad, qkv_weight)
    feed_back = against(preact_grad, up_weight)
    gain_terms = jnp.stack(
        [
            jnp.sum(normed * attention_back, axis=0),
            jnp.sum(attention_back, axis=0),
            jnp.sum(normed * feed_back, axis=0),
            jnp.sum(feed_back, axis=0),
        ]
    )
    normed_grad = lax.psum_scatter(
        (attention_back * gain_attn + feed_back * gain_mlp).astype(jnp.bfloat16),
        "tensor",
        scatter_dimension=0,
        tiled=True,
    ).astype(jnp.float32)
    centred_term = (
        normed_grad
        - jnp.mean(normed_grad, axis=-1, keepdims=True)
        - own_normed * jnp.mean(normed_grad * own_normed, axis=-1, keepdims=True)
    )
    input_grad = own_scale * centred_term + cotangent.astype(jnp.float32)
    (
        qkv_weight_grad,
        qkv_bias_grad,
        out_weight_grad,
        up_weight_grad,
        up_bias_grad,
        down_weight_grad,
    ) = lax.psum(
        (
            qkv_weight_grad,
            qkv_bias_grad,
            out_weight_grad,
            up_weight_grad,
            up_bias_grad,
            down_weight_grad,
        ),
        "dp",
    )
    bias_rows = jnp.sum(cotangent, axis=0, dtype=jnp.float32)
    grad_square = jnp.sum(input_grad * input_grad)
    gain_totals, bias_totals, grad_total = lax.psum(
        (gain_terms, bias_rows, grad_square), ("dp", "tensor")
    )
    square_totals = jnp.concatenate([forward_totals, grad_total[None]])
    elements = own_rows * model_width * lax.axis_size("dp") * lax.axis_size("tensor")
    statistics = jnp.sqrt(square_totals / elements)
    return (
        mixed_out,
        input_grad,
        gain_totals[0],
        gain_totals[1],
        gain_totals[2],
        gain_totals[3],
        qkv_weight_grad,
        qkv_bias_grad,
        out_weight_grad,
        bias_totals,
        up_weight_grad,
        up_bias_grad,
        down_weight_grad,
        bias_totals,
        statistics,
    )


F32 = jnp.float32
BF16 = jnp.bfloat16
MESH = pl.DeviceIdType.MESH
TILE = 256
RING_X = 4


def dot_nn(left, right):
    return jnp.dot(left, right, preferred_element_type=F32)


def dot_nt(left, right):
    return lax.dot_general(left, right, (((1,), (1,)), ((), ())), preferred_element_type=F32)


def dot_tn(left, right):
    return lax.dot_general(left, right, (((0,), (0,)), ((), ())), preferred_element_type=F32)


def fused_kernel(
    ring,
    tok, cot, ga, ba, gm, bm, bo, bd, bqkv, bup, wqkv_h, wout_h, wup_h, wdn_h, cos_a, sin_a, cos_b, sin_b,
    mixed, igrad, gd_o, gu_o, gq_o, go_o, sv_o,
    T, C, AI, FI, HID, GP, PG, QG, QH, KH, VH, CGH, CTXH, CTX, DQ, DKT, DVT, SCO, DPS, COS, SIN,
    WQKV, WOUT, WUP, WDN, RSB, GB, PSC, PART, RA, RB, SV, ES, EX,
    lsem, g_s, g_r, r_s, r_r, b_s, b_r, e_s, e_r, o_s, p_s,
):
    rows = tok.shape[0]
    width = tok.shape[1]
    seq = T.shape[0]
    heads = QH.shape[0]
    hidden_width = WUP.shape[1]
    half_rows = rows // 2
    blocks = seq // TILE
    scale = HD ** (-0.5)
    dp = lax.axis_index("dp")
    t = lax.axis_index("tensor")
    core = lax.rem(t, 2)
    x = lax.div(t, 2)
    depth = ring // 2
    y = lax.rem(dp, 2)
    z = lax.div(dp, 2)
    at = z + y * (2 * depth - 1 - 2 * z)

    def ring_device(place):
        ny = lax.div(place, depth)
        return (2 * (place + ny * (2 * depth - 1 - 2 * place)) + ny, t)

    following = ring_device(lax.rem(at + 1, ring))
    previous = ring_device(lax.rem(at + ring - 1, ring))
    onward = (following, previous)
    core_mate = (dp, t + 1 - 2 * core)
    x_block = 2 * (1 - x) + core
    x_mate = (dp, x_block)

    def remote(src, dst, send, recv, device):
        return pltpu.make_async_remote_copy(
            src_ref=src, dst_ref=dst, send_sem=send, recv_sem=recv, device_id=device, device_id_type=MESH
        )

    def gather(which, kind):
        src, full = (tok, T) if which == 0 else (cot, C)
        sems = (g_s.at[which, kind], g_r.at[which, kind])
        if kind == 0:
            return remote(src, full.at[pl.ds(t * rows, rows)], *sems, core_mate)
        if kind <= 2:
            off = (kind - 1) * half_rows
            return remote(
                src.at[pl.ds(off, half_rows)], full.at[pl.ds(t * rows + off, half_rows)], *sems, x_mate
            )
        part = full.at[pl.ds(x_block * rows + (kind - 3) * half_rows, half_rows)]
        return remote(part, part, *sems, core_mate)

    local = [
        pltpu.make_async_copy(tok, T.at[pl.ds(t * rows, rows)], lsem.at[0]),
        pltpu.make_async_copy(cot, C.at[pl.ds(t * rows, rows)], lsem.at[1]),
        pltpu.make_async_copy(wqkv_h, WQKV, lsem.at[2]),
        pltpu.make_async_copy(wup_h, WUP, lsem.at[3]),
        pltpu.make_async_copy(wdn_h, WDN, lsem.at[4]),
        pltpu.make_async_copy(wout_h, WOUT, lsem.at[5]),
    ]
    gather(0, 1).start()
    gather(0, 2).start()
    gather(0, 0).start()
    for copy in (local[0], local[2], local[3], local[1], local[4], local[5]):
        copy.start()

    @pl.loop(0, seq // 32)
    def _(a):
        ca, sa = cos_a[pl.ds(a, 1), :], sin_a[pl.ds(a, 1), :]
        cb, sb = cos_b[...], sin_b[...]
        COS[pl.ds(a * 32, 32), :] = ca * cb - sa * sb
        SIN[pl.ds(a * 32, 32), :] = sa * cb + ca * sb

    SV[...] = jnp.zeros_like(SV)

    @pl.loop(0, heads)
    def _(h):
        DKT[h] = jnp.zeros(DKT.shape[1:], F32)
        DVT[h] = jnp.zeros(DVT.shape[1:], F32)

    lane = lax.broadcasted_iota(jnp.int32, (TILE, 128), 1)
    low_lane = jnp.where(lane >= 64, lane - 64, lane)

    def tables(base, group):
        cosine, sine = COS[pl.ds(base, TILE), :], SIN[pl.ds(base, TILE), :]
        if group == 1:
            cosine = jnp.where(lane >= 64, cosine, 1.0)
            sine = jnp.where(lane >= 64, sine, 0.0)
        if group == 2:
            cosine = jnp.where(lane < 64, cosine, 1.0)
            sine = jnp.where(lane < 64, sine, 0.0)
        upper = jnp.where(low_lane >= ROT // 2, sine, 0.0)
        return cosine, upper, sine - upper

    def norm_rows(base, count):
        raw = T[pl.ds(base, count), :].astype(F32)
        centred = raw - jnp.mean(raw, axis=1, keepdims=True)
        inverse_root = lax.rsqrt(jnp.mean(centred * centred, axis=1, keepdims=True) + epsilon)
        return centred * inverse_root, inverse_root

    def forward_block(block):
        base = pl.multiple_of(block * rows, rows)

        @pl.loop(0, rows // 64)
        def _(part):
            off = pl.multiple_of(base + part * 64, 64)
            normed, _ = norm_rows(off, 64)
            AI[pl.ds(off, 64), :] = (normed * ga[...] + ba[...]).astype(BF16)
            FI[pl.ds(off, 64), :] = (normed * gm[...] + bm[...]).astype(BF16)

        for group in range(3 * heads // 2):
            if group % 2 == 0:
                columns = slice(group * 128, group * 128 + 256)
                pair = dot_nn(AI[pl.ds(base, rows), :], WQKV[:, columns]) + bqkv[:, columns]
            value = pair[:, (group % 2) * 128 : (group % 2) * 128 + 128]
            cosine, upper, lower = tables(base, group % 3)
            turned = (
                value * cosine
                - lower * pltpu.roll(value, 128 - ROT // 2, 1)
                + upper * pltpu.roll(value, ROT // 2, 1)
            ).astype(BF16)
            first = 2 * (group // 3)
            left, left_head = ((QH, first), (VH, first), (KH, first + 1))[group % 3]
            right, right_head = ((KH, first), (QH, first + 1), (VH, first + 1))[group % 3]
            left[left_head, pl.ds(base, rows), :] = turned[:, :HD]
            right[right_head, pl.ds(base, rows), :] = turned[:, HD:]

        @pl.loop(0, hidden_width // TILE)
        def _(part):
            columns = pl.ds(pl.multiple_of(part * TILE, TILE), TILE)
            preact = dot_nn(FI[pl.ds(base, rows), :], WUP[:, columns]) + bup[:, columns]
            cdf = 0.5 * (1.0 + lax.erf(preact * 0.5**0.5))
            density = jnp.exp(-0.5 * preact * preact) * (1.0 / math.sqrt(2.0 * math.pi))
            HID[pl.ds(base, rows), columns] = (preact * cdf).astype(BF16)
            GP[pl.ds(base, rows), columns] = cdf + preact * density

    def cotangent_block(block):
        base = pl.multiple_of(block * rows, rows)
        upstream = C[pl.ds(base, rows), :]
        grad = dot_nt(upstream, WOUT[...]).astype(BF16)
        for h in range(heads):
            CGH[h, pl.ds(base, rows), :] = grad[:, h * HD : (h + 1) * HD]

        @pl.loop(0, hidden_width // TILE)
        def _(part):
            columns = pl.ds(pl.multiple_of(part * TILE, TILE), TILE)
            back = dot_nt(C[pl.ds(base, rows), :], WDN[columns, :])
            rounded = (back * GP[pl.ds(base, rows), columns]).astype(BF16)
            PG[pl.ds(base, rows), columns] = rounded
            SV[6:7, columns] += jnp.sum(rounded.astype(F32), axis=0, keepdims=True)

    def attention_unit(unit):
        h = lax.div(unit, blocks)
        own = lax.rem(unit, blocks)
        here = pl.ds(pl.multiple_of(own * TILE, TILE), TILE)
        query = QH[h, here, :]
        grad = CGH[h, here, :]
        query_t = query.astype(F32).T.astype(BF16)
        grad_t = grad.astype(F32).T.astype(BF16)

        def place(number):
            return pl.ds(pl.multiple_of(number * TILE, TILE), TILE)

        def raw(number):
            return dot_nt(query, KH[h, place(number), :]) * scale

        def first(number, top):
            scores = raw(number)
            SCO[:, place(number)] = scores
            return jnp.maximum(top, jnp.max(scores, axis=1, keepdims=True))

        top = lax.fori_loop(0, own, first, jnp.full((TILE, 1), -1e30, F32))
        row_at = lax.broadcasted_iota(jnp.int32, (TILE, TILE), 0)
        column_at = lax.broadcasted_iota(jnp.int32, (TILE, TILE), 1)
        scores = jnp.where(column_at <= row_at, raw(own), -1e30)
        SCO[:, here] = scores
        top = jnp.maximum(top, jnp.max(scores, axis=1, keepdims=True))

        def second(number, total):
            weights = jnp.exp(SCO[:, place(number)] - top)
            SCO[:, place(number)] = weights
            return total + jnp.sum(weights, axis=1, keepdims=True)

        total = lax.fori_loop(0, own + 1, second, jnp.zeros((TILE, 1), F32))
        inverse = 1.0 / total

        def third(number, carried):
            context, delta = carried
            probs = SCO[:, place(number)] * inverse
            value = VH[h, place(number), :]
            context = context + dot_nn(probs.astype(BF16), value)
            prob_grad = dot_nt(grad, value)
            SCO[:, place(number)] = probs
            DPS[:, place(number)] = prob_grad
            return context, delta + jnp.sum(probs * prob_grad, axis=1, keepdims=True)

        context, delta = lax.fori_loop(
            0, own + 1, third, (jnp.zeros((TILE, HD), F32), jnp.zeros((TILE, 1), F32))
        )
        CTXH[h, here, :] = context.astype(BF16)

        def fourth(number, query_grad):
            probs = SCO[:, place(number)]
            score_grad = (probs * (DPS[:, place(number)] - delta)).astype(BF16)
            DKT[h, :, place(number)] += dot_nn(query_t, score_grad)
            DVT[h, :, place(number)] += dot_nn(grad_t, probs.astype(BF16))
            return query_grad + dot_nn(score_grad, KH[h, place(number), :])

        DQ[h, here, :] = scale * lax.fori_loop(0, own + 1, fourth, jnp.zeros((TILE, HD), F32))

    def assemble(block):
        base = pl.multiple_of(block * TILE, TILE)
        here = pl.ds(base, TILE)
        for pair in range(heads // 2):
            one, two = 2 * pair, 2 * pair + 1
            CTX[here, pair * 128 : (pair + 1) * 128] = jnp.concatenate(
                [CTXH[one, here, :], CTXH[two, here, :]], axis=1
            )
            parts = [
                (DQ[one, here, :], scale * DKT[one, :, here].T),
                (DVT[one, :, here].T, DQ[two, here, :]),
                (scale * DKT[two, :, here].T, DVT[two, :, here].T),
            ]
            for group, (left, right) in enumerate(parts):
                grad = jnp.concatenate([left, right], axis=1)
                cosine, upper, lower = tables(base, group)
                turned = (
                    grad * cosine
                    + pltpu.roll(grad * upper, 128 - ROT // 2, 1)
                    - pltpu.roll(grad * lower, ROT // 2, 1)
                ).astype(BF16)
                columns = slice((3 * pair + group) * 128, (3 * pair + group + 1) * 128)
                QG[here, columns] = turned
                SV[7:8, columns] += jnp.sum(turned.astype(F32), axis=0, keepdims=True)

    def order(step):
        flip_core = 1 - lax.div(step, 2)
        flip_x = 1 - lax.rem(step, 2)
        return 2 * lax.rem(x + flip_x, 2) + lax.rem(core + flip_core, 2)

    def to_core(which, slot):
        block = (2 * x + 1 - core) if slot == 0 else (2 * (1 - x) + 1 - core)
        return remote(
            PART.at[which, pl.ds(block * rows, rows)], RA.at[which, slot],
            b_s.at[which, slot], b_r.at[which, slot], core_mate,
        )

    def to_x(which):
        return remote(
            PART.at[which, pl.ds(x_block * rows, rows)], RB.at[which],
            b_s.at[which, 2], b_r.at[which, 2], x_mate,
        )

    def send_after(which, step):
        @pl.when(step == 0)
        def _():
            to_core(which, 1).start()

        @pl.when(step == 1)
        def _():
            to_core(which, 0).start()

    def branch_block(step):
        base = pl.multiple_of(order(step) * rows, rows)
        here = pl.ds(base, rows)

        @pl.loop(0, width // TILE)
        def _(part):
            columns = pl.ds(pl.multiple_of(part * TILE, TILE), TILE)
            PART[0, here, columns] = (
                dot_nn(CTX[here, :], WOUT[:, columns]) + dot_nn(HID[here, :], WDN[:, columns])
            ).astype(BF16)

        send_after(0, step)

    def back_block(step):
        base = pl.multiple_of(order(step) * rows, rows)
        here = pl.ds(base, rows)
        raw = T[here, :].astype(F32)
        average = jnp.mean(raw, axis=1, keepdims=True)
        spread = jnp.mean((raw - average) * (raw - average), axis=1, keepdims=True)
        inverse_root = lax.rsqrt(spread + epsilon)

        @pl.loop(0, width // TILE)
        def _(part):
            columns = pl.ds(pl.multiple_of(part * TILE, TILE), TILE)
            normed = (T[here, columns].astype(F32) - average) * inverse_root
            attention_back = dot_nt(QG[here, :], WQKV[columns, :])
            feed_back = dot_nt(PG[here, :], WUP[columns, :])
            SV[0:1, columns] += jnp.sum(normed * attention_back, axis=0, keepdims=True)
            SV[1:2, columns] += jnp.sum(attention_back, axis=0, keepdims=True)
            SV[2:3, columns] += jnp.sum(normed * feed_back, axis=0, keepdims=True)
            SV[3:4, columns] += jnp.sum(feed_back, axis=0, keepdims=True)
            PART[1, here, columns] = (attention_back * ga[:, columns] + feed_back * gm[:, columns]).astype(BF16)

        send_after(1, step)

    def chip_sum(which):
        to_core(which, 1).wait_recv()
        there = pl.ds(pl.multiple_of(x_block * rows, rows), rows)
        PART[which, there, :] = (PART[which, there, :].astype(F32) + RA[which, 1].astype(F32)).astype(BF16)
        to_x(which).start()

    def finish():
        for which in range(2):
            to_core(which, 0).wait_recv()
            to_x(which).wait_recv()
        SV[4:5, :] = jnp.sum(C[pl.ds(t * rows, rows), :].astype(F32), axis=0, keepdims=True)

        def total(which, off):
            return (
                PART[which, pl.ds(pl.multiple_of(t * rows + off, 64), 64), :].astype(F32)
                + RA[which, 0, pl.ds(off, 64), :].astype(F32)
                + RB[which, pl.ds(off, 64), :].astype(F32)
            )

        def square(value):
            return jnp.sum(jnp.sum(value * value, axis=1, keepdims=True), axis=0, keepdims=True)

        def part(number, sums):
            off = pl.multiple_of(number * 64, 64)
            here = pl.ds(pl.multiple_of(t * rows + off, 64), 64)
            branch = total(0, off) + bo[...] + bd[...]
            residual = T[here, :].astype(F32) + branch
            mixed[pl.ds(off, 64), :] = residual.astype(BF16)
            normed, inverse_root = norm_rows(t * rows + off, 64)
            grad = total(1, off)
            grad = inverse_root * (
                grad
                - jnp.mean(grad, axis=1, keepdims=True)
                - normed * jnp.mean(grad * normed, axis=1, keepdims=True)
            ) + C[here, :].astype(F32)
            igrad[pl.ds(off, 64), :] = grad
            return sums[0] + square(residual), sums[1] + square(branch), sums[2] + square(grad)

        zero = jnp.zeros((1, 1), F32)
        sums = lax.fori_loop(0, rows // 64, part, (zero, zero, zero))
        spot = lax.broadcasted_iota(jnp.int32, (1, width), 1)
        SV[5:6, :] = jnp.where(
            spot == 0, sums[0], jnp.where(spot == 1, sums[1], jnp.where(spot == 2, sums[2], 0.0))
        )

    def exchange(step):
        mate = (
            core_mate,
            x_mate,
            (dp + 1 - 2 * y, t),
            (2 * (z + 1 - 2 * lax.rem(z, 2)) + y, t),
            (2 * lax.rem(z + 2, depth) + y, t),
        )[step]
        return remote(ES.at[step], EX.at[step], e_s.at[step], e_r.at[step], mate)

    def exchange_send(step):
        ES[step] = SV[...]
        exchange(step).start()

    def exchange_receive(step):
        exchange(step).wait_recv()
        if step < 2:
            row = lax.broadcasted_iota(jnp.int32, SV.shape, 0)
            SV[...] += jnp.where(row < 6, EX[step], 0.0)
        else:
            SV[...] += EX[step]

    def chunk(direction, step):
        return lax.rem(at + ring - step, ring) if direction == 0 else lax.rem(at + step, ring)

    def gathered(direction, step):
        return lax.rem(at + 1 + ring - step, ring) if direction == 0 else lax.rem(at + ring - 1 + step, ring)

    def own_partial(segment, step):
        for direction in range(2):
            number = chunk(direction, step)
            columns = pl.ds(pl.multiple_of(number * 128, 128), 128)
            if segment < 2:
                left, right = (HID, C) if segment == 0 else (FI, PG)
                PSC[direction] = dot_tn(left[:, columns], right[:, direction * 512 : (direction + 1) * 512])
            else:
                PSC[direction, :, 0:384] = dot_tn(AI[:, columns], QG[:, direction * 384 : (direction + 1) * 384])
                PSC[direction, :, 384:512] = dot_tn(
                    CTX[:, direction * 128 : (direction + 1) * 128], C[:, columns]
                )

    def scatter(segment, direction, half, step):
        return remote(
            RSB.at[segment, direction, half, step], RSB.at[segment, direction, half, step + 1],
            r_s.at[segment, direction, half, step], r_r.at[segment, direction, half, step], onward[direction],
        )

    def collect(segment, direction, half, step):
        piece = GB.at[segment, direction, half, gathered(direction, step)]
        sem = ring - 1 + step
        return remote(
            piece, piece,
            r_s.at[segment, direction, half, sem], r_r.at[segment, direction, half, sem], onward[direction],
        )

    pieces = [(half, direction) for half in range(2) for direction in range(2)]

    def ring_open(segment):
        own_partial(segment, 0)
        for half, direction in pieces:
            RSB[segment, direction, half, 0] = PSC[direction, :, half * 256 : (half + 1) * 256].astype(BF16)
            scatter(segment, direction, half, 0).start()

    def ring_scatter(segment, step):
        for half, direction in pieces:
            scatter(segment, direction, half, step - 1).wait_recv()
            RSB[segment, direction, half, step] = (
                RSB[segment, direction, half, step].astype(F32)
                + PSC[direction, :, half * 256 : (half + 1) * 256]
            ).astype(BF16)
            scatter(segment, direction, half, step).start()

    def ring_turn(segment):
        last = ring - 1
        for half, direction in pieces:
            scatter(segment, direction, half, last - 1).wait_recv()
            GB[segment, direction, half, gathered(direction, 0)] = (
                RSB[segment, direction, half, last].astype(F32)
                + PSC[direction, :, half * 256 : (half + 1) * 256]
            ).astype(BF16)
            collect(segment, direction, half, 0).start()

    def ring_collect(segment, step):
        for half, direction in pieces:
            collect(segment, direction, half, step - 1).wait_recv()
            collect(segment, direction, half, step).start()

    def ring_close(segment):
        for half, direction in pieces:
            collect(segment, direction, half, ring - 2).wait_recv()

    def out_copies(segment, direction, half, number):
        piece = GB.at[segment, direction, half, number]
        there = pl.ds(number * 128, 128)
        sem = o_s.at[segment, direction, half, number]
        if segment < 2:
            out = gd_o if segment == 0 else gu_o
            return [pltpu.make_async_copy(piece, out.at[there, pl.ds(direction * 512 + half * 256, 256)], sem)]
        if half == 0:
            return [pltpu.make_async_copy(piece, gq_o.at[there, pl.ds(direction * 384, 256)], sem)]
        return [
            pltpu.make_async_copy(
                piece.at[:, pl.ds(0, 128)], gq_o.at[there, pl.ds(direction * 384 + 256, 128)], sem
            ),
            pltpu.make_async_copy(
                piece.at[:, pl.ds(128, 128)], go_o.at[pl.ds(direction * 128, 128), there], p_s.at[direction, number]
            ),
        ]

    def ring_out(segment, action):
        @pl.loop(0, ring)
        def _(number):
            for half, direction in pieces:
                for copy in out_copies(segment, direction, half, number):
                    getattr(copy, action)()

    local[0].wait()
    local[2].wait()
    local[3].wait()

    @pl.loop(0, 4)
    def _(step):
        @pl.when(step == 1)
        def _():
            gather(0, 0).wait_recv()

        @pl.when(step == 2)
        def _():
            gather(0, 1).wait_recv()
            gather(0, 3).start()
            gather(0, 2).wait_recv()
            gather(0, 4).start()
            gather(1, 1).start()
            gather(1, 2).start()
            gather(1, 0).start()

        @pl.when(step == 3)
        def _():
            gather(0, 3).wait_recv()
            gather(0, 4).wait_recv()

        forward_block(2 * lax.rem(x + lax.div(step, 2), 2) + lax.rem(core + lax.rem(step, 2), 2))

    local[1].wait()
    local[4].wait()
    local[5].wait()
    gather(1, 1).wait_recv()
    gather(1, 3).start()
    gather(1, 0).wait_recv()
    gather(1, 2).wait_recv()
    gather(1, 4).start()
    gather(1, 3).wait_recv()
    gather(1, 4).wait_recv()

    turns = ring - 1

    def during(condition, work):
        pl.when(condition)(work)

    ring_open(0)

    @pl.loop(1, turns)
    def _(step):
        own_partial(0, step)
        during(step <= 4, lambda: cotangent_block(step - 1))
        during(step > 4, lambda: attention_unit(step - 5))
        ring_scatter(0, step)

    own_partial(0, turns)
    ring_turn(0)

    @pl.loop(1, turns)
    def _(step):
        attention_unit(step + 1)
        ring_collect(0, step)

    ring_open(1)
    ring_close(0)
    ring_out(0, "start")

    @pl.loop(1, turns)
    def _(step):
        own_partial(1, step)
        attention_unit(step + 7)
        ring_scatter(1, step)

    own_partial(1, turns)
    ring_turn(1)

    @pl.loop(1, turns)
    def _(step):
        during(step <= 2, lambda: attention_unit(step + 13))
        during(step > 2, lambda: assemble(step - 3))
        ring_collect(1, step)

    ring_open(2)
    ring_close(1)
    ring_out(1, "start")

    @pl.loop(1, turns)
    def _(step):
        own_partial(2, step)
        during(step <= 4, lambda: branch_block(step - 1))
        during(step > 4, lambda: back_block(step - 5))
        during(step == 6, lambda: chip_sum(0))
        ring_scatter(2, step)

    own_partial(2, turns)
    ring_turn(2)

    @pl.loop(1, turns)
    def _(step):
        during(step <= 2, lambda: back_block(step + 1))
        during(step == 3, lambda: chip_sum(1))
        during(step == 6, finish)
        ring_collect(2, step)

    exchange_send(0)
    ring_close(2)
    ring_out(2, "start")
    exchange_receive(0)
    for step in range(1, 5):
        exchange_send(step)
        exchange_receive(step)
    sv_o[...] = SV[...]

    for which in range(2):
        for kind in range(5):
            gather(which, kind).wait_send()
        for slot in range(2):
            to_core(which, slot).wait_send()
        to_x(which).wait_send()
    for step in range(5):
        exchange(step).wait_send()
    for segment in range(3):

        @pl.loop(0, ring - 1)
        def _(step):
            for half, direction in pieces:
                scatter(segment, direction, half, step).wait_send()
                collect(segment, direction, half, step).wait_send()

        ring_out(segment, "wait")


def angle_parts(seq_len):
    inverse = 10000.0 ** (-(np.arange(ROT // 2) * 2.0 / ROT))
    per_lane = np.zeros((128,))
    for start in (0, ROT // 2, HD, HD + ROT // 2):
        per_lane[start : start + ROT // 2] = inverse
    coarse = (np.arange(seq_len // 32) * 32.0)[:, None] * per_lane[None, :]
    fine = np.arange(32.0)[:, None] * per_lane[None, :]
    return [f(a).astype(np.float32) for a in (coarse, fine) for f in (np.cos, np.sin)]


def per_device_fused(
    tokens, cotangent, gain_attn, bias_attn, gain_mlp, bias_mlp, qkv_weight, qkv_bias,
    out_weight, out_bias, up_weight, up_bias, down_weight, down_bias,
):
    rows, width = tokens.shape
    ring = lax.axis_size("dp")
    seq = rows * lax.axis_size("tensor")
    heads = out_weight.shape[0] // HD
    hidden_width = up_weight.shape[1]
    qkv_width = qkv_weight.shape[1]
    cos_a, sin_a, cos_b, sin_b = angle_parts(seq)
    vmem = pl.BlockSpec(memory_space=pltpu.VMEM)
    hbm = pl.BlockSpec(memory_space=pl.ANY)
    V = pltpu.VMEM
    D = pltpu.SemaphoreType.DMA
    scratch = [
        V((seq, width), BF16), V((seq, width), BF16), V((seq, width), BF16), V((seq, width), BF16),
        V((seq, hidden_width), BF16), V((seq, hidden_width), F32), V((seq, hidden_width), BF16),
        V((seq, qkv_width), BF16),
        V((heads, seq, HD), BF16), V((heads, seq, HD), BF16), V((heads, seq, HD), BF16),
        V((heads, seq, HD), BF16), V((heads, seq, HD), BF16), V((seq, heads * HD), BF16),
        V((heads, seq, HD), F32), V((heads, HD, seq), F32), V((heads, HD, seq), F32),
        V((TILE, seq), F32), V((TILE, seq), F32),
        V((seq, 128), F32), V((seq, 128), F32),
        V(qkv_weight.shape, BF16), V(out_weight.shape, BF16), V(up_weight.shape, BF16), V(down_weight.shape, BF16),
        V((3, 2, 2, ring, 128, 256), BF16), V((3, 2, 2, ring, 128, 256), BF16), V((2, 128, 512), F32),
        V((2, seq, width), BF16), V((2, 2, rows, width), BF16), V((2, rows, width), BF16),
        V((8, width), F32), V((5, 8, width), F32), V((5, 8, width), F32),
        D((6,)), D((2, 5)), D((2, 5)),
        D((3, 2, 2, 2 * ring - 2)), D((3, 2, 2, 2 * ring - 2)),
        D((2, 3)), D((2, 3)), D((5,)), D((5,)), D((3, 2, 2, ring)), D((2, ring)),
    ]
    mixed, input_grad, gd, gu, gq, go, sv = pl.pallas_call(
        functools.partial(fused_kernel, ring),
        out_shape=[
            jax.ShapeDtypeStruct((rows, width), BF16),
            jax.ShapeDtypeStruct((rows, width), F32),
            jax.ShapeDtypeStruct(down_weight.shape, BF16),
            jax.ShapeDtypeStruct(up_weight.shape, BF16),
            jax.ShapeDtypeStruct(qkv_weight.shape, BF16),
            jax.ShapeDtypeStruct(out_weight.shape, BF16),
            jax.ShapeDtypeStruct((8, width), F32),
        ],
        in_specs=[hbm, hbm] + [vmem] * 8 + [hbm] * 4 + [vmem] * 4,
        out_specs=[vmem, vmem, hbm, hbm, hbm, hbm, vmem],
        scratch_shapes=scratch,
        compiler_params=pltpu.CompilerParams(has_side_effects=True, vmem_limit_bytes=VMEM_LIMIT),
        name="layer",
    )(
        tokens, cotangent,
        *(v.reshape(1, -1) for v in (gain_attn, bias_attn, gain_mlp, bias_mlp, out_bias, down_bias, qkv_bias, up_bias)),
        qkv_weight, out_weight, up_weight, down_weight, cos_a, sin_a, cos_b, sin_b,
    )
    elements = rows * width * ring * lax.axis_size("tensor")
    statistics = jnp.sqrt(sv[5, :3] / elements)
    return (
        mixed, input_grad, sv[0], sv[1], sv[2], sv[3],
        gq.astype(F32), sv[7, :qkv_width], go.astype(F32), sv[4],
        gu.astype(F32), sv[6], gd.astype(F32), sv[4], statistics,
    )


def solution(mesh):
    in_specs = (
        P(("dp", "tensor"), None),
        P(("dp", "tensor"), None),
        P(),
        P(),
        P(),
        P(),
        P(None, "tensor"),
        P("tensor"),
        P("tensor", None),
        P(),
        P(None, "tensor"),
        P("tensor"),
        P("tensor", None),
        P(),
    )
    out_specs = (
        P(("dp", "tensor"), None),
        P(("dp", "tensor"), None),
        P(),
        P(),
        P(),
        P(),
        P(None, "tensor"),
        P("tensor"),
        P("tensor", None),
        P(),
        P(None, "tensor"),
        P("tensor"),
        P("tensor", None),
        P(),
        P(),
    )
    fused = mesh.shape["tensor"] == 4 and mesh.shape["dp"] == 8
    return jax.shard_map(
        per_device_fused if fused else per_device, mesh=mesh, in_specs=in_specs, out_specs=out_specs, check_vma=False
    )
```

```python
import functools
import math

import jax
import jax.numpy as jnp
import numpy as np
from jax import lax
from jax.experimental import pallas as pl
from jax.experimental.pallas import tpu as pltpu
from jax.sharding import PartitionSpec as P

HD = 64
ROT = 16
VMEM_LIMIT = 62 << 20


epsilon = 1e-05


def angle_tables(seq_len):
    positions = jnp.arange(seq_len, dtype=jnp.float32)
    inverse = 10000.0 ** (-(jnp.arange(ROT // 2, dtype=jnp.float32) * 2.0 / ROT))
    angles = positions[:, None] * inverse[None, :]
    cosine = jnp.concatenate([jnp.cos(angles), jnp.cos(angles)], axis=-1)[:, None, :]
    sine_part = jnp.concatenate([jnp.sin(angles), jnp.sin(angles)], axis=-1)[:, None, :]
    return (cosine, sine_part)


def rotate(field_in, cosine, sine_part):
    half_rot = ROT // 2
    first_half = field_in[..., :half_rot]
    second = field_in[..., half_rot:ROT]
    turned = jnp.concatenate([-second, first_half], axis=-1)
    return jnp.concatenate(
        [field_in[..., :ROT] * cosine + turned * sine_part, field_in[..., ROT:]], axis=-1
    )


def unrotate(grad_in, cosine, sine_part):
    half_rot = ROT // 2
    head_part = grad_in[..., :ROT]
    scaled = head_part * sine_part
    turned = jnp.concatenate([scaled[..., half_rot:], -scaled[..., :half_rot]], axis=-1)
    return jnp.concatenate([head_part * cosine + turned, grad_in[..., ROT:]], axis=-1)


def normalize(raw_rows):
    average = jnp.mean(raw_rows, axis=-1, keepdims=True)
    centred = raw_rows - average
    spread = jnp.mean(centred * centred, axis=-1, keepdims=True)
    inverse_root = lax.rsqrt(spread + epsilon)
    return (centred * inverse_root, inverse_root)


def against(left, right):
    return lax.dot_general(
        left, right, (((1,), (1,)), ((), ())), preferred_element_type=jnp.float32
    )


def per_device(
    tokens,
    cotangent,
    gain_attn,
    bias_attn,
    gain_mlp,
    bias_mlp,
    qkv_weight,
    qkv_bias,
    out_weight,
    out_bias,
    up_weight,
    up_bias,
    down_weight,
    down_bias,
):
    own_rows = tokens.shape[0]
    model_width = tokens.shape[1]
    heads_here = out_weight.shape[0] // HD
    score_scale = HD ** (-0.5)
    whole_rows = lax.all_gather(tokens, "tensor", axis=0, tiled=True)
    seq_len = whole_rows.shape[0]
    normed, _ = normalize(whole_rows.astype(jnp.float32))
    attention_input = (normed * gain_attn + bias_attn).astype(jnp.bfloat16)
    feed_input = (normed * gain_mlp + bias_mlp).astype(jnp.bfloat16)
    projected = jnp.dot(attention_input, qkv_weight, preferred_element_type=jnp.float32) + qkv_bias
    projected = projected.reshape(seq_len, heads_here, 3, HD)
    cosine, sine_part = angle_tables(seq_len)
    queries = rotate(projected[:, :, 0], cosine, sine_part).astype(jnp.bfloat16)
    keys_all = rotate(projected[:, :, 1], cosine, sine_part).astype(jnp.bfloat16)
    values_all = projected[:, :, 2].astype(jnp.bfloat16)
    preact = jnp.dot(feed_input, up_weight, preferred_element_type=jnp.float32) + up_bias
    hidden = jax.nn.gelu(preact, approximate=False).astype(jnp.bfloat16)
    block_rows = min(512, seq_len)
    block_total = seq_len // block_rows
    key_positions = jnp.arange(seq_len, dtype=jnp.int32)

    def causal_mask(offset):
        return key_positions[None, :] <= (offset + jnp.arange(block_rows, dtype=jnp.int32))[:, None]

    def forward_block(number):
        offset = number * block_rows
        query_rows = lax.dynamic_slice_in_dim(queries, offset, block_rows, 0)
        scores = (
            jnp.einsum("qhd,khd->hqk", query_rows, keys_all, preferred_element_type=jnp.float32)
            * score_scale
        )
        scores = jnp.where(causal_mask(offset)[None], scores, -1e30)
        highest = jnp.max(scores, axis=-1, keepdims=True)
        weights = jnp.exp(scores - highest)
        totals = jnp.sum(weights, axis=-1, keepdims=True)
        soft_rows = (weights / totals).astype(jnp.bfloat16)
        context_rows = jnp.einsum(
            "hqk,khd->qhd", soft_rows, values_all, preferred_element_type=jnp.float32
        ).astype(jnp.bfloat16)
        log_totals = (highest + jnp.log(totals))[:, :, 0].T
        return (context_rows, log_totals)

    context_blocks, log_blocks = lax.map(forward_block, jnp.arange(block_total, dtype=jnp.int32))
    context = context_blocks.reshape(seq_len, heads_here * HD)
    log_sums = log_blocks.reshape(seq_len, heads_here)
    context_rows = context
    branch = lax.psum_scatter(
        jnp.dot(context_rows, out_weight, preferred_element_type=jnp.float32)
        + jnp.dot(hidden, down_weight, preferred_element_type=jnp.float32),
        "tensor",
        scatter_dimension=0,
        tiled=True,
    )
    branch = branch + out_bias + down_bias
    residual_out = tokens.astype(jnp.float32) + branch
    mixed_out = residual_out.astype(jnp.bfloat16)
    forward_squares = jnp.stack([jnp.sum(residual_out * residual_out), jnp.sum(branch * branch)])
    forward_totals = lax.psum(forward_squares, ("dp", "tensor"))
    upstream = lax.all_gather(cotangent, "tensor", axis=0, tiled=True)
    out_weight_grad = jnp.einsum("sa,sd->ad", context, upstream, preferred_element_type=jnp.float32)
    down_weight_grad = jnp.einsum("sf,sd->fd", hidden, upstream, preferred_element_type=jnp.float32)
    context_grad = against(upstream, out_weight).astype(jnp.bfloat16)
    hidden_grad = against(upstream, down_weight)
    normal_cdf = 0.5 * (1.0 + lax.erf(preact * 0.5**0.5))
    density = jnp.exp(-0.5 * preact * preact) * (1.0 / math.sqrt(2.0 * math.pi))
    preact_grad = (hidden_grad * (normal_cdf + preact * density)).astype(jnp.bfloat16)
    context_grad3 = context_grad.reshape(seq_len, heads_here, HD)

    def backward_block(carried, number):
        key_grad, value_grad = carried
        offset = number * block_rows
        query_rows = lax.dynamic_slice_in_dim(queries, offset, block_rows, 0)
        grad_rows = lax.dynamic_slice_in_dim(context_grad3, offset, block_rows, 0)
        log_rows = lax.dynamic_slice_in_dim(log_sums, offset, block_rows, 0).T
        scores = (
            jnp.einsum("qhd,khd->hqk", query_rows, keys_all, preferred_element_type=jnp.float32)
            * score_scale
        )
        soft_full = jnp.exp(
            jnp.where(causal_mask(offset)[None], scores - log_rows[:, :, None], -1e30)
        )
        prob_grad = jnp.einsum(
            "qhd,khd->hqk", grad_rows, values_all, preferred_element_type=jnp.float32
        )
        deltas = jnp.sum(soft_full * prob_grad, axis=-1, keepdims=True)
        score_grad = (soft_full * (prob_grad - deltas)).astype(jnp.bfloat16)
        query_grad = (
            jnp.einsum("hqk,khd->qhd", score_grad, keys_all, preferred_element_type=jnp.float32)
            * score_scale
        )
        key_grad = (
            key_grad
            + jnp.einsum("hqk,qhd->khd", score_grad, query_rows, preferred_element_type=jnp.float32)
            * score_scale
        )
        value_grad = value_grad + jnp.einsum(
            "hqk,qhd->khd",
            soft_full.astype(jnp.bfloat16),
            grad_rows,
            preferred_element_type=jnp.float32,
        )
        return ((key_grad, value_grad), query_grad)

    empty = jnp.zeros((seq_len, heads_here, HD), jnp.float32)
    (key_grad, value_grad), query_blocks = lax.scan(
        backward_block, (empty, empty), jnp.arange(block_total, dtype=jnp.int32)
    )
    query_grad = unrotate(query_blocks.reshape(seq_len, heads_here, HD), cosine, sine_part)
    key_grad = unrotate(key_grad, cosine, sine_part)
    qkv_grad = (
        jnp.stack([query_grad, key_grad, value_grad], axis=2)
        .reshape(seq_len, 3 * heads_here * HD)
        .astype(jnp.bfloat16)
    )
    qkv_weight_grad = jnp.einsum(
        "sd,sc->dc", attention_input, qkv_grad, preferred_element_type=jnp.float32
    )
    qkv_bias_grad = jnp.sum(qkv_grad, axis=0, dtype=jnp.float32)
    up_weight_grad = jnp.einsum(
        "sd,sf->df", feed_input, preact_grad, preferred_element_type=jnp.float32
    )
    up_bias_grad = jnp.sum(preact_grad, axis=0, dtype=jnp.float32)
    own_normed, own_scale = normalize(tokens.astype(jnp.float32))
    attention_back = against(qkv_grad, qkv_weight)
    feed_back = against(preact_grad, up_weight)
    gain_terms = jnp.stack(
        [
            jnp.sum(normed * attention_back, axis=0),
            jnp.sum(attention_back, axis=0),
            jnp.sum(normed * feed_back, axis=0),
            jnp.sum(feed_back, axis=0),
        ]
    )
    normed_grad = lax.psum_scatter(
        (attention_back * gain_attn + feed_back * gain_mlp).astype(jnp.bfloat16),
        "tensor",
        scatter_dimension=0,
        tiled=True,
    ).astype(jnp.float32)
    centred_term = (
        normed_grad
        - jnp.mean(normed_grad, axis=-1, keepdims=True)
        - own_normed * jnp.mean(normed_grad * own_normed, axis=-1, keepdims=True)
    )
    input_grad = own_scale * centred_term + cotangent.astype(jnp.float32)
    (
        qkv_weight_grad,
        qkv_bias_grad,
        out_weight_grad,
        up_weight_grad,
        up_bias_grad,
        down_weight_grad,
    ) = lax.psum(
        (
            qkv_weight_grad,
            qkv_bias_grad,
            out_weight_grad,
            up_weight_grad,
            up_bias_grad,
            down_weight_grad,
        ),
        "dp",
    )
    bias_rows = jnp.sum(cotangent, axis=0, dtype=jnp.float32)
    grad_square = jnp.sum(input_grad * input_grad)
    gain_totals, bias_totals, grad_total = lax.psum(
        (gain_terms, bias_rows, grad_square), ("dp", "tensor")
    )
    square_totals = jnp.concatenate([forward_totals, grad_total[None]])
    elements = own_rows * model_width * lax.axis_size("dp") * lax.axis_size("tensor")
    statistics = jnp.sqrt(square_totals / elements)
    return (
        mixed_out,
        input_grad,
        gain_totals[0],
        gain_totals[1],
        gain_totals[2],
        gain_totals[3],
        qkv_weight_grad,
        qkv_bias_grad,
        out_weight_grad,
        bias_totals,
        up_weight_grad,
        up_bias_grad,
        down_weight_grad,
        bias_totals,
        statistics,
    )


F32 = jnp.float32
BF16 = jnp.bfloat16
MESH = pl.DeviceIdType.MESH
TILE = 256
PARTS = 4


def dot_nn(left, right):
    return jnp.dot(left, right, preferred_element_type=F32)


def dot_nt(left, right):
    return lax.dot_general(left, right, (((1,), (1,)), ((), ())), preferred_element_type=F32)


def dot_tn(left, right):
    return lax.dot_general(left, right, (((0,), (0,)), ((), ())), preferred_element_type=F32)


def fused_kernel(
    ring,
    tok, cot, ga, ba, gm, bm, bo, bd, bqkv, bup, wqkv_h, wout_h, wup_h, wdn_h, cos_a, sin_a, cos_b, sin_b,
    mixed, igrad, gd_o, gu_o, gq_o, go_o, sv_o,
    T, C, AI, FI, HID, GP, PG, QG, QH, KH, VH, CGH, CTXH, CTX, DQ, DKT, DVT, COS, SIN,
    WQKV, WOUT, WUP, WDN, RSB, GB, PSC, PART, RA, RB, SV, ES, EX,
    lsem, g_s, g_r, r_s, r_r, b_s, b_r, e_s, e_r, o_s,
):
    rows = tok.shape[0]
    width = tok.shape[1]
    seq = T.shape[0]
    heads = QH.shape[0]
    hidden_width = WUP.shape[1]
    half_rows = rows // 2
    blocks = seq // TILE
    scale = HD ** (-0.5)
    dp = lax.axis_index("dp")
    t = lax.axis_index("tensor")
    core = lax.rem(t, 2)
    x = lax.div(t, 2)
    depth = ring // 2
    y = lax.rem(dp, 2)
    z = lax.div(dp, 2)
    at = z + y * (2 * depth - 1 - 2 * z)

    def ring_device(place):
        ny = lax.div(place, depth)
        return (2 * (place + ny * (2 * depth - 1 - 2 * place)) + ny, t)

    following = ring_device(lax.rem(at + 1, ring))
    previous = ring_device(lax.rem(at + ring - 1, ring))
    onward = (following, previous)
    core_mate = (dp, t + 1 - 2 * core)
    x_block = 2 * (1 - x) + core
    x_mate = (dp, x_block)

    def remote(src, dst, send, recv, device):
        return pltpu.make_async_remote_copy(
            src_ref=src, dst_ref=dst, send_sem=send, recv_sem=recv, device_id=device, device_id_type=MESH
        )

    def gather(which, kind):
        src, full = (tok, T) if which == 0 else (cot, C)
        sems = (g_s.at[which, kind], g_r.at[which, kind])
        if kind == 0:
            return remote(src, full.at[pl.ds(t * rows, rows)], *sems, core_mate)
        if kind <= 2:
            off = (kind - 1) * half_rows
            return remote(
                src.at[pl.ds(off, half_rows)], full.at[pl.ds(t * rows + off, half_rows)], *sems, x_mate
            )
        part = full.at[pl.ds(x_block * rows + (kind - 3) * half_rows, half_rows)]
        return remote(part, part, *sems, core_mate)

    local = [
        pltpu.make_async_copy(tok, T.at[pl.ds(t * rows, rows)], lsem.at[0]),
        pltpu.make_async_copy(cot, C.at[pl.ds(t * rows, rows)], lsem.at[1]),
        pltpu.make_async_copy(wqkv_h, WQKV, lsem.at[2]),
        pltpu.make_async_copy(wup_h, WUP, lsem.at[3]),
        pltpu.make_async_copy(wdn_h, WDN, lsem.at[4]),
        pltpu.make_async_copy(wout_h, WOUT, lsem.at[5]),
    ]
    gather(0, 1).start()
    gather(0, 2).start()
    gather(0, 0).start()
    gather(1, 1).start()
    gather(1, 2).start()
    gather(1, 0).start()
    for copy in (local[0], local[2], local[3], local[1], local[4], local[5]):
        copy.start()

    @pl.loop(0, seq // 32)
    def _(a):
        ca, sa = cos_a[pl.ds(a, 1), :], sin_a[pl.ds(a, 1), :]
        cb, sb = cos_b[...], sin_b[...]
        COS[pl.ds(a * 32, 32), :] = ca * cb - sa * sb
        SIN[pl.ds(a * 32, 32), :] = sa * cb + ca * sb

    SV[...] = jnp.zeros_like(SV)

    @pl.loop(0, heads)
    def _(h):
        DKT[h] = jnp.zeros(DKT.shape[1:], F32)
        DVT[h] = jnp.zeros(DVT.shape[1:], F32)

    lane = lax.broadcasted_iota(jnp.int32, (TILE, 128), 1)
    low_lane = jnp.where(lane >= 64, lane - 64, lane)

    def tables(base, group):
        cosine, sine = COS[pl.ds(base, TILE), :], SIN[pl.ds(base, TILE), :]
        if group == 1:
            cosine = jnp.where(lane >= 64, cosine, 1.0)
            sine = jnp.where(lane >= 64, sine, 0.0)
        if group == 2:
            cosine = jnp.where(lane < 64, cosine, 1.0)
            sine = jnp.where(lane < 64, sine, 0.0)
        upper = jnp.where(low_lane >= ROT // 2, sine, 0.0)
        return cosine, upper, sine - upper

    def norm_rows(base, count):
        raw = T[pl.ds(base, count), :].astype(F32)
        centred = raw - jnp.mean(raw, axis=1, keepdims=True)
        inverse_root = lax.rsqrt(jnp.mean(centred * centred, axis=1, keepdims=True) + epsilon)
        return centred * inverse_root, inverse_root

    def forward_block(block):
        base = pl.multiple_of(block * rows, rows)

        @pl.loop(0, rows // 64)
        def _(part):
            off = pl.multiple_of(base + part * 64, 64)
            normed, _ = norm_rows(off, 64)
            AI[pl.ds(off, 64), :] = (normed * ga[...] + ba[...]).astype(BF16)
            FI[pl.ds(off, 64), :] = (normed * gm[...] + bm[...]).astype(BF16)

        for group in range(3 * heads // 2):
            if group % 2 == 0:
                columns = slice(group * 128, group * 128 + 256)
                pair = dot_nn(AI[pl.ds(base, rows), :], WQKV[:, columns]) + bqkv[:, columns]
            value = pair[:, (group % 2) * 128 : (group % 2) * 128 + 128]
            cosine, upper, lower = tables(base, group % 3)
            turned = (
                value * cosine
                - lower * pltpu.roll(value, 128 - ROT // 2, 1)
                + upper * pltpu.roll(value, ROT // 2, 1)
            ).astype(BF16)
            first = 2 * (group // 3)
            left, left_head = ((QH, first), (VH, first), (KH, first + 1))[group % 3]
            right, right_head = ((KH, first), (QH, first + 1), (VH, first + 1))[group % 3]
            left[left_head, pl.ds(base, rows), :] = turned[:, :HD]
            right[right_head, pl.ds(base, rows), :] = turned[:, HD:]

        for part in range(hidden_width // TILE):
            columns = slice(part * TILE, (part + 1) * TILE)
            preact = dot_nn(FI[pl.ds(base, rows), :], WUP[:, columns]) + bup[:, columns]
            cdf = 0.5 * (1.0 + lax.erf(preact * 0.5**0.5))
            density = jnp.exp(-0.5 * preact * preact) * (1.0 / math.sqrt(2.0 * math.pi))
            HID[pl.ds(base, rows), columns] = (preact * cdf).astype(BF16)
            GP[pl.ds(base, rows), columns] = cdf + preact * density

    def cotangent_block(block):
        base = pl.multiple_of(block * rows, rows)
        upstream = C[pl.ds(base, rows), :]
        grad = dot_nt(upstream, WOUT[...]).astype(BF16)
        for h in range(heads):
            CGH[h, pl.ds(base, rows), :] = grad[:, h * HD : (h + 1) * HD]

        for part in range(hidden_width // TILE):
            columns = slice(part * TILE, (part + 1) * TILE)
            back = dot_nt(upstream, WDN[columns, :])
            rounded = (back * GP[pl.ds(base, rows), columns]).astype(BF16)
            PG[pl.ds(base, rows), columns] = rounded
            SV[6:7, columns] += jnp.sum(rounded.astype(F32), axis=0, keepdims=True)

    def attention_rows(h, own):
        here = slice(own * TILE, (own + 1) * TILE)
        before = own * TILE
        reach = before + TILE
        query = QH[h, here, :]
        grad = CGH[h, here, :]
        keys = KH[h, :reach, :]
        values = VH[h, :reach, :]
        scores = dot_nt(query, keys) * scale
        row_at = lax.broadcasted_iota(jnp.int32, (TILE, TILE), 0)
        column_at = lax.broadcasted_iota(jnp.int32, (TILE, TILE), 1)
        corner = jnp.where(column_at <= row_at, scores[:, before:], -1e30)
        scores = jnp.concatenate([scores[:, :before], corner], axis=1) if own else corner
        weights = jnp.exp(scores - jnp.max(scores, axis=1, keepdims=True))
        probs = weights * (1.0 / jnp.sum(weights, axis=1, keepdims=True))
        soft = probs.astype(BF16)
        CTXH[h, here, :] = dot_nn(soft, values).astype(BF16)
        prob_grad = dot_nt(grad, values)
        delta = jnp.sum(probs * prob_grad, axis=1, keepdims=True)
        score_grad = (probs * (prob_grad - delta)).astype(BF16)
        DQ[h, here, :] = scale * dot_nn(score_grad, keys)
        DKT[h, :, :reach] += dot_nn(query.astype(F32).T.astype(BF16), score_grad)
        DVT[h, :, :reach] += dot_nn(grad.astype(F32).T.astype(BF16), soft)

    def attention_unit(unit):
        h = lax.div(unit, blocks)
        for own in range(blocks):
            pl.when(lax.rem(unit, blocks) == own)(functools.partial(attention_rows, h, own))

    def assemble(block):
        base = pl.multiple_of(block * TILE, TILE)
        here = pl.ds(base, TILE)
        for pair in range(heads // 2):
            one, two = 2 * pair, 2 * pair + 1
            CTX[here, pair * 128 : (pair + 1) * 128] = jnp.concatenate(
                [CTXH[one, here, :], CTXH[two, here, :]], axis=1
            )
            parts = [
                (DQ[one, here, :], scale * DKT[one, :, here].T),
                (DVT[one, :, here].T, DQ[two, here, :]),
                (scale * DKT[two, :, here].T, DVT[two, :, here].T),
            ]
            for group, (left, right) in enumerate(parts):
                grad = jnp.concatenate([left, right], axis=1)
                cosine, upper, lower = tables(base, group)
                turned = (
                    grad * cosine
                    + pltpu.roll(grad * upper, 128 - ROT // 2, 1)
                    - pltpu.roll(grad * lower, ROT // 2, 1)
                ).astype(BF16)
                columns = slice((3 * pair + group) * 128, (3 * pair + group + 1) * 128)
                QG[here, columns] = turned
                SV[7:8, columns] += jnp.sum(turned.astype(F32), axis=0, keepdims=True)

    def order(step):
        flip_core = 1 - lax.div(step, 2)
        flip_x = 1 - lax.rem(step, 2)
        return 2 * lax.rem(x + flip_x, 2) + lax.rem(core + flip_core, 2)

    def to_core(which, slot):
        block = (2 * x + 1 - core) if slot == 0 else (2 * (1 - x) + 1 - core)
        return remote(
            PART.at[which, pl.ds(block * rows, rows)], RA.at[which, slot],
            b_s.at[which, slot], b_r.at[which, slot], core_mate,
        )

    def to_x(which):
        return remote(
            PART.at[which, pl.ds(x_block * rows, rows)], RB.at[which],
            b_s.at[which, 2], b_r.at[which, 2], x_mate,
        )

    def send_after(which, step):
        @pl.when(step == 0)
        def _():
            to_core(which, 1).start()

        @pl.when(step == 1)
        def _():
            to_core(which, 0).start()

    def branch_block(step):
        base = pl.multiple_of(order(step) * rows, rows)
        here = pl.ds(base, rows)

        for part in range(width // TILE):
            columns = slice(part * TILE, (part + 1) * TILE)
            PART[0, here, columns] = (
                dot_nn(CTX[here, :], WOUT[:, columns]) + dot_nn(HID[here, :], WDN[:, columns])
            ).astype(BF16)

        send_after(0, step)

    def back_block(step):
        base = pl.multiple_of(order(step) * rows, rows)
        here = pl.ds(base, rows)
        raw = T[here, :].astype(F32)
        average = jnp.mean(raw, axis=1, keepdims=True)
        spread = jnp.mean((raw - average) * (raw - average), axis=1, keepdims=True)
        inverse_root = lax.rsqrt(spread + epsilon)

        for part in range(width // TILE):
            columns = slice(part * TILE, (part + 1) * TILE)
            normed = (T[here, columns].astype(F32) - average) * inverse_root
            attention_back = dot_nt(QG[here, :], WQKV[columns, :])
            feed_back = dot_nt(PG[here, :], WUP[columns, :])
            SV[0:1, columns] += jnp.sum(normed * attention_back, axis=0, keepdims=True)
            SV[1:2, columns] += jnp.sum(attention_back, axis=0, keepdims=True)
            SV[2:3, columns] += jnp.sum(normed * feed_back, axis=0, keepdims=True)
            SV[3:4, columns] += jnp.sum(feed_back, axis=0, keepdims=True)
            PART[1, here, columns] = (attention_back * ga[:, columns] + feed_back * gm[:, columns]).astype(BF16)

        send_after(1, step)

    def chip_sum(which):
        to_core(which, 1).wait_recv()
        there = pl.ds(pl.multiple_of(x_block * rows, rows), rows)
        PART[which, there, :] = (PART[which, there, :].astype(F32) + RA[which, 1].astype(F32)).astype(BF16)
        to_x(which).start()

    def finish():
        for which in range(2):
            to_core(which, 0).wait_recv()
            to_x(which).wait_recv()
        SV[4:5, :] = jnp.sum(C[pl.ds(t * rows, rows), :].astype(F32), axis=0, keepdims=True)

        def total(which, off):
            return (
                PART[which, pl.ds(pl.multiple_of(t * rows + off, 64), 64), :].astype(F32)
                + RA[which, 0, pl.ds(off, 64), :].astype(F32)
                + RB[which, pl.ds(off, 64), :].astype(F32)
            )

        def square(value):
            return jnp.sum(jnp.sum(value * value, axis=1, keepdims=True), axis=0, keepdims=True)

        def part(number, sums):
            off = pl.multiple_of(number * 64, 64)
            here = pl.ds(pl.multiple_of(t * rows + off, 64), 64)
            branch = total(0, off) + bo[...] + bd[...]
            residual = T[here, :].astype(F32) + branch
            mixed[pl.ds(off, 64), :] = residual.astype(BF16)
            normed, inverse_root = norm_rows(t * rows + off, 64)
            grad = total(1, off)
            grad = inverse_root * (
                grad
                - jnp.mean(grad, axis=1, keepdims=True)
                - normed * jnp.mean(grad * normed, axis=1, keepdims=True)
            ) + C[here, :].astype(F32)
            igrad[pl.ds(off, 64), :] = grad
            return sums[0] + square(residual), sums[1] + square(branch), sums[2] + square(grad)

        zero = jnp.zeros((1, 1), F32)
        sums = lax.fori_loop(0, rows // 64, part, (zero, zero, zero))
        spot = lax.broadcasted_iota(jnp.int32, (1, width), 1)
        SV[5:6, :] = jnp.where(
            spot == 0, sums[0], jnp.where(spot == 1, sums[1], jnp.where(spot == 2, sums[2], 0.0))
        )

    def share(over, offset):
        if over == 0:
            slot, mate = t, (dp, lax.rem(t + offset, 4))
        else:
            slot, mate = 4 + dp, (lax.rem(dp + offset, ring), t)
        return remote(ES.at[over], EX.at[slot], e_s.at[over, offset], e_r.at[over, offset], mate)

    members = (4, ring)

    def share_send(over):
        ES[over] = SV[...]
        EX[(4 * over) + (dp if over else t)] = SV[...]
        for offset in range(1, members[over]):
            share(over, offset).start()

    def share_receive(over):
        for offset in range(1, members[over]):
            share(over, offset).wait_recv()
        total = EX[4 * over]
        for number in range(1, members[over]):
            total = total + EX[4 * over + number]
        if over == 0:
            row = lax.broadcasted_iota(jnp.int32, SV.shape, 0)
            total = jnp.where(row < 6, total, SV[...])
        SV[...] = total

    def chunk(direction, step):
        return lax.rem(at + ring - step, ring) if direction == 0 else lax.rem(at + step, ring)

    def gathered(direction, step):
        return lax.rem(at + 1 + ring - step, ring) if direction == 0 else lax.rem(at + ring - 1 + step, ring)

    def own_partial(segment, step):
        for direction in range(2):
            number = chunk(direction, step)
            columns = pl.ds(pl.multiple_of(number * 128, 128), 128)
            if segment < 2:
                left, right = (HID, C) if segment == 0 else (FI, PG)
                PSC[direction] = dot_tn(left[:, columns], right[:, direction * 512 : (direction + 1) * 512])
            else:
                PSC[direction, :, 0:384] = dot_tn(AI[:, columns], QG[:, direction * 384 : (direction + 1) * 384])
                PSC[direction, :, 384:512] = dot_tn(
                    CTX[:, direction * 128 : (direction + 1) * 128], C[:, columns]
                )

    def scatter(segment, direction, part, step):
        return remote(
            RSB.at[segment, direction, part, step], RSB.at[segment, direction, part, step + 1],
            r_s.at[segment, direction, part, step], r_r.at[segment, direction, part, step], onward[direction],
        )

    def collect(segment, direction, part, step):
        piece = GB.at[segment, direction, part, gathered(direction, step)]
        sem = ring - 1 + step
        return remote(
            piece, piece,
            r_s.at[segment, direction, part, sem], r_r.at[segment, direction, part, sem], onward[direction],
        )

    pieces = [(part, direction) for part in range(PARTS) for direction in range(2)]

    def ring_open(segment):
        own_partial(segment, 0)
        for part, direction in pieces:
            RSB[segment, direction, part, 0] = PSC[direction, :, part * 128 : (part + 1) * 128].astype(BF16)
            scatter(segment, direction, part, 0).start()

    def ring_scatter(segment, step):
        for part, direction in pieces:
            scatter(segment, direction, part, step - 1).wait_recv()
            RSB[segment, direction, part, step] = (
                RSB[segment, direction, part, step].astype(F32)
                + PSC[direction, :, part * 128 : (part + 1) * 128]
            ).astype(BF16)
            scatter(segment, direction, part, step).start()

    def ring_turn(segment):
        last = ring - 1
        for part, direction in pieces:
            scatter(segment, direction, part, last - 1).wait_recv()
            GB[segment, direction, part, gathered(direction, 0)] = (
                RSB[segment, direction, part, last].astype(F32)
                + PSC[direction, :, part * 128 : (part + 1) * 128]
            ).astype(BF16)
            collect(segment, direction, part, 0).start()

    def ring_collect(segment, step):
        for part, direction in pieces:
            collect(segment, direction, part, step - 1).wait_recv()
            collect(segment, direction, part, step).start()

    def ring_close(segment):
        for part, direction in pieces:
            collect(segment, direction, part, ring - 2).wait_recv()

    def out_copy(segment, direction, part, number):
        there = pl.ds(number * 128, 128)
        if segment < 2:
            out = (gd_o if segment == 0 else gu_o).at[there, pl.ds(direction * 512 + part * 128, 128)]
        elif part < 3:
            out = gq_o.at[there, pl.ds(direction * 384 + part * 128, 128)]
        else:
            out = go_o.at[pl.ds(direction * 128, 128), there]
        return pltpu.make_async_copy(
            GB.at[segment, direction, part, number], out, o_s.at[segment, direction, part, number]
        )

    def ring_out(segment, action):
        @pl.loop(0, ring)
        def _(number):
            for part, direction in pieces:
                getattr(out_copy(segment, direction, part, number), action)()

    local[0].wait()
    local[2].wait()
    local[3].wait()

    @pl.loop(0, 4)
    def _(step):
        @pl.when(step == 1)
        def _():
            gather(0, 0).wait_recv()

        @pl.when(step == 2)
        def _():
            gather(0, 1).wait_recv()
            gather(0, 3).start()
            gather(0, 2).wait_recv()
            gather(0, 4).start()

        @pl.when(step == 3)
        def _():
            gather(0, 3).wait_recv()
            gather(0, 4).wait_recv()

        forward_block(2 * lax.rem(x + lax.div(step, 2), 2) + lax.rem(core + lax.rem(step, 2), 2))

    local[1].wait()
    local[4].wait()
    local[5].wait()

    def place_of(step):
        return 2 * lax.rem(x + lax.div(step, 2), 2) + lax.rem(core + lax.rem(step, 2), 2)

    gather(1, 1).wait_recv()
    gather(1, 3).start()
    cotangent_block(place_of(0))
    gather(1, 0).wait_recv()
    gather(1, 2).wait_recv()
    gather(1, 4).start()
    gather(1, 3).wait_recv()
    gather(1, 4).wait_recv()

    turns = ring - 1

    def during(condition, work):
        pl.when(condition)(work)

    ring_open(0)

    @pl.loop(1, 4)
    def _(step):
        cotangent_block(place_of(step))

    ring_open(1)

    @pl.loop(1, turns)
    def _(step):
        for segment in range(2):
            own_partial(segment, step)
            ring_scatter(segment, step)

        @pl.loop(2 * step - 2, 2 * step)
        def _(unit):
            attention_unit(unit)

    for segment in range(2):
        own_partial(segment, turns)
        ring_turn(segment)

    @pl.loop(1, 3)
    def _(step):
        @pl.loop(2 * step + 10, 2 * step + 12)
        def _(unit):
            attention_unit(unit)

        for segment in range(2):
            ring_collect(segment, step)

    @pl.loop(0, blocks)
    def _(block):
        assemble(block)

    ring_open(2)

    @pl.loop(3, turns)
    def _(step):
        for segment in range(2):
            ring_collect(segment, step)
        own_partial(2, step - 2)
        ring_scatter(2, step - 2)

        @pl.when(step <= 4)
        def _():
            @pl.loop(2 * step - 6, 2 * step - 4)
            def _(number):
                back_block(number)

        @pl.when(step == 5)
        def _():
            @pl.loop(0, 4)
            def _(number):
                branch_block(number)

            chip_sum(1)

        during(step == 6, lambda: chip_sum(0))

    for segment in range(2):
        ring_close(segment)
        ring_out(segment, "start")

    @pl.loop(5, turns)
    def _(step):
        own_partial(2, step)
        ring_scatter(2, step)

    own_partial(2, turns)
    ring_turn(2)

    @pl.loop(1, turns)
    def _(step):
        ring_collect(2, step)

        @pl.when(step == 3)
        def _():
            finish()
            share_send(0)

        @pl.when(step == 5)
        def _():
            share_receive(0)
            share_send(1)

    ring_close(2)
    ring_out(2, "start")
    share_receive(1)
    sv_o[...] = SV[...]

    for which in range(2):
        for kind in range(5):
            gather(which, kind).wait_send()
        for slot in range(2):
            to_core(which, slot).wait_send()
        to_x(which).wait_send()
    for over in range(2):
        for offset in range(1, members[over]):
            share(over, offset).wait_send()
    for segment in range(3):

        @pl.loop(0, ring - 1)
        def _(step):
            for part, direction in pieces:
                scatter(segment, direction, part, step).wait_send()
                collect(segment, direction, part, step).wait_send()

        ring_out(segment, "wait")


def angle_parts(seq_len):
    inverse = 10000.0 ** (-(np.arange(ROT // 2) * 2.0 / ROT))
    per_lane = np.zeros((128,))
    for start in (0, ROT // 2, HD, HD + ROT // 2):
        per_lane[start : start + ROT // 2] = inverse
    coarse = (np.arange(seq_len // 32) * 32.0)[:, None] * per_lane[None, :]
    fine = np.arange(32.0)[:, None] * per_lane[None, :]
    return [f(a).astype(np.float32) for a in (coarse, fine) for f in (np.cos, np.sin)]


def per_device_fused(
    tokens, cotangent, gain_attn, bias_attn, gain_mlp, bias_mlp, qkv_weight, qkv_bias,
    out_weight, out_bias, up_weight, up_bias, down_weight, down_bias,
):
    rows, width = tokens.shape
    ring = lax.axis_size("dp")
    seq = rows * lax.axis_size("tensor")
    heads = out_weight.shape[0] // HD
    hidden_width = up_weight.shape[1]
    qkv_width = qkv_weight.shape[1]
    cos_a, sin_a, cos_b, sin_b = angle_parts(seq)
    vmem = pl.BlockSpec(memory_space=pltpu.VMEM)
    hbm = pl.BlockSpec(memory_space=pl.ANY)
    V = pltpu.VMEM
    D = pltpu.SemaphoreType.DMA
    scratch = [
        V((seq, width), BF16), V((seq, width), BF16), V((seq, width), BF16), V((seq, width), BF16),
        V((seq, hidden_width), BF16), V((seq, hidden_width), F32), V((seq, hidden_width), BF16),
        V((seq, qkv_width), BF16),
        V((heads, seq, HD), BF16), V((heads, seq, HD), BF16), V((heads, seq, HD), BF16),
        V((heads, seq, HD), BF16), V((heads, seq, HD), BF16), V((seq, heads * HD), BF16),
        V((heads, seq, HD), F32), V((heads, HD, seq), F32), V((heads, HD, seq), F32),
        V((seq, 128), F32), V((seq, 128), F32),
        V(qkv_weight.shape, BF16), V(out_weight.shape, BF16), V(up_weight.shape, BF16), V(down_weight.shape, BF16),
        V((3, 2, PARTS, ring, 128, 128), BF16), V((3, 2, PARTS, ring, 128, 128), BF16), V((2, 128, 512), F32),
        V((2, seq, width), BF16), V((2, 2, rows, width), BF16), V((2, rows, width), BF16),
        V((8, width), F32), V((2, 8, width), F32), V((4 + ring, 8, width), F32),
        D((6,)), D((2, 5)), D((2, 5)),
        D((3, 2, PARTS, 2 * ring - 2)), D((3, 2, PARTS, 2 * ring - 2)),
        D((2, 3)), D((2, 3)), D((2, ring)), D((2, ring)), D((3, 2, PARTS, ring)),
    ]
    mixed, input_grad, gd, gu, gq, go, sv = pl.pallas_call(
        functools.partial(fused_kernel, ring),
        out_shape=[
            jax.ShapeDtypeStruct((rows, width), BF16),
            jax.ShapeDtypeStruct((rows, width), F32),
            jax.ShapeDtypeStruct(down_weight.shape, BF16),
            jax.ShapeDtypeStruct(up_weight.shape, BF16),
            jax.ShapeDtypeStruct(qkv_weight.shape, BF16),
            jax.ShapeDtypeStruct(out_weight.shape, BF16),
            jax.ShapeDtypeStruct((8, width), F32),
        ],
        in_specs=[hbm, hbm] + [vmem] * 8 + [hbm] * 4 + [vmem] * 4,
        out_specs=[vmem, vmem, hbm, hbm, hbm, hbm, vmem],
        scratch_shapes=scratch,
        compiler_params=pltpu.CompilerParams(has_side_effects=True, vmem_limit_bytes=VMEM_LIMIT),
        name="layer",
    )(
        tokens, cotangent,
        *(v.reshape(1, -1) for v in (gain_attn, bias_attn, gain_mlp, bias_mlp, out_bias, down_bias, qkv_bias, up_bias)),
        qkv_weight, out_weight, up_weight, down_weight, cos_a, sin_a, cos_b, sin_b,
    )
    elements = rows * width * ring * lax.axis_size("tensor")
    return export_outputs(mixed, input_grad, gd, gu, gq, go, sv, elements)


def export_kernel(
    elements,
    mixed, igrad, gd, gu, gq, go, sv,
    mixed_o, igrad_o, ga_o, ba_o, gm_o, bm_o, gq_o, bqkv_o, go_o, bo_o, gu_o, bup_o, gd_o, bd_o, stats_o,
):
    @pl.when(pl.program_id(0) == 0)
    def _():
        for row, out in enumerate((ga_o, ba_o, gm_o, bm_o, bo_o)):
            out[...] = sv[row : row + 1, :]
        bd_o[...] = sv[4:5, :]
        bup_o[...] = sv[6:7, :]
        bqkv_o[...] = sv[7, : bqkv_o.shape[0]]
        stats_o[...] = jnp.sqrt(sv[5, : stats_o.shape[0]] * (1.0 / elements))

    for source, out in ((gd, gd_o), (gu, gu_o), (gq, gq_o), (go, go_o), (mixed, mixed_o), (igrad, igrad_o)):
        out[...] = source[...].astype(out.dtype)


def export_outputs(mixed, input_grad, gd, gu, gq, go, sv, elements):
    steps = 4

    def tiled(array):
        return pl.BlockSpec((array.shape[0] // steps, array.shape[1]), lambda i: (i, 0))

    def whole(*shape):
        return pl.BlockSpec(shape, lambda i: (0,) * len(shape))

    def like(array, dtype=F32):
        return jax.ShapeDtypeStruct(array.shape, dtype)

    width = sv.shape[1]
    row = jax.ShapeDtypeStruct((1, width), F32)
    row_spec = whole(1, width)
    qkv_width = gq.shape[1]
    outs = pl.pallas_call(
        functools.partial(export_kernel, elements),
        grid=(steps,),
        in_specs=[tiled(mixed), tiled(input_grad), tiled(gd), tiled(gu), tiled(gq), tiled(go), whole(*sv.shape)],
        out_specs=[
            tiled(mixed), tiled(input_grad), row_spec, row_spec, row_spec, row_spec, tiled(gq), whole(qkv_width), tiled(go), row_spec,
            tiled(gu), row_spec, tiled(gd), row_spec, whole(3),
        ],
        out_shape=[
            like(mixed, BF16), like(input_grad), row, row, row, row, like(gq), jax.ShapeDtypeStruct((qkv_width,), F32),
            like(go), row, like(gu), row, like(gd), row, jax.ShapeDtypeStruct((3,), F32),
        ],
        compiler_params=pltpu.CompilerParams(vmem_limit_bytes=VMEM_LIMIT),
        name="outputs",
    )(mixed, input_grad, gd, gu, gq, go, sv)
    return tuple(out.reshape(-1) if out.shape == (1, width) else out for out in outs)


def solution(mesh):
    in_specs = (
        P(("dp", "tensor"), None),
        P(("dp", "tensor"), None),
        P(),
        P(),
        P(),
        P(),
        P(None, "tensor"),
        P("tensor"),
        P("tensor", None),
        P(),
        P(None, "tensor"),
        P("tensor"),
        P("tensor", None),
        P(),
    )
    out_specs = (
        P(("dp", "tensor"), None),
        P(("dp", "tensor"), None),
        P(),
        P(),
        P(),
        P(),
        P(None, "tensor"),
        P("tensor"),
        P("tensor", None),
        P(),
        P(None, "tensor"),
        P("tensor"),
        P("tensor", None),
        P(),
        P(),
    )
    fused = mesh.shape["tensor"] == 4 and mesh.shape["dp"] == 8
    return jax.shard_map(
        per_device_fused if fused else per_device, mesh=mesh, in_specs=in_specs, out_specs=out_specs, check_vma=False
    )
```

```python
import functools
import math

import jax
import jax.numpy as jnp
import numpy as np
from jax import lax
from jax.experimental import pallas as pl
from jax.experimental.pallas import tpu as pltpu
from jax.sharding import PartitionSpec as P

HD = 64
ROT = 16
VMEM_LIMIT = 54 << 20


epsilon = 1e-05


def angle_tables(seq_len):
    positions = jnp.arange(seq_len, dtype=jnp.float32)
    inverse = 10000.0 ** (-(jnp.arange(ROT // 2, dtype=jnp.float32) * 2.0 / ROT))
    angles = positions[:, None] * inverse[None, :]
    cosine = jnp.concatenate([jnp.cos(angles), jnp.cos(angles)], axis=-1)[:, None, :]
    sine_part = jnp.concatenate([jnp.sin(angles), jnp.sin(angles)], axis=-1)[:, None, :]
    return (cosine, sine_part)


def rotate(field_in, cosine, sine_part):
    half_rot = ROT // 2
    first_half = field_in[..., :half_rot]
    second = field_in[..., half_rot:ROT]
    turned = jnp.concatenate([-second, first_half], axis=-1)
    return jnp.concatenate(
        [field_in[..., :ROT] * cosine + turned * sine_part, field_in[..., ROT:]], axis=-1
    )


def unrotate(grad_in, cosine, sine_part):
    half_rot = ROT // 2
    head_part = grad_in[..., :ROT]
    scaled = head_part * sine_part
    turned = jnp.concatenate([scaled[..., half_rot:], -scaled[..., :half_rot]], axis=-1)
    return jnp.concatenate([head_part * cosine + turned, grad_in[..., ROT:]], axis=-1)


def normalize(raw_rows):
    average = jnp.mean(raw_rows, axis=-1, keepdims=True)
    centred = raw_rows - average
    spread = jnp.mean(centred * centred, axis=-1, keepdims=True)
    inverse_root = lax.rsqrt(spread + epsilon)
    return (centred * inverse_root, inverse_root)


def against(left, right):
    return lax.dot_general(
        left, right, (((1,), (1,)), ((), ())), preferred_element_type=jnp.float32
    )


def per_device(
    tokens,
    cotangent,
    gain_attn,
    bias_attn,
    gain_mlp,
    bias_mlp,
    qkv_weight,
    qkv_bias,
    out_weight,
    out_bias,
    up_weight,
    up_bias,
    down_weight,
    down_bias,
):
    own_rows = tokens.shape[0]
    model_width = tokens.shape[1]
    heads_here = out_weight.shape[0] // HD
    score_scale = HD ** (-0.5)
    whole_rows = lax.all_gather(tokens, "tensor", axis=0, tiled=True)
    seq_len = whole_rows.shape[0]
    normed, _ = normalize(whole_rows.astype(jnp.float32))
    attention_input = (normed * gain_attn + bias_attn).astype(jnp.bfloat16)
    feed_input = (normed * gain_mlp + bias_mlp).astype(jnp.bfloat16)
    projected = jnp.dot(attention_input, qkv_weight, preferred_element_type=jnp.float32) + qkv_bias
    projected = projected.reshape(seq_len, heads_here, 3, HD)
    cosine, sine_part = angle_tables(seq_len)
    queries = rotate(projected[:, :, 0], cosine, sine_part).astype(jnp.bfloat16)
    keys_all = rotate(projected[:, :, 1], cosine, sine_part).astype(jnp.bfloat16)
    values_all = projected[:, :, 2].astype(jnp.bfloat16)
    preact = jnp.dot(feed_input, up_weight, preferred_element_type=jnp.float32) + up_bias
    hidden = jax.nn.gelu(preact, approximate=False).astype(jnp.bfloat16)
    block_rows = min(512, seq_len)
    block_total = seq_len // block_rows
    key_positions = jnp.arange(seq_len, dtype=jnp.int32)

    def causal_mask(offset):
        return key_positions[None, :] <= (offset + jnp.arange(block_rows, dtype=jnp.int32))[:, None]

    def forward_block(number):
        offset = number * block_rows
        query_rows = lax.dynamic_slice_in_dim(queries, offset, block_rows, 0)
        scores = (
            jnp.einsum("qhd,khd->hqk", query_rows, keys_all, preferred_element_type=jnp.float32)
            * score_scale
        )
        scores = jnp.where(causal_mask(offset)[None], scores, -1e30)
        highest = jnp.max(scores, axis=-1, keepdims=True)
        weights = jnp.exp(scores - highest)
        totals = jnp.sum(weights, axis=-1, keepdims=True)
        soft_rows = (weights / totals).astype(jnp.bfloat16)
        context_rows = jnp.einsum(
            "hqk,khd->qhd", soft_rows, values_all, preferred_element_type=jnp.float32
        ).astype(jnp.bfloat16)
        log_totals = (highest + jnp.log(totals))[:, :, 0].T
        return (context_rows, log_totals)

    context_blocks, log_blocks = lax.map(forward_block, jnp.arange(block_total, dtype=jnp.int32))
    context = context_blocks.reshape(seq_len, heads_here * HD)
    log_sums = log_blocks.reshape(seq_len, heads_here)
    context_rows = context
    branch = lax.psum_scatter(
        jnp.dot(context_rows, out_weight, preferred_element_type=jnp.float32)
        + jnp.dot(hidden, down_weight, preferred_element_type=jnp.float32),
        "tensor",
        scatter_dimension=0,
        tiled=True,
    )
    branch = branch + out_bias + down_bias
    residual_out = tokens.astype(jnp.float32) + branch
    mixed_out = residual_out.astype(jnp.bfloat16)
    forward_squares = jnp.stack([jnp.sum(residual_out * residual_out), jnp.sum(branch * branch)])
    forward_totals = lax.psum(forward_squares, ("dp", "tensor"))
    upstream = lax.all_gather(cotangent, "tensor", axis=0, tiled=True)
    out_weight_grad = jnp.einsum("sa,sd->ad", context, upstream, preferred_element_type=jnp.float32)
    down_weight_grad = jnp.einsum("sf,sd->fd", hidden, upstream, preferred_element_type=jnp.float32)
    context_grad = against(upstream, out_weight).astype(jnp.bfloat16)
    hidden_grad = against(upstream, down_weight)
    normal_cdf = 0.5 * (1.0 + lax.erf(preact * 0.5**0.5))
    density = jnp.exp(-0.5 * preact * preact) * (1.0 / math.sqrt(2.0 * math.pi))
    preact_grad = (hidden_grad * (normal_cdf + preact * density)).astype(jnp.bfloat16)
    context_grad3 = context_grad.reshape(seq_len, heads_here, HD)

    def backward_block(carried, number):
        key_grad, value_grad = carried
        offset = number * block_rows
        query_rows = lax.dynamic_slice_in_dim(queries, offset, block_rows, 0)
        grad_rows = lax.dynamic_slice_in_dim(context_grad3, offset, block_rows, 0)
        log_rows = lax.dynamic_slice_in_dim(log_sums, offset, block_rows, 0).T
        scores = (
            jnp.einsum("qhd,khd->hqk", query_rows, keys_all, preferred_element_type=jnp.float32)
            * score_scale
        )
        soft_full = jnp.exp(
            jnp.where(causal_mask(offset)[None], scores - log_rows[:, :, None], -1e30)
        )
        prob_grad = jnp.einsum(
            "qhd,khd->hqk", grad_rows, values_all, preferred_element_type=jnp.float32
        )
        deltas = jnp.sum(soft_full * prob_grad, axis=-1, keepdims=True)
        score_grad = (soft_full * (prob_grad - deltas)).astype(jnp.bfloat16)
        query_grad = (
            jnp.einsum("hqk,khd->qhd", score_grad, keys_all, preferred_element_type=jnp.float32)
            * score_scale
        )
        key_grad = (
            key_grad
            + jnp.einsum("hqk,qhd->khd", score_grad, query_rows, preferred_element_type=jnp.float32)
            * score_scale
        )
        value_grad = value_grad + jnp.einsum(
            "hqk,qhd->khd",
            soft_full.astype(jnp.bfloat16),
            grad_rows,
            preferred_element_type=jnp.float32,
        )
        return ((key_grad, value_grad), query_grad)

    empty = jnp.zeros((seq_len, heads_here, HD), jnp.float32)
    (key_grad, value_grad), query_blocks = lax.scan(
        backward_block, (empty, empty), jnp.arange(block_total, dtype=jnp.int32)
    )
    query_grad = unrotate(query_blocks.reshape(seq_len, heads_here, HD), cosine, sine_part)
    key_grad = unrotate(key_grad, cosine, sine_part)
    qkv_grad = (
        jnp.stack([query_grad, key_grad, value_grad], axis=2)
        .reshape(seq_len, 3 * heads_here * HD)
        .astype(jnp.bfloat16)
    )
    qkv_weight_grad = jnp.einsum(
        "sd,sc->dc", attention_input, qkv_grad, preferred_element_type=jnp.float32
    )
    qkv_bias_grad = jnp.sum(qkv_grad, axis=0, dtype=jnp.float32)
    up_weight_grad = jnp.einsum(
        "sd,sf->df", feed_input, preact_grad, preferred_element_type=jnp.float32
    )
    up_bias_grad = jnp.sum(preact_grad, axis=0, dtype=jnp.float32)
    own_normed, own_scale = normalize(tokens.astype(jnp.float32))
    attention_back = against(qkv_grad, qkv_weight)
    feed_back = against(preact_grad, up_weight)
    gain_terms = jnp.stack(
        [
            jnp.sum(normed * attention_back, axis=0),
            jnp.sum(attention_back, axis=0),
            jnp.sum(normed * feed_back, axis=0),
            jnp.sum(feed_back, axis=0),
        ]
    )
    normed_grad = lax.psum_scatter(
        (attention_back * gain_attn + feed_back * gain_mlp).astype(jnp.bfloat16),
        "tensor",
        scatter_dimension=0,
        tiled=True,
    ).astype(jnp.float32)
    centred_term = (
        normed_grad
        - jnp.mean(normed_grad, axis=-1, keepdims=True)
        - own_normed * jnp.mean(normed_grad * own_normed, axis=-1, keepdims=True)
    )
    input_grad = own_scale * centred_term + cotangent.astype(jnp.float32)
    (
        qkv_weight_grad,
        qkv_bias_grad,
        out_weight_grad,
        up_weight_grad,
        up_bias_grad,
        down_weight_grad,
    ) = lax.psum(
        (
            qkv_weight_grad,
            qkv_bias_grad,
            out_weight_grad,
            up_weight_grad,
            up_bias_grad,
            down_weight_grad,
        ),
        "dp",
    )
    bias_rows = jnp.sum(cotangent, axis=0, dtype=jnp.float32)
    grad_square = jnp.sum(input_grad * input_grad)
    gain_totals, bias_totals, grad_total = lax.psum(
        (gain_terms, bias_rows, grad_square), ("dp", "tensor")
    )
    square_totals = jnp.concatenate([forward_totals, grad_total[None]])
    elements = own_rows * model_width * lax.axis_size("dp") * lax.axis_size("tensor")
    statistics = jnp.sqrt(square_totals / elements)
    return (
        mixed_out,
        input_grad,
        gain_totals[0],
        gain_totals[1],
        gain_totals[2],
        gain_totals[3],
        qkv_weight_grad,
        qkv_bias_grad,
        out_weight_grad,
        bias_totals,
        up_weight_grad,
        up_bias_grad,
        down_weight_grad,
        bias_totals,
        statistics,
    )


F32 = jnp.float32
BF16 = jnp.bfloat16
MESH = pl.DeviceIdType.MESH
TILE = 256
PARTS = 4


def dot_nn(left, right):
    return jnp.dot(left, right, preferred_element_type=F32)


def dot_nt(left, right):
    return lax.dot_general(left, right, (((1,), (1,)), ((), ())), preferred_element_type=F32)


def dot_tn(left, right):
    return lax.dot_general(left, right, (((0,), (0,)), ((), ())), preferred_element_type=F32)


def fused_kernel(
    ring,
    tok, cot, ga, ba, gm, bm, bo, bd, bqkv, bup, wqkv_h, wout_h, wup_h, wdn_h, cos_a, sin_a, cos_b, sin_b,
    mixed, igrad, GB, SV,
    T, C, AI, FI, HID, GP, PG, QG, QH, KH, VH, CGH, CTXH, CTX, DQ, DKT, DVT, COS, SIN,
    WQKV, WOUT, WUP, WDN, RSB, PSC, PART, RA, RB, ES, EX,
    lsem, g_s, g_r, r_s, r_r, b_s, b_r, e_s, e_r,
):
    rows = tok.shape[0]
    width = tok.shape[1]
    seq = T.shape[0]
    heads = QH.shape[0]
    hidden_width = WUP.shape[1]
    half_rows = rows // 2
    blocks = seq // TILE
    scale = HD ** (-0.5)
    dp = lax.axis_index("dp")
    t = lax.axis_index("tensor")
    core = lax.rem(t, 2)
    x = lax.div(t, 2)
    depth = ring // 2
    y = lax.rem(dp, 2)
    z = lax.div(dp, 2)
    at = z + y * (2 * depth - 1 - 2 * z)

    def ring_device(place):
        ny = lax.div(place, depth)
        return (2 * (place + ny * (2 * depth - 1 - 2 * place)) + ny, t)

    following = ring_device(lax.rem(at + 1, ring))
    previous = ring_device(lax.rem(at + ring - 1, ring))
    onward = (following, previous)
    core_mate = (dp, t + 1 - 2 * core)
    x_block = 2 * (1 - x) + core
    x_mate = (dp, x_block)

    def remote(src, dst, send, recv, device):
        return pltpu.make_async_remote_copy(
            src_ref=src, dst_ref=dst, send_sem=send, recv_sem=recv, device_id=device, device_id_type=MESH
        )

    def gather(which, kind):
        src, full = (tok, T) if which == 0 else (cot, C)
        sems = (g_s.at[which, kind], g_r.at[which, kind])
        if kind == 0:
            return remote(src, full.at[pl.ds(t * rows, rows)], *sems, core_mate)
        if kind <= 2:
            off = (kind - 1) * half_rows
            return remote(
                src.at[pl.ds(off, half_rows)], full.at[pl.ds(t * rows + off, half_rows)], *sems, x_mate
            )
        part = full.at[pl.ds(x_block * rows + (kind - 3) * half_rows, half_rows)]
        return remote(part, part, *sems, core_mate)

    local = [
        pltpu.make_async_copy(tok, T.at[pl.ds(t * rows, rows)], lsem.at[0]),
        pltpu.make_async_copy(wqkv_h, WQKV, lsem.at[2]),
        pltpu.make_async_copy(wup_h, WUP, lsem.at[3]),
        pltpu.make_async_copy(cot, C.at[pl.ds(t * rows, rows)], lsem.at[1]),
        pltpu.make_async_copy(wdn_h, WDN, lsem.at[4]),
        pltpu.make_async_copy(wout_h, WOUT, lsem.at[5]),
    ]
    for copy in local:
        copy.start()
    barrier = pltpu.get_barrier_semaphore()
    for mate in (core_mate, x_mate, following, previous):
        pl.semaphore_signal(barrier, inc=1, device_id=mate, device_id_type=MESH)
    pl.semaphore_wait(barrier, 4)
    gather(0, 1).start()
    gather(0, 2).start()
    gather(0, 0).start()
    gather(1, 1).start()
    gather(1, 2).start()
    gather(1, 0).start()

    @pl.loop(0, seq // 32)
    def _(a):
        ca, sa = cos_a[pl.ds(a, 1), :], sin_a[pl.ds(a, 1), :]
        cb, sb = cos_b[...], sin_b[...]
        COS[pl.ds(a * 32, 32), :] = ca * cb - sa * sb
        SIN[pl.ds(a * 32, 32), :] = sa * cb + ca * sb

    SV[...] = jnp.zeros_like(SV)

    @pl.loop(0, heads)
    def _(h):
        DKT[h] = jnp.zeros(DKT.shape[1:], F32)
        DVT[h] = jnp.zeros(DVT.shape[1:], F32)

    lane = lax.broadcasted_iota(jnp.int32, (TILE, 128), 1)
    low_lane = jnp.where(lane >= 64, lane - 64, lane)

    def tables(base, group):
        cosine, sine = COS[pl.ds(base, TILE), :], SIN[pl.ds(base, TILE), :]
        if group == 1:
            cosine = jnp.where(lane >= 64, cosine, 1.0)
            sine = jnp.where(lane >= 64, sine, 0.0)
        if group == 2:
            cosine = jnp.where(lane < 64, cosine, 1.0)
            sine = jnp.where(lane < 64, sine, 0.0)
        upper = jnp.where(low_lane >= ROT // 2, sine, 0.0)
        return cosine, upper, sine - upper

    def norm_rows(base, count):
        raw = T[pl.ds(base, count), :].astype(F32)
        centred = raw - jnp.mean(raw, axis=1, keepdims=True)
        inverse_root = lax.rsqrt(jnp.mean(centred * centred, axis=1, keepdims=True) + epsilon)
        return centred * inverse_root, inverse_root

    def forward_block(block):
        base = pl.multiple_of(block * rows, rows)

        @pl.loop(0, rows // 64)
        def _(part):
            off = pl.multiple_of(base + part * 64, 64)
            normed, _ = norm_rows(off, 64)
            AI[pl.ds(off, 64), :] = (normed * ga[...] + ba[...]).astype(BF16)
            FI[pl.ds(off, 64), :] = (normed * gm[...] + bm[...]).astype(BF16)

        for group in range(3 * heads // 2):
            if group % 2 == 0:
                columns = slice(group * 128, group * 128 + 256)
                pair = dot_nn(AI[pl.ds(base, rows), :], WQKV[:, columns]) + bqkv[columns].reshape(1, 256)
            value = pair[:, (group % 2) * 128 : (group % 2) * 128 + 128]
            cosine, upper, lower = tables(base, group % 3)
            turned = (
                value * cosine
                - lower * pltpu.roll(value, 128 - ROT // 2, 1)
                + upper * pltpu.roll(value, ROT // 2, 1)
            ).astype(BF16)
            first = 2 * (group // 3)
            left, left_head = ((QH, first), (VH, first), (KH, first + 1))[group % 3]
            right, right_head = ((KH, first), (QH, first + 1), (VH, first + 1))[group % 3]
            left[left_head, pl.ds(base, rows), :] = turned[:, :HD]
            right[right_head, pl.ds(base, rows), :] = turned[:, HD:]

        for part in range(hidden_width // TILE):
            columns = slice(part * TILE, (part + 1) * TILE)
            preact = dot_nn(FI[pl.ds(base, rows), :], WUP[:, columns]) + bup[:, columns]
            cdf = 0.5 * (1.0 + lax.erf(preact * 0.5**0.5))
            density = jnp.exp(-0.5 * preact * preact) * (1.0 / math.sqrt(2.0 * math.pi))
            HID[pl.ds(base, rows), columns] = (preact * cdf).astype(BF16)
            GP[pl.ds(base, rows), columns] = cdf + preact * density

    def cotangent_block(block):
        base = pl.multiple_of(block * rows, rows)
        upstream = C[pl.ds(base, rows), :]
        grad = dot_nt(upstream, WOUT[...]).astype(BF16)
        for h in range(heads):
            CGH[h, pl.ds(base, rows), :] = grad[:, h * HD : (h + 1) * HD]

        for part in range(hidden_width // TILE):
            columns = slice(part * TILE, (part + 1) * TILE)
            back = dot_nt(upstream, WDN[columns, :])
            rounded = (back * GP[pl.ds(base, rows), columns]).astype(BF16)
            PG[pl.ds(base, rows), columns] = rounded
            SV[6:7, columns] += jnp.sum(rounded.astype(F32), axis=0, keepdims=True)

    def attention_rows(h, own):
        here = slice(own * TILE, (own + 1) * TILE)
        before = own * TILE
        reach = before + TILE
        query = QH[h, here, :]
        grad = CGH[h, here, :]
        keys = KH[h, :reach, :]
        values = VH[h, :reach, :]
        scores = dot_nt(query, keys) * scale
        row_at = lax.broadcasted_iota(jnp.int32, (TILE, TILE), 0)
        column_at = lax.broadcasted_iota(jnp.int32, (TILE, TILE), 1)
        corner = jnp.where(column_at <= row_at, scores[:, before:], -1e30)
        scores = jnp.concatenate([scores[:, :before], corner], axis=1) if own else corner
        weights = jnp.exp(scores - jnp.max(scores, axis=1, keepdims=True))
        probs = weights * (1.0 / jnp.sum(weights, axis=1, keepdims=True))
        soft = probs.astype(BF16)
        CTXH[h, here, :] = dot_nn(soft, values).astype(BF16)
        prob_grad = dot_nt(grad, values)
        delta = jnp.sum(probs * prob_grad, axis=1, keepdims=True)
        score_grad = (probs * (prob_grad - delta)).astype(BF16)
        DQ[h, here, :] = scale * dot_nn(score_grad, keys)
        DKT[h, :, :reach] += dot_nn(query.astype(F32).T.astype(BF16), score_grad)
        DVT[h, :, :reach] += dot_nn(grad.astype(F32).T.astype(BF16), soft)

    def attention_unit(unit):
        h = lax.div(unit, blocks)
        for own in range(blocks):
            pl.when(lax.rem(unit, blocks) == own)(functools.partial(attention_rows, h, own))

    def assemble(block):
        base = pl.multiple_of(block * TILE, TILE)
        here = pl.ds(base, TILE)
        for pair in range(heads // 2):
            one, two = 2 * pair, 2 * pair + 1
            CTX[here, pair * 128 : (pair + 1) * 128] = jnp.concatenate(
                [CTXH[one, here, :], CTXH[two, here, :]], axis=1
            )
            parts = [
                (DQ[one, here, :], scale * DKT[one, :, here].T),
                (DVT[one, :, here].T, DQ[two, here, :]),
                (scale * DKT[two, :, here].T, DVT[two, :, here].T),
            ]
            for group, (left, right) in enumerate(parts):
                grad = jnp.concatenate([left, right], axis=1)
                cosine, upper, lower = tables(base, group)
                turned = (
                    grad * cosine
                    + pltpu.roll(grad * upper, 128 - ROT // 2, 1)
                    - pltpu.roll(grad * lower, ROT // 2, 1)
                ).astype(BF16)
                columns = slice((3 * pair + group) * 128, (3 * pair + group + 1) * 128)
                QG[here, columns] = turned
                SV[7:8, columns] += jnp.sum(turned.astype(F32), axis=0, keepdims=True)

    def order(step):
        flip_core = 1 - lax.div(step, 2)
        flip_x = 1 - lax.rem(step, 2)
        return 2 * lax.rem(x + flip_x, 2) + lax.rem(core + flip_core, 2)

    def to_core(which, slot):
        block = (2 * x + 1 - core) if slot == 0 else (2 * (1 - x) + 1 - core)
        return remote(
            PART.at[which, pl.ds(block * rows, rows)], RA.at[which, slot],
            b_s.at[which, slot], b_r.at[which, slot], core_mate,
        )

    def to_x(which):
        return remote(
            PART.at[which, pl.ds(x_block * rows, rows)], RB.at[which],
            b_s.at[which, 2], b_r.at[which, 2], x_mate,
        )

    def send_after(which, step):
        @pl.when(step == 0)
        def _():
            to_core(which, 1).start()

        @pl.when(step == 1)
        def _():
            to_core(which, 0).start()

    def branch_block(step):
        base = pl.multiple_of(order(step) * rows, rows)
        here = pl.ds(base, rows)

        for part in range(width // TILE):
            columns = slice(part * TILE, (part + 1) * TILE)
            PART[0, here, columns] = (
                dot_nn(CTX[here, :], WOUT[:, columns]) + dot_nn(HID[here, :], WDN[:, columns])
            ).astype(BF16)

        send_after(0, step)

    def back_block(step):
        base = pl.multiple_of(order(step) * rows, rows)
        here = pl.ds(base, rows)
        raw = T[here, :].astype(F32)
        average = jnp.mean(raw, axis=1, keepdims=True)
        spread = jnp.mean((raw - average) * (raw - average), axis=1, keepdims=True)
        inverse_root = lax.rsqrt(spread + epsilon)

        for part in range(width // TILE):
            columns = slice(part * TILE, (part + 1) * TILE)
            normed = (T[here, columns].astype(F32) - average) * inverse_root
            attention_back = dot_nt(QG[here, :], WQKV[columns, :])
            feed_back = dot_nt(PG[here, :], WUP[columns, :])
            SV[0:1, columns] += jnp.sum(normed * attention_back, axis=0, keepdims=True)
            SV[1:2, columns] += jnp.sum(attention_back, axis=0, keepdims=True)
            SV[2:3, columns] += jnp.sum(normed * feed_back, axis=0, keepdims=True)
            SV[3:4, columns] += jnp.sum(feed_back, axis=0, keepdims=True)
            PART[1, here, columns] = (attention_back * ga[:, columns] + feed_back * gm[:, columns]).astype(BF16)

        send_after(1, step)

    def chip_sum(which):
        to_core(which, 1).wait_recv()
        there = pl.ds(pl.multiple_of(x_block * rows, rows), rows)
        PART[which, there, :] = (PART[which, there, :].astype(F32) + RA[which, 1].astype(F32)).astype(BF16)
        to_x(which).start()

    def finish():
        for which in range(2):
            to_core(which, 0).wait_recv()
            to_x(which).wait_recv()
        SV[4:5, :] = jnp.sum(C[pl.ds(t * rows, rows), :].astype(F32), axis=0, keepdims=True)

        def total(which, off):
            return (
                PART[which, pl.ds(pl.multiple_of(t * rows + off, 64), 64), :].astype(F32)
                + RA[which, 0, pl.ds(off, 64), :].astype(F32)
                + RB[which, pl.ds(off, 64), :].astype(F32)
            )

        def square(value):
            return jnp.sum(jnp.sum(value * value, axis=1, keepdims=True), axis=0, keepdims=True)

        def part(number, sums):
            off = pl.multiple_of(number * 64, 64)
            here = pl.ds(pl.multiple_of(t * rows + off, 64), 64)
            branch = total(0, off) + bo[...] + bd[...]
            residual = T[here, :].astype(F32) + branch
            mixed[pl.ds(off, 64), :] = residual.astype(BF16)
            normed, inverse_root = norm_rows(t * rows + off, 64)
            grad = total(1, off)
            grad = inverse_root * (
                grad
                - jnp.mean(grad, axis=1, keepdims=True)
                - normed * jnp.mean(grad * normed, axis=1, keepdims=True)
            ) + C[here, :].astype(F32)
            igrad[pl.ds(off, 64), :] = grad
            return sums[0] + square(residual), sums[1] + square(branch), sums[2] + square(grad)

        zero = jnp.zeros((1, 1), F32)
        sums = lax.fori_loop(0, rows // 64, part, (zero, zero, zero))
        spot = lax.broadcasted_iota(jnp.int32, (1, width), 1)
        SV[5:6, :] = jnp.where(
            spot == 0, sums[0], jnp.where(spot == 1, sums[1], jnp.where(spot == 2, sums[2], 0.0))
        )

    def share(over, offset):
        if over == 0:
            slot, mate = t, (dp, lax.rem(t + offset, 4))
        else:
            slot, mate = 4 + dp, (lax.rem(dp + offset, ring), t)
        return remote(ES.at[over], EX.at[slot], e_s.at[over, offset], e_r.at[over, offset], mate)

    members = (4, ring)

    def share_send(over):
        ES[over] = SV[...]
        EX[(4 * over) + (dp if over else t)] = SV[...]
        for offset in range(1, members[over]):
            share(over, offset).start()

    def share_receive(over):
        for offset in range(1, members[over]):
            share(over, offset).wait_recv()
        total = EX[4 * over]
        for number in range(1, members[over]):
            total = total + EX[4 * over + number]
        if over == 0:
            row = lax.broadcasted_iota(jnp.int32, SV.shape, 0)
            total = jnp.where(row < 6, total, SV[...])
        SV[...] = total

    def chunk(direction, step):
        return lax.rem(at + ring - step, ring) if direction == 0 else lax.rem(at + step, ring)

    def gathered(direction, step):
        return lax.rem(at + 1 + ring - step, ring) if direction == 0 else lax.rem(at + ring - 1 + step, ring)

    def own_partial(segment, step):
        for direction in range(2):
            number = chunk(direction, step)
            columns = pl.ds(pl.multiple_of(number * 128, 128), 128)
            if segment < 2:
                left, right = (HID, C) if segment == 0 else (FI, PG)
                PSC[direction] = dot_tn(left[:, columns], right[:, direction * 512 : (direction + 1) * 512])
            else:
                PSC[direction, :, 0:384] = dot_tn(AI[:, columns], QG[:, direction * 384 : (direction + 1) * 384])
                PSC[direction, :, 384:512] = dot_tn(
                    CTX[:, direction * 128 : (direction + 1) * 128], C[:, columns]
                )

    def scatter(segment, direction, part, step):
        return remote(
            RSB.at[segment, direction, part, step], RSB.at[segment, direction, part, step + 1],
            r_s.at[segment, direction, part, step], r_r.at[segment, direction, part, step], onward[direction],
        )

    def collect(segment, direction, part, step):
        piece = GB.at[segment, direction, part, gathered(direction, step)]
        sem = ring - 1 + step
        return remote(
            piece, piece,
            r_s.at[segment, direction, part, sem], r_r.at[segment, direction, part, sem], onward[direction],
        )

    pieces = [(part, direction) for part in range(PARTS) for direction in range(2)]

    def ring_open(segment):
        own_partial(segment, 0)
        for part, direction in pieces:
            RSB[segment, direction, part, 0] = PSC[direction, :, part * 128 : (part + 1) * 128].astype(BF16)
            scatter(segment, direction, part, 0).start()

    def ring_scatter(segment, step):
        for part, direction in pieces:
            scatter(segment, direction, part, step - 1).wait_recv()
            RSB[segment, direction, part, step] = (
                RSB[segment, direction, part, step].astype(F32)
                + PSC[direction, :, part * 128 : (part + 1) * 128]
            ).astype(BF16)
            scatter(segment, direction, part, step).start()

    def ring_turn(segment):
        last = ring - 1
        for part, direction in pieces:
            scatter(segment, direction, part, last - 1).wait_recv()
            GB[segment, direction, part, gathered(direction, 0)] = (
                RSB[segment, direction, part, last].astype(F32)
                + PSC[direction, :, part * 128 : (part + 1) * 128]
            ).astype(BF16)
            collect(segment, direction, part, 0).start()

    def ring_collect(segment, step):
        for part, direction in pieces:
            collect(segment, direction, part, step - 1).wait_recv()
            collect(segment, direction, part, step).start()

    def ring_close(segment):
        for part, direction in pieces:
            collect(segment, direction, part, ring - 2).wait_recv()

    for copy in local[:3]:
        copy.wait()

    @pl.loop(0, 4)
    def _(step):
        @pl.when(step == 1)
        def _():
            gather(0, 0).wait_recv()

        @pl.when(step == 2)
        def _():
            gather(0, 1).wait_recv()
            gather(0, 3).start()
            gather(0, 2).wait_recv()
            gather(0, 4).start()

        @pl.when(step == 3)
        def _():
            gather(0, 3).wait_recv()
            gather(0, 4).wait_recv()

        forward_block(2 * lax.rem(x + lax.div(step, 2), 2) + lax.rem(core + lax.rem(step, 2), 2))

    for copy in local[3:]:
        copy.wait()

    def place_of(step):
        return 2 * lax.rem(x + lax.div(step, 2), 2) + lax.rem(core + lax.rem(step, 2), 2)

    gather(1, 1).wait_recv()
    gather(1, 3).start()
    cotangent_block(place_of(0))
    gather(1, 0).wait_recv()
    gather(1, 2).wait_recv()
    gather(1, 4).start()
    gather(1, 3).wait_recv()
    gather(1, 4).wait_recv()

    turns = ring - 1

    def during(condition, work):
        pl.when(condition)(work)

    ring_open(0)

    @pl.loop(1, 4)
    def _(step):
        cotangent_block(place_of(step))

    ring_open(1)

    @pl.loop(1, turns)
    def _(step):
        for segment in range(2):
            own_partial(segment, step)
            ring_scatter(segment, step)

        @pl.loop(2 * step - 2, 2 * step)
        def _(unit):
            attention_unit(unit)

    for segment in range(2):
        own_partial(segment, turns)
        ring_turn(segment)

    @pl.loop(1, 3)
    def _(step):
        @pl.loop(2 * step + 10, 2 * step + 12)
        def _(unit):
            attention_unit(unit)

        for segment in range(2):
            ring_collect(segment, step)

    @pl.loop(0, blocks)
    def _(block):
        assemble(block)

    ring_open(2)

    @pl.loop(3, turns)
    def _(step):
        for segment in range(2):
            ring_collect(segment, step)
        own_partial(2, step - 2)
        ring_scatter(2, step - 2)

        @pl.when(step <= 4)
        def _():
            @pl.loop(2 * step - 6, 2 * step - 4)
            def _(number):
                back_block(number)

        @pl.when(step == 5)
        def _():
            @pl.loop(0, 4)
            def _(number):
                branch_block(number)

            chip_sum(1)

        during(step == 6, lambda: chip_sum(0))

    for segment in range(2):
        ring_close(segment)

    @pl.loop(5, turns)
    def _(step):
        own_partial(2, step)
        ring_scatter(2, step)

    own_partial(2, turns)
    ring_turn(2)

    @pl.loop(1, turns)
    def _(step):
        ring_collect(2, step)

        @pl.when(step == 3)
        def _():
            finish()
            share_send(0)

        @pl.when(step == 5)
        def _():
            share_receive(0)
            share_send(1)

    ring_close(2)
    share_receive(1)

    for which in range(2):
        for kind in range(5):
            gather(which, kind).wait_send()
        for slot in range(2):
            to_core(which, slot).wait_send()
        to_x(which).wait_send()
    for over in range(2):
        for offset in range(1, members[over]):
            share(over, offset).wait_send()
    for segment in range(3):

        @pl.loop(0, ring - 1)
        def _(step):
            for part, direction in pieces:
                scatter(segment, direction, part, step).wait_send()
                collect(segment, direction, part, step).wait_send()


def angle_parts(seq_len):
    inverse = 10000.0 ** (-(np.arange(ROT // 2) * 2.0 / ROT))
    per_lane = np.zeros((128,))
    for start in (0, ROT // 2, HD, HD + ROT // 2):
        per_lane[start : start + ROT // 2] = inverse
    coarse = (np.arange(seq_len // 32) * 32.0)[:, None] * per_lane[None, :]
    fine = np.arange(32.0)[:, None] * per_lane[None, :]
    return [f(a).astype(np.float32) for a in (coarse, fine) for f in (np.cos, np.sin)]


def per_device_fused(
    tokens, cotangent, gain_attn, bias_attn, gain_mlp, bias_mlp, qkv_weight, qkv_bias,
    out_weight, out_bias, up_weight, up_bias, down_weight, down_bias,
):
    rows, width = tokens.shape
    ring = lax.axis_size("dp")
    seq = rows * lax.axis_size("tensor")
    heads = out_weight.shape[0] // HD
    hidden_width = up_weight.shape[1]
    qkv_width = qkv_weight.shape[1]
    cos_a, sin_a, cos_b, sin_b = angle_parts(seq)
    vmem = pl.BlockSpec(memory_space=pltpu.VMEM)
    hbm = pl.BlockSpec(memory_space=pl.ANY)
    V = pltpu.VMEM
    D = pltpu.SemaphoreType.DMA
    scratch = [
        V((seq, width), BF16), V((seq, width), BF16), V((seq, width), BF16), V((seq, width), BF16),
        V((seq, hidden_width), BF16), V((seq, hidden_width), F32), V((seq, hidden_width), BF16),
        V((seq, qkv_width), BF16),
        V((heads, seq, HD), BF16), V((heads, seq, HD), BF16), V((heads, seq, HD), BF16),
        V((heads, seq, HD), BF16), V((heads, seq, HD), BF16), V((seq, heads * HD), BF16),
        V((heads, seq, HD), F32), V((heads, HD, seq), F32), V((heads, HD, seq), F32),
        V((seq, 128), F32), V((seq, 128), F32),
        V(qkv_weight.shape, BF16), V(out_weight.shape, BF16), V(up_weight.shape, BF16), V(down_weight.shape, BF16),
        V((3, 2, PARTS, ring, 128, 128), BF16), V((2, 128, 512), F32),
        V((2, seq, width), BF16), V((2, 2, rows, width), BF16), V((2, rows, width), BF16),
        V((2, 8, width), F32), V((4 + ring, 8, width), F32),
        D((6,)), D((2, 5)), D((2, 5)),
        D((3, 2, PARTS, 2 * ring - 2)), D((3, 2, PARTS, 2 * ring - 2)),
        D((2, 3)), D((2, 3)), D((2, ring)), D((2, ring)),
    ]
    mixed, input_grad, gradients, sums = pl.pallas_call(
        functools.partial(fused_kernel, ring),
        out_shape=[
            V((rows, width), BF16),
            V((rows, width), F32),
            V((3, 2, PARTS, ring, 128, 128), BF16),
            V((8, width), F32),
        ],
        in_specs=[hbm, hbm] + [vmem] * 8 + [hbm] * 4 + [vmem] * 4,
        out_specs=[vmem] * 4,
        scratch_shapes=scratch,
        compiler_params=pltpu.CompilerParams(
            collective_id=0, has_side_effects=True, vmem_limit_bytes=VMEM_LIMIT
        ),
        name="layer",
    )(
        tokens, cotangent,
        *(v.reshape(1, -1) for v in (gain_attn, bias_attn, gain_mlp, bias_mlp, out_bias, down_bias)),
        qkv_bias, up_bias.reshape(1, -1),
        qkv_weight, out_weight, up_weight, down_weight, cos_a, sin_a, cos_b, sin_b,
    )
    elements = rows * width * ring * lax.axis_size("tensor")
    return closing(mixed, input_grad, gradients, sums, elements, down_weight, up_weight, qkv_weight, out_weight)


def closing_kernel(
    elements,
    mixed, igrad, GB, SV,
    mixed_o, igrad_o, ga_o, ba_o, gm_o, bm_o, gq_o, bqkv_o, go_o, bo_o, gu_o, bup_o, gd_o, bd_o, stats_o,
    SD, SU, SQ, SO, sems, msem,
):
    copies = [
        pltpu.make_async_copy(mixed, mixed_o, msem.at[0]),
        pltpu.make_async_copy(igrad, igrad_o, msem.at[1]),
    ]
    for copy in copies:
        copy.start()
    for segment, stage in enumerate((SD, SU, SQ)):
        for number in range(GB.shape[3]):
            there = slice(number * 128, number * 128 + 128)
            for direction in range(2):
                for part in range(PARTS):
                    piece = GB[segment, direction, part, number].astype(F32)
                    if segment == 2 and part == 3:
                        SO[direction * 128 : direction * 128 + 128, there] = piece
                    else:
                        column = direction * (384 if segment == 2 else 512) + part * 128
                        stage[there, column : column + 128] = piece
            rows = pl.ds(number * 128, 128)
            copy = pltpu.make_async_copy(
                stage.at[rows], (gd_o, gu_o, gq_o)[segment].at[rows], sems.at[segment, number]
            )
            copy.start()
            copies.append(copy)
    copies.append(pltpu.make_async_copy(SO, go_o, msem.at[2]))
    copies[-1].start()
    for row, out in enumerate((ga_o, ba_o, gm_o, bm_o, bo_o)):
        out[...] = SV[row : row + 1, :]
    bd_o[...] = SV[4:5, :]
    bup_o[...] = SV[6:7, :]
    bqkv_o[...] = SV[7, : bqkv_o.shape[0]]
    stats_o[...] = jnp.sqrt(SV[5, : stats_o.shape[0]] * (1.0 / elements))
    for copy in copies:
        copy.wait()


def closing(mixed, input_grad, gradients, sums, elements, down_weight, up_weight, qkv_weight, out_weight):
    hbm = pl.BlockSpec(memory_space=pl.ANY)
    vmem = pl.BlockSpec(memory_space=pltpu.VMEM)

    def like(array, dtype=F32):
        return jax.ShapeDtypeStruct(array.shape, dtype)

    width = sums.shape[1]
    row = jax.ShapeDtypeStruct((1, width), F32)
    outs = pl.pallas_call(
        functools.partial(closing_kernel, elements),
        in_specs=[vmem] * 4,
        out_specs=[
            hbm, hbm, vmem, vmem, vmem, vmem, hbm, vmem, hbm, vmem, hbm, vmem, hbm, vmem, vmem,
        ],
        out_shape=[
            like(mixed, BF16), like(input_grad), row, row, row, row,
            like(qkv_weight), jax.ShapeDtypeStruct((qkv_weight.shape[1],), F32), like(out_weight), row,
            like(up_weight), row, like(down_weight), row, jax.ShapeDtypeStruct((3,), F32),
        ],
        scratch_shapes=[
            pltpu.VMEM(down_weight.shape, F32),
            pltpu.VMEM(up_weight.shape, F32),
            pltpu.VMEM(qkv_weight.shape, F32),
            pltpu.VMEM(out_weight.shape, F32),
            pltpu.SemaphoreType.DMA((3, gradients.shape[3])),
            pltpu.SemaphoreType.DMA((3,)),
        ],
        compiler_params=pltpu.CompilerParams(vmem_limit_bytes=24 << 20),
        name="outputs",
    )(mixed, input_grad, gradients, sums)
    return tuple(out.reshape(-1) if out.shape == (1, width) else out for out in outs)


def solution(mesh):
    in_specs = (
        P(("dp", "tensor"), None),
        P(("dp", "tensor"), None),
        P(),
        P(),
        P(),
        P(),
        P(None, "tensor"),
        P("tensor"),
        P("tensor", None),
        P(),
        P(None, "tensor"),
        P("tensor"),
        P("tensor", None),
        P(),
    )
    out_specs = (
        P(("dp", "tensor"), None),
        P(("dp", "tensor"), None),
        P(),
        P(),
        P(),
        P(),
        P(None, "tensor"),
        P("tensor"),
        P("tensor", None),
        P(),
        P(None, "tensor"),
        P("tensor"),
        P("tensor", None),
        P(),
        P(),
    )
    fused = mesh.shape["tensor"] == 4 and mesh.shape["dp"] == 8
    return jax.shard_map(
        per_device_fused if fused else per_device, mesh=mesh, in_specs=in_specs, out_specs=out_specs, check_vma=False
    )
```

```python
import functools
import math

import jax
import jax.numpy as jnp
import numpy as np
from jax import lax
from jax.experimental import pallas as pl
from jax.experimental.pallas import tpu as pltpu
from jax.sharding import PartitionSpec as P

HD = 64
ROT = 16
VMEM_LIMIT = 54 << 20


epsilon = 1e-05


def angle_tables(seq_len):
    positions = jnp.arange(seq_len, dtype=jnp.float32)
    inverse = 10000.0 ** (-(jnp.arange(ROT // 2, dtype=jnp.float32) * 2.0 / ROT))
    angles = positions[:, None] * inverse[None, :]
    cosine = jnp.concatenate([jnp.cos(angles), jnp.cos(angles)], axis=-1)[:, None, :]
    sine_part = jnp.concatenate([jnp.sin(angles), jnp.sin(angles)], axis=-1)[:, None, :]
    return (cosine, sine_part)


def rotate(field_in, cosine, sine_part):
    half_rot = ROT // 2
    first_half = field_in[..., :half_rot]
    second = field_in[..., half_rot:ROT]
    turned = jnp.concatenate([-second, first_half], axis=-1)
    return jnp.concatenate(
        [field_in[..., :ROT] * cosine + turned * sine_part, field_in[..., ROT:]], axis=-1
    )


def unrotate(grad_in, cosine, sine_part):
    half_rot = ROT // 2
    head_part = grad_in[..., :ROT]
    scaled = head_part * sine_part
    turned = jnp.concatenate([scaled[..., half_rot:], -scaled[..., :half_rot]], axis=-1)
    return jnp.concatenate([head_part * cosine + turned, grad_in[..., ROT:]], axis=-1)


def normalize(raw_rows):
    average = jnp.mean(raw_rows, axis=-1, keepdims=True)
    centred = raw_rows - average
    spread = jnp.mean(centred * centred, axis=-1, keepdims=True)
    inverse_root = lax.rsqrt(spread + epsilon)
    return (centred * inverse_root, inverse_root)


def against(left, right):
    return lax.dot_general(
        left, right, (((1,), (1,)), ((), ())), preferred_element_type=jnp.float32
    )


def per_device(
    tokens,
    cotangent,
    gain_attn,
    bias_attn,
    gain_mlp,
    bias_mlp,
    qkv_weight,
    qkv_bias,
    out_weight,
    out_bias,
    up_weight,
    up_bias,
    down_weight,
    down_bias,
):
    own_rows = tokens.shape[0]
    model_width = tokens.shape[1]
    heads_here = out_weight.shape[0] // HD
    score_scale = HD ** (-0.5)
    whole_rows = lax.all_gather(tokens, "tensor", axis=0, tiled=True)
    seq_len = whole_rows.shape[0]
    normed, _ = normalize(whole_rows.astype(jnp.float32))
    attention_input = (normed * gain_attn + bias_attn).astype(jnp.bfloat16)
    feed_input = (normed * gain_mlp + bias_mlp).astype(jnp.bfloat16)
    projected = jnp.dot(attention_input, qkv_weight, preferred_element_type=jnp.float32) + qkv_bias
    projected = projected.reshape(seq_len, heads_here, 3, HD)
    cosine, sine_part = angle_tables(seq_len)
    queries = rotate(projected[:, :, 0], cosine, sine_part).astype(jnp.bfloat16)
    keys_all = rotate(projected[:, :, 1], cosine, sine_part).astype(jnp.bfloat16)
    values_all = projected[:, :, 2].astype(jnp.bfloat16)
    preact = jnp.dot(feed_input, up_weight, preferred_element_type=jnp.float32) + up_bias
    hidden = jax.nn.gelu(preact, approximate=False).astype(jnp.bfloat16)
    block_rows = min(512, seq_len)
    block_total = seq_len // block_rows
    key_positions = jnp.arange(seq_len, dtype=jnp.int32)

    def causal_mask(offset):
        return key_positions[None, :] <= (offset + jnp.arange(block_rows, dtype=jnp.int32))[:, None]

    def forward_block(number):
        offset = number * block_rows
        query_rows = lax.dynamic_slice_in_dim(queries, offset, block_rows, 0)
        scores = (
            jnp.einsum("qhd,khd->hqk", query_rows, keys_all, preferred_element_type=jnp.float32)
            * score_scale
        )
        scores = jnp.where(causal_mask(offset)[None], scores, -1e30)
        highest = jnp.max(scores, axis=-1, keepdims=True)
        weights = jnp.exp(scores - highest)
        totals = jnp.sum(weights, axis=-1, keepdims=True)
        soft_rows = (weights / totals).astype(jnp.bfloat16)
        context_rows = jnp.einsum(
            "hqk,khd->qhd", soft_rows, values_all, preferred_element_type=jnp.float32
        ).astype(jnp.bfloat16)
        log_totals = (highest + jnp.log(totals))[:, :, 0].T
        return (context_rows, log_totals)

    context_blocks, log_blocks = lax.map(forward_block, jnp.arange(block_total, dtype=jnp.int32))
    context = context_blocks.reshape(seq_len, heads_here * HD)
    log_sums = log_blocks.reshape(seq_len, heads_here)
    context_rows = context
    branch = lax.psum_scatter(
        jnp.dot(context_rows, out_weight, preferred_element_type=jnp.float32)
        + jnp.dot(hidden, down_weight, preferred_element_type=jnp.float32),
        "tensor",
        scatter_dimension=0,
        tiled=True,
    )
    branch = branch + out_bias + down_bias
    residual_out = tokens.astype(jnp.float32) + branch
    mixed_out = residual_out.astype(jnp.bfloat16)
    forward_squares = jnp.stack([jnp.sum(residual_out * residual_out), jnp.sum(branch * branch)])
    forward_totals = lax.psum(forward_squares, ("dp", "tensor"))
    upstream = lax.all_gather(cotangent, "tensor", axis=0, tiled=True)
    out_weight_grad = jnp.einsum("sa,sd->ad", context, upstream, preferred_element_type=jnp.float32)
    down_weight_grad = jnp.einsum("sf,sd->fd", hidden, upstream, preferred_element_type=jnp.float32)
    context_grad = against(upstream, out_weight).astype(jnp.bfloat16)
    hidden_grad = against(upstream, down_weight)
    normal_cdf = 0.5 * (1.0 + lax.erf(preact * 0.5**0.5))
    density = jnp.exp(-0.5 * preact * preact) * (1.0 / math.sqrt(2.0 * math.pi))
    preact_grad = (hidden_grad * (normal_cdf + preact * density)).astype(jnp.bfloat16)
    context_grad3 = context_grad.reshape(seq_len, heads_here, HD)

    def backward_block(carried, number):
        key_grad, value_grad = carried
        offset = number * block_rows
        query_rows = lax.dynamic_slice_in_dim(queries, offset, block_rows, 0)
        grad_rows = lax.dynamic_slice_in_dim(context_grad3, offset, block_rows, 0)
        log_rows = lax.dynamic_slice_in_dim(log_sums, offset, block_rows, 0).T
        scores = (
            jnp.einsum("qhd,khd->hqk", query_rows, keys_all, preferred_element_type=jnp.float32)
            * score_scale
        )
        soft_full = jnp.exp(
            jnp.where(causal_mask(offset)[None], scores - log_rows[:, :, None], -1e30)
        )
        prob_grad = jnp.einsum(
            "qhd,khd->hqk", grad_rows, values_all, preferred_element_type=jnp.float32
        )
        deltas = jnp.sum(soft_full * prob_grad, axis=-1, keepdims=True)
        score_grad = (soft_full * (prob_grad - deltas)).astype(jnp.bfloat16)
        query_grad = (
            jnp.einsum("hqk,khd->qhd", score_grad, keys_all, preferred_element_type=jnp.float32)
            * score_scale
        )
        key_grad = (
            key_grad
            + jnp.einsum("hqk,qhd->khd", score_grad, query_rows, preferred_element_type=jnp.float32)
            * score_scale
        )
        value_grad = value_grad + jnp.einsum(
            "hqk,qhd->khd",
            soft_full.astype(jnp.bfloat16),
            grad_rows,
            preferred_element_type=jnp.float32,
        )
        return ((key_grad, value_grad), query_grad)

    empty = jnp.zeros((seq_len, heads_here, HD), jnp.float32)
    (key_grad, value_grad), query_blocks = lax.scan(
        backward_block, (empty, empty), jnp.arange(block_total, dtype=jnp.int32)
    )
    query_grad = unrotate(query_blocks.reshape(seq_len, heads_here, HD), cosine, sine_part)
    key_grad = unrotate(key_grad, cosine, sine_part)
    qkv_grad = (
        jnp.stack([query_grad, key_grad, value_grad], axis=2)
        .reshape(seq_len, 3 * heads_here * HD)
        .astype(jnp.bfloat16)
    )
    qkv_weight_grad = jnp.einsum(
        "sd,sc->dc", attention_input, qkv_grad, preferred_element_type=jnp.float32
    )
    qkv_bias_grad = jnp.sum(qkv_grad, axis=0, dtype=jnp.float32)
    up_weight_grad = jnp.einsum(
        "sd,sf->df", feed_input, preact_grad, preferred_element_type=jnp.float32
    )
    up_bias_grad = jnp.sum(preact_grad, axis=0, dtype=jnp.float32)
    own_normed, own_scale = normalize(tokens.astype(jnp.float32))
    attention_back = against(qkv_grad, qkv_weight)
    feed_back = against(preact_grad, up_weight)
    gain_terms = jnp.stack(
        [
            jnp.sum(normed * attention_back, axis=0),
            jnp.sum(attention_back, axis=0),
            jnp.sum(normed * feed_back, axis=0),
            jnp.sum(feed_back, axis=0),
        ]
    )
    normed_grad = lax.psum_scatter(
        (attention_back * gain_attn + feed_back * gain_mlp).astype(jnp.bfloat16),
        "tensor",
        scatter_dimension=0,
        tiled=True,
    ).astype(jnp.float32)
    centred_term = (
        normed_grad
        - jnp.mean(normed_grad, axis=-1, keepdims=True)
        - own_normed * jnp.mean(normed_grad * own_normed, axis=-1, keepdims=True)
    )
    input_grad = own_scale * centred_term + cotangent.astype(jnp.float32)
    (
        qkv_weight_grad,
        qkv_bias_grad,
        out_weight_grad,
        up_weight_grad,
        up_bias_grad,
        down_weight_grad,
    ) = lax.psum(
        (
            qkv_weight_grad,
            qkv_bias_grad,
            out_weight_grad,
            up_weight_grad,
            up_bias_grad,
            down_weight_grad,
        ),
        "dp",
    )
    bias_rows = jnp.sum(cotangent, axis=0, dtype=jnp.float32)
    grad_square = jnp.sum(input_grad * input_grad)
    gain_totals, bias_totals, grad_total = lax.psum(
        (gain_terms, bias_rows, grad_square), ("dp", "tensor")
    )
    square_totals = jnp.concatenate([forward_totals, grad_total[None]])
    elements = own_rows * model_width * lax.axis_size("dp") * lax.axis_size("tensor")
    statistics = jnp.sqrt(square_totals / elements)
    return (
        mixed_out,
        input_grad,
        gain_totals[0],
        gain_totals[1],
        gain_totals[2],
        gain_totals[3],
        qkv_weight_grad,
        qkv_bias_grad,
        out_weight_grad,
        bias_totals,
        up_weight_grad,
        up_bias_grad,
        down_weight_grad,
        bias_totals,
        statistics,
    )


F32 = jnp.float32
BF16 = jnp.bfloat16
MESH = pl.DeviceIdType.MESH
TILE = 256
PARTS = 4
TOGETHER = (1, 2, 1)


def dot_nn(left, right):
    return jnp.dot(left, right, preferred_element_type=F32)


def dot_nt(left, right):
    return lax.dot_general(left, right, (((1,), (1,)), ((), ())), preferred_element_type=F32)


def dot_tn(left, right):
    return lax.dot_general(left, right, (((0,), (0,)), ((), ())), preferred_element_type=F32)


def fused_kernel(
    ring,
    tok, cot, ga, ba, gm, bm, bo, bd, bqkv, bup, wqkv_h, wout_h, wup_h, wdn_h, cos_a, sin_a, cos_b, sin_b,
    mixed, igrad, GB, SUMS, SQO,
    T, CB, AI, FI, HID, GP, PG, QG, QH, KH, VH, CGH, CTXH, CTX, DQ, DKT, DVT, COS, SIN,
    WQKV, WOUT, WUP, WDN, RSB, PSD, PSC, PART, RA, RB, SV, ES, EX, EROWS, EY, SQ, EQ, EZ,
    lsem, g_s, g_r, r_s, r_r, b_s, b_r, e_s, e_r,
):
    rows = tok.shape[0]
    width = tok.shape[1]
    seq = T.shape[0]
    heads = QH.shape[0]
    hidden_width = WUP.shape[1]
    half_rows = rows // 2
    blocks = seq // TILE
    scale = HD ** (-0.5)
    dp = lax.axis_index("dp")
    t = lax.axis_index("tensor")
    core = lax.rem(t, 2)
    x = lax.div(t, 2)
    depth = ring // 2
    y = lax.rem(dp, 2)
    z = lax.div(dp, 2)
    at = z + y * (2 * depth - 1 - 2 * z)

    def ring_device(place):
        ny = lax.div(place, depth)
        return (2 * (place + ny * (2 * depth - 1 - 2 * place)) + ny, t)

    following = ring_device(lax.rem(at + 1, ring))
    previous = ring_device(lax.rem(at + ring - 1, ring))
    onward = (following, previous)
    core_mate = (dp, t + 1 - 2 * core)
    x_block = 2 * (1 - x) + core
    x_mate = (dp, x_block)

    def remote(src, dst, send, recv, device):
        return pltpu.make_async_remote_copy(
            src_ref=src, dst_ref=dst, send_sem=send, recv_sem=recv, device_id=device, device_id_type=MESH
        )

    def gather(which, kind):
        sems = (g_s.at[which, kind], g_r.at[which, kind])
        own = pl.ds(t * rows, rows)
        there = pl.ds(x_block * rows, rows)
        if which == 1:
            if kind == 0:
                return remote(CB.at[:, :, own], CB.at[:, :, own], *sems, core_mate)
            if kind <= PARTS:
                return remote(CB.at[kind - 1, :, own], CB.at[kind - 1, :, own], *sems, x_mate)
            piece = CB.at[kind - 1 - PARTS, :, there]
            return remote(piece, piece, *sems, core_mate)
        if kind == 0:
            return remote(tok, T.at[own], *sems, core_mate)
        if kind <= 2:
            off = (kind - 1) * half_rows
            return remote(tok.at[pl.ds(off, half_rows)], T.at[pl.ds(t * rows + off, half_rows)], *sems, x_mate)
        part = T.at[pl.ds(x_block * rows + (kind - 3) * half_rows, half_rows)]
        return remote(part, part, *sems, core_mate)

    kinds = (5, 1 + 2 * PARTS)

    def upstream_rows(here):
        return jnp.concatenate([CB[part, direction, here, :] for direction in range(2) for part in range(PARTS)], axis=1)

    local = [
        pltpu.make_async_copy(tok, T.at[pl.ds(t * rows, rows)], lsem.at[0]),
        pltpu.make_async_copy(wqkv_h, WQKV, lsem.at[2]),
        pltpu.make_async_copy(wup_h, WUP, lsem.at[3]),
        *(
            pltpu.make_async_copy(
                cot.at[:, pl.ds(direction * 512 + part * 128, 128)],
                CB.at[part, direction, pl.ds(t * rows, rows)],
                lsem.at[6 + 2 * part + direction],
            )
            for part in range(PARTS)
            for direction in range(2)
        ),
        pltpu.make_async_copy(wdn_h, WDN, lsem.at[4]),
        pltpu.make_async_copy(wout_h, WOUT, lsem.at[5]),
    ]
    for copy in local:
        copy.start()
    barrier = pltpu.get_barrier_semaphore()
    for mate in (core_mate, x_mate, following, previous):
        pl.semaphore_signal(barrier, inc=1, device_id=mate, device_id_type=MESH)
    pl.semaphore_wait(barrier, 4)
    gather(0, 1).start()
    gather(0, 2).start()
    gather(0, 0).start()

    @pl.loop(0, seq // 32)
    def _(a):
        ca, sa = cos_a[pl.ds(a, 1), :], sin_a[pl.ds(a, 1), :]
        cb, sb = cos_b[...], sin_b[...]
        COS[pl.ds(a * 32, 32), :] = ca * cb - sa * sb
        SIN[pl.ds(a * 32, 32), :] = sa * cb + ca * sb

    SV[...] = jnp.zeros_like(SV)
    SQ[...] = jnp.zeros_like(SQ)

    @pl.loop(0, heads)
    def _(h):
        DKT[h] = jnp.zeros(DKT.shape[1:], F32)
        DVT[h] = jnp.zeros(DVT.shape[1:], F32)


    def tables(base, group, count):
        lane = lax.broadcasted_iota(jnp.int32, (count, 128), 1)
        low_lane = jnp.where(lane >= 64, lane - 64, lane)
        cosine, sine = COS[pl.ds(base, count), :], SIN[pl.ds(base, count), :]
        if group == 1:
            cosine = jnp.where(lane >= 64, cosine, 1.0)
            sine = jnp.where(lane >= 64, sine, 0.0)
        if group == 2:
            cosine = jnp.where(lane < 64, cosine, 1.0)
            sine = jnp.where(lane < 64, sine, 0.0)
        upper = jnp.where(low_lane >= ROT // 2, sine, 0.0)
        return cosine, upper, sine - upper

    def norm_rows(base, count):
        raw = T[pl.ds(base, count), :].astype(F32)
        centred = raw - jnp.mean(raw, axis=1, keepdims=True)
        inverse_root = lax.rsqrt(jnp.mean(centred * centred, axis=1, keepdims=True) + epsilon)
        return centred * inverse_root, inverse_root

    def forward_block(block, half):
        base = pl.multiple_of(block * rows + half * half_rows, half_rows)

        @pl.loop(0, half_rows // 64)
        def _(part):
            off = pl.multiple_of(base + part * 64, 64)
            normed, _ = norm_rows(off, 64)
            AI[pl.ds(off, 64), :] = (normed * ga[...] + ba[...]).astype(BF16)
            FI[pl.ds(off, 64), :] = (normed * gm[...] + bm[...]).astype(BF16)

        for group in range(3 * heads // 2):
            if group % 2 == 0:
                columns = slice(group * 128, group * 128 + 256)
                pair = dot_nn(AI[pl.ds(base, half_rows), :], WQKV[:, columns]) + bqkv[columns].reshape(1, 256)
            value = pair[:, (group % 2) * 128 : (group % 2) * 128 + 128]
            cosine, upper, lower = tables(base, group % 3, half_rows)
            turned = (
                value * cosine
                - lower * pltpu.roll(value, 128 - ROT // 2, 1)
                + upper * pltpu.roll(value, ROT // 2, 1)
            ).astype(BF16)
            first = 2 * (group // 3)
            left, left_head = ((QH, first), (VH, first), (KH, first + 1))[group % 3]
            right, right_head = ((KH, first), (QH, first + 1), (VH, first + 1))[group % 3]
            left[left_head, pl.ds(base, half_rows), :] = turned[:, :HD]
            right[right_head, pl.ds(base, half_rows), :] = turned[:, HD:]

        for part in range(hidden_width // TILE):
            columns = slice(part * TILE, (part + 1) * TILE)
            preact = dot_nn(FI[pl.ds(base, half_rows), :], WUP[:, columns]) + bup[:, columns]
            cdf = 0.5 * (1.0 + lax.erf(preact * 0.5**0.5))
            density = jnp.exp(-0.5 * preact * preact) * (1.0 / math.sqrt(2.0 * math.pi))
            HID[pl.ds(base, half_rows), columns] = (preact * cdf).astype(BF16)
            GP[pl.ds(base, half_rows), columns] = cdf + preact * density

    def cotangent_block(block):
        base = pl.multiple_of(block * rows, rows)
        upstream = upstream_rows(pl.ds(base, rows))
        grad = dot_nt(upstream, WOUT[...]).astype(BF16)
        for h in range(heads):
            CGH[h, pl.ds(base, rows), :] = grad[:, h * HD : (h + 1) * HD]

        for part in range(hidden_width // TILE):
            columns = slice(part * TILE, (part + 1) * TILE)
            back = dot_nt(upstream, WDN[columns, :])
            rounded = (back * GP[pl.ds(base, rows), columns]).astype(BF16)
            PG[pl.ds(base, rows), columns] = rounded
            SV[6:7, columns] += jnp.sum(rounded.astype(F32), axis=0, keepdims=True)

    def attention_rows(h, own):
        here = slice(own * TILE, (own + 1) * TILE)
        before = own * TILE
        reach = before + TILE
        query = QH[h, here, :]
        grad = CGH[h, here, :]
        keys = KH[h, :reach, :]
        values = VH[h, :reach, :]
        scores = dot_nt(query, keys) * scale
        row_at = lax.broadcasted_iota(jnp.int32, (TILE, TILE), 0)
        column_at = lax.broadcasted_iota(jnp.int32, (TILE, TILE), 1)
        corner = jnp.where(column_at <= row_at, scores[:, before:], -1e30)
        scores = jnp.concatenate([scores[:, :before], corner], axis=1) if own else corner
        weights = jnp.exp(scores - jnp.max(scores, axis=1, keepdims=True))
        probs = weights * (1.0 / jnp.sum(weights, axis=1, keepdims=True))
        soft = probs.astype(BF16)
        CTXH[h, here, :] = dot_nn(soft, values).astype(BF16)
        prob_grad = dot_nt(grad, values)
        delta = jnp.sum(probs * prob_grad, axis=1, keepdims=True)
        score_grad = (probs * (prob_grad - delta)).astype(BF16)
        DQ[h, here, :] = scale * dot_nn(score_grad, keys)
        DKT[h, :, :reach] += dot_nn(query.astype(F32).T.astype(BF16), score_grad)
        DVT[h, :, :reach] += dot_nn(grad.astype(F32).T.astype(BF16), soft)

    def attention_unit(unit):
        h = lax.div(unit, blocks)
        for number, own in enumerate(sorted(range(blocks), key=lambda own: min(own, blocks - 1 - own))):
            pl.when(lax.rem(unit, blocks) == number)(functools.partial(attention_rows, h, own))

    def assemble(block):
        base = pl.multiple_of(block * TILE, TILE)
        here = pl.ds(base, TILE)
        for pair in range(heads // 2):
            one, two = 2 * pair, 2 * pair + 1
            CTX[here, pair * 128 : (pair + 1) * 128] = jnp.concatenate(
                [CTXH[one, here, :], CTXH[two, here, :]], axis=1
            )
            parts = [
                (DQ[one, here, :], scale * DKT[one, :, here].T),
                (DVT[one, :, here].T, DQ[two, here, :]),
                (scale * DKT[two, :, here].T, DVT[two, :, here].T),
            ]
            for group, (left, right) in enumerate(parts):
                grad = jnp.concatenate([left, right], axis=1)
                cosine, upper, lower = tables(base, group, TILE)
                turned = (
                    grad * cosine
                    + pltpu.roll(grad * upper, 128 - ROT // 2, 1)
                    - pltpu.roll(grad * lower, ROT // 2, 1)
                ).astype(BF16)
                columns = slice((3 * pair + group) * 128, (3 * pair + group + 1) * 128)
                QG[here, columns] = turned
                SV[7:8, columns] += jnp.sum(turned.astype(F32), axis=0, keepdims=True)

    def order(step):
        flip_core = 1 - lax.div(step, 2)
        flip_x = 1 - lax.rem(step, 2)
        return 2 * lax.rem(x + flip_x, 2) + lax.rem(core + flip_core, 2)

    def to_core(which, slot):
        block = (2 * x + 1 - core) if slot == 0 else (2 * (1 - x) + 1 - core)
        return remote(
            PART.at[which, pl.ds(block * rows, rows)], RA.at[which, slot],
            b_s.at[which, slot], b_r.at[which, slot], core_mate,
        )

    def to_x(which):
        return remote(
            PART.at[which, pl.ds(x_block * rows, rows)], RB.at[which],
            b_s.at[which, 2], b_r.at[which, 2], x_mate,
        )

    def send_after(which, step):
        @pl.when(step == 0)
        def _():
            to_core(which, 1).start()

        @pl.when(step == 1)
        def _():
            to_core(which, 0).start()

    def branch_block(step):
        base = pl.multiple_of(order(step) * rows, rows)
        here = pl.ds(base, rows)

        for part in range(width // TILE):
            columns = slice(part * TILE, (part + 1) * TILE)
            PART[0, here, columns] = (
                dot_nn(CTX[here, :], WOUT[:, columns]) + dot_nn(HID[here, :], WDN[:, columns])
            ).astype(BF16)

        send_after(0, step)

    def back_block(step):
        base = pl.multiple_of(order(step) * rows, rows)
        here = pl.ds(base, rows)
        raw = T[here, :].astype(F32)
        average = jnp.mean(raw, axis=1, keepdims=True)
        spread = jnp.mean((raw - average) * (raw - average), axis=1, keepdims=True)
        inverse_root = lax.rsqrt(spread + epsilon)

        for part in range(width // TILE):
            columns = slice(part * TILE, (part + 1) * TILE)
            normed = (T[here, columns].astype(F32) - average) * inverse_root
            attention_back = dot_nt(QG[here, :], WQKV[columns, :])
            feed_back = dot_nt(PG[here, :], WUP[columns, :])
            SV[0:1, columns] += jnp.sum(normed * attention_back, axis=0, keepdims=True)
            SV[1:2, columns] += jnp.sum(attention_back, axis=0, keepdims=True)
            SV[2:3, columns] += jnp.sum(normed * feed_back, axis=0, keepdims=True)
            SV[3:4, columns] += jnp.sum(feed_back, axis=0, keepdims=True)
            PART[1, here, columns] = (attention_back * ga[:, columns] + feed_back * gm[:, columns]).astype(BF16)

        send_after(1, step)

    def chip_sum(which):
        to_core(which, 1).wait_recv()
        there = pl.ds(pl.multiple_of(x_block * rows, rows), rows)
        PART[which, there, :] = (PART[which, there, :].astype(F32) + RA[which, 1].astype(F32)).astype(BF16)
        to_x(which).start()

    def finish_start():
        for which in range(2):
            to_core(which, 0).wait_recv()
            to_x(which).wait_recv()
    def total(which, off):
        return (
            PART[which, pl.ds(pl.multiple_of(t * rows + off, 64), 64), :].astype(F32)
            + RA[which, 0, pl.ds(off, 64), :].astype(F32)
            + RB[which, pl.ds(off, 64), :].astype(F32)
        )

    def square(value):
        return jnp.sum(jnp.sum(value * value, axis=1, keepdims=True), axis=0, keepdims=True)

    def finish_part(number):
        off = pl.multiple_of(number * 64, 64)
        here = pl.ds(pl.multiple_of(t * rows + off, 64), 64)
        branch = total(0, off) + bo[...] + bd[...]
        residual = T[here, :].astype(F32) + branch
        mixed[pl.ds(off, 64), :] = residual.astype(BF16)
        normed, inverse_root = norm_rows(t * rows + off, 64)
        grad = total(1, off)
        grad = inverse_root * (
            grad
            - jnp.mean(grad, axis=1, keepdims=True)
            - normed * jnp.mean(grad * normed, axis=1, keepdims=True)
        ) + upstream_rows(here).astype(F32)
        igrad[pl.ds(off, 64), :] = grad
        spot = lax.broadcasted_iota(jnp.int32, SQ.shape, 1)
        for place, value in enumerate((residual, branch, grad)):
            SQ[...] += jnp.where(spot == place, square(value), 0.0)

    members = (4, ring, ring, 4, ring)

    def share(stage, offset):
        over_tensor = stage in (0, 3)
        mate = (dp, lax.rem(t + offset, 4)) if over_tensor else (lax.rem(dp + offset, ring), t)
        src, dst = (
            lambda: (ES, EX.at[t]),
            lambda: (EROWS.at[lax.rem(dp + offset, ring)], EY.at[dp]),
            lambda: (SUMS.at[dp], SUMS.at[dp]),
            lambda: (EQ.at[0], EZ.at[t]),
            lambda: (EQ.at[1], EZ.at[4 + dp]),
        )[stage]()
        number = sum(members[:stage]) - stage + offset - 1
        return remote(src, dst, e_s.at[number], e_r.at[number], mate)

    def share_start(stage):
        for offset in range(1, members[stage]):
            share(stage, offset).start()

    def share_wait(stage):
        for offset in range(1, members[stage]):
            share(stage, offset).wait_recv()

    def added(ref, first, count):
        total = ref[first]
        for number in range(1, count):
            total = total + ref[first + number]
        return total

    def share_tensor():
        ES[...] = SV[...]
        EX[t] = SV[...]
        share_start(0)

    def share_rows():
        share_wait(0)
        row = lax.broadcasted_iota(jnp.int32, SV.shape, 0)
        total = jnp.where(row < 5, added(EX, 0, 4), SV[...])
        for place in range(ring):
            EROWS[:, place, :] = total[:, place * 128 : (place + 1) * 128]
        EY[dp] = EROWS[dp]
        share_start(1)

    def share_gather():
        share_wait(1)
        SUMS[dp] = added(EY, 0, ring)
        share_start(2)

    def share_squares():
        EQ[0] = SQ[...]
        EZ[t] = SQ[...]
        share_start(3)

    def share_squares_dp():
        share_wait(3)
        total = added(EZ, 0, 4)
        EQ[1] = total
        EZ[4 + dp] = total
        share_start(4)

    def share_end():
        share_wait(2)
        share_wait(4)
        SQO[...] = added(EZ, 4, ring)

    def chunk(direction, step):
        return lax.rem(at + ring - step, ring) if direction == 0 else lax.rem(at + step, ring)

    def gathered(direction, step):
        return lax.rem(at + 1 + ring - step, ring) if direction == 0 else lax.rem(at + ring - 1 + step, ring)

    def left_of(segment, direction, step):
        columns = pl.ds(pl.multiple_of(chunk(direction, step) * 128, 128), 128)
        return (HID, FI, AI)[segment][:, columns]

    def own_piece(step, part):
        for direction in range(2):
            PSD[lax.rem(step, PARTS), direction, :, part * 128 : (part + 1) * 128] = dot_tn(
                left_of(0, direction, step), CB[part, direction]
            )

    def own_down(step):
        for direction in range(2):
            right = jnp.concatenate([CB[part, direction] for part in range(PARTS)], axis=1)
            PSD[lax.rem(step, PARTS), direction] = dot_tn(left_of(0, direction, step), right)

    def own_partial(segment, step):
        for direction in range(2):
            left = left_of(segment, direction, step)
            if segment == 1:
                PSC[direction] = dot_tn(left, PG[:, direction * 512 : (direction + 1) * 512])
            else:
                number = chunk(direction, step)
                PSC[direction, :, 0:384] = dot_tn(left, QG[:, direction * 384 : (direction + 1) * 384])
                PSC[direction, :, 384:512] = dot_tn(
                    CTX[:, direction * 128 : (direction + 1) * 128], CB[lax.rem(number, PARTS), lax.div(number, PARTS)]
                )

    def parts_of(segment, piece):
        return pl.ds(piece * TOGETHER[segment], TOGETHER[segment])

    def sems_of(segment, direction, piece, step):
        return r_s.at[segment, direction, piece], r_r.at[segment, direction, piece, lax.rem(step, ring)]

    def scatter(segment, direction, piece, step):
        parts = parts_of(segment, piece)
        return remote(
            RSB.at[segment, direction, parts, step], RSB.at[segment, direction, parts, step + 1],
            *sems_of(segment, direction, piece, step), onward[direction],
        )

    def collect(segment, direction, piece, step):
        block = GB.at[segment, direction, parts_of(segment, piece), gathered(direction, step)]
        return remote(
            block, block, *sems_of(segment, direction, piece, ring - 1 + step), onward[direction]
        )

    turns = ring - 1

    def during(condition, work):
        pl.when(condition)(work)

    def pieces(segment, parts=None):
        parts = range(PARTS // TOGETHER[segment]) if parts is None else parts
        return [(piece, direction) for piece in parts for direction in range(2)]

    def members_of(segment, piece):
        return range(piece * TOGETHER[segment], (piece + 1) * TOGETHER[segment])

    def term(segment, direction, part, step):
        columns = slice(part * 128, (part + 1) * 128)
        if segment == 0:
            return PSD[lax.rem(step, PARTS), direction, :, columns]
        return PSC[direction, :, columns]

    def sent(segment, direction, piece):
        scatter(segment, direction, piece, 0).wait_send()

    def ring_open(segment, parts=None):
        for piece, direction in pieces(segment, parts):
            for part in members_of(segment, piece):
                RSB[segment, direction, part, 0] = term(segment, direction, part, 0).astype(BF16)
            scatter(segment, direction, piece, 0).start()

    def ring_scatter(segment, step, parts=None):
        for piece, direction in pieces(segment, parts):
            scatter(segment, direction, piece, step - 1).wait_recv()
            for part in members_of(segment, piece):
                RSB[segment, direction, part, step] = (
                    RSB[segment, direction, part, step].astype(F32) + term(segment, direction, part, step)
                ).astype(BF16)
            sent(segment, direction, piece)
            scatter(segment, direction, piece, step).start()

    def ring_turn(segment, parts=None):
        last = ring - 1
        for piece, direction in pieces(segment, parts):
            scatter(segment, direction, piece, last - 1).wait_recv()
            for part in members_of(segment, piece):
                GB[segment, direction, part, gathered(direction, 0)] = (
                    RSB[segment, direction, part, last].astype(F32) + term(segment, direction, part, last)
                ).astype(BF16)
            sent(segment, direction, piece)
            collect(segment, direction, piece, 0).start()

    def ring_collect(segment, step, parts=None):
        for piece, direction in pieces(segment, parts):
            collect(segment, direction, piece, step - 1).wait_recv()
            sent(segment, direction, piece)
            collect(segment, direction, piece, step).start()

    def ring_close(segment, parts=None):
        for piece, direction in pieces(segment, parts):
            collect(segment, direction, piece, ring - 2).wait_recv()
            sent(segment, direction, piece)

    def down_slot(slot):
        @pl.when(slot <= turns)
        def _():
            own_down(slot)

        for part in range(PARTS):
            event = slot - part
            during(event < PARTS, lambda: own_piece(event, part))
            during(event < turns, lambda: ring_scatter(0, event, (part,)))
            during(event == turns, lambda: ring_turn(0, (part,)))
            during((event > turns) & (event < 2 * turns), lambda: ring_collect(0, event - turns, (part,)))
            during(event == 2 * turns, lambda: ring_close(0, (part,)))

    for copy in local[:3]:
        copy.wait()

    def place_of(step):
        return 2 * lax.rem(x + lax.div(step, 2), 2) + lax.rem(core + lax.rem(step, 2), 2)

    @pl.loop(0, 8)
    def _(step):
        @pl.when(step == 1)
        def _():
            for copy in local[3:]:
                copy.wait()
            for kind in range(PARTS + 1):
                gather(1, kind).start()

        @pl.when(step == 2)
        def _():
            gather(0, 0).wait_recv()

        for half in range(2):

            @pl.when(step == 4 + 2 * half)
            def _():
                gather(0, 1 + half).wait_recv()
                gather(0, 3 + half).start()

            @pl.when(step == 5 + 2 * half)
            def _():
                gather(0, 3 + half).wait_recv()

        late = lax.div(step, 4)
        block = place_of(2 * late + jnp.where(late == 1, lax.rem(step, 2), lax.div(step, 2)))
        forward_block(block, jnp.where(late == 1, lax.div(step - 4, 2), lax.rem(step, 2)))

        @pl.when(step == 5)
        def _():
            cotangent_block(place_of(0))

    gather(1, 0).wait_recv()
    for slot in range(PARTS):
        gather(1, 1 + slot).wait_recv()
        gather(1, 1 + PARTS + slot).start()
        for part in range(slot):
            own_piece(slot - part, part)
            ring_scatter(0, slot - part, (part,))
        gather(1, 1 + PARTS + slot).wait_recv()
        own_piece(0, slot)
        ring_open(0, (slot,))
        if slot == 0:
            cotangent_block(place_of(1))

    cotangent_block(place_of(2))
    down_slot(4)
    cotangent_block(place_of(3))
    own_partial(1, 0)
    ring_open(1)

    def advance(segment, step):
        @pl.when(step <= turns)
        def _():
            own_partial(segment, step)

        during(step < turns, lambda: ring_scatter(segment, step))
        during(step == turns, lambda: ring_turn(segment))
        during(step > turns, lambda: ring_collect(segment, step - turns))

    @pl.loop(0, heads * blocks)
    def _(unit):
        slot = 5 + lax.div(unit, 2)
        during(lax.rem(unit, 2) == 0, lambda: down_slot(slot))
        during(lax.rem(unit, 2) == 1, lambda: advance(1, slot - 4))
        attention_unit(unit)

    @pl.loop(0, blocks)
    def _(block):
        during(block == 0, lambda: down_slot(13))
        during(block == 2, lambda: ring_collect(1, 2))
        assemble(block)

    own_partial(2, 0)
    ring_open(2)
    SV[4:5, :] = jnp.sum(upstream_rows(pl.ds(t * rows, rows)).astype(F32), axis=0, keepdims=True)

    @pl.loop(0, 8)
    def _(half):
        slot = 14 + lax.div(half, 2)
        during(half == 2, lambda: chip_sum(0))
        during(half == 4, lambda: chip_sum(1))
        during(half == 5, share_tensor)
        during(lax.rem(half, 2) == 0, lambda: down_slot(slot))

        @pl.when(lax.rem(half, 2) == 1)
        def _():
            ring_collect(1, slot - 11)
            own_partial(2, slot - 13)
            ring_scatter(2, slot - 13)

        @pl.when(half < 2)
        def _():
            @pl.loop(2 * half, 2 * half + 2)
            def _(number):
                branch_block(number)

        @pl.when((half >= 2) & (half < 4))
        def _():
            @pl.loop(2 * half - 4, 2 * half - 2)
            def _(number):
                back_block(number)

    ring_close(1)

    @pl.loop(5, 2 * turns)
    def _(step):
        advance(2, step)
        during(step == 6, finish_start)
        during((step >= 6) & (step < 10), lambda: finish_part(step - 6))
        during(step == 7, share_rows)
        during(step == 10, share_gather)
        during(step == 9, share_squares)
        during(step == 11, share_squares_dp)

    ring_close(2)
    share_end()

    for which in range(2):
        for kind in range(kinds[which]):
            gather(which, kind).wait_send()
        for slot in range(2):
            to_core(which, slot).wait_send()
        to_x(which).wait_send()
    for stage in range(5):
        for offset in range(1, members[stage]):
            share(stage, offset).wait_send()


def angle_parts(seq_len):
    inverse = 10000.0 ** (-(np.arange(ROT // 2) * 2.0 / ROT))
    per_lane = np.zeros((128,))
    for start in (0, ROT // 2, HD, HD + ROT // 2):
        per_lane[start : start + ROT // 2] = inverse
    coarse = (np.arange(seq_len // 32) * 32.0)[:, None] * per_lane[None, :]
    fine = np.arange(32.0)[:, None] * per_lane[None, :]
    return [f(a).astype(np.float32) for a in (coarse, fine) for f in (np.cos, np.sin)]


def per_device_fused(
    tokens, cotangent, gain_attn, bias_attn, gain_mlp, bias_mlp, qkv_weight, qkv_bias,
    out_weight, out_bias, up_weight, up_bias, down_weight, down_bias,
):
    rows, width = tokens.shape
    ring = lax.axis_size("dp")
    seq = rows * lax.axis_size("tensor")
    heads = out_weight.shape[0] // HD
    hidden_width = up_weight.shape[1]
    qkv_width = qkv_weight.shape[1]
    cos_a, sin_a, cos_b, sin_b = angle_parts(seq)
    vmem = pl.BlockSpec(memory_space=pltpu.VMEM)
    hbm = pl.BlockSpec(memory_space=pl.ANY)
    V = pltpu.VMEM
    D = pltpu.SemaphoreType.DMA
    scratch = [
        V((seq, width), BF16), V((PARTS, 2, seq, 128), BF16), V((seq, width), BF16), V((seq, width), BF16),
        V((seq, hidden_width), BF16), V((seq, hidden_width), F32), V((seq, hidden_width), BF16),
        V((seq, qkv_width), BF16),
        V((heads, seq, HD), BF16), V((heads, seq, HD), BF16), V((heads, seq, HD), BF16),
        V((heads, seq, HD), BF16), V((heads, seq, HD), BF16), V((seq, heads * HD), BF16),
        V((heads, seq, HD), F32), V((heads, HD, seq), F32), V((heads, HD, seq), F32),
        V((seq, 128), F32), V((seq, 128), F32),
        V(qkv_weight.shape, BF16), V(out_weight.shape, BF16), V(up_weight.shape, BF16), V(down_weight.shape, BF16),
        V((3, 2, PARTS, ring, 128, 128), BF16), V((PARTS, 2, 128, 512), F32), V((2, 128, 512), F32),
        V((2, seq, width), BF16), V((2, 2, rows, width), BF16), V((2, rows, width), BF16),
        V((8, width), F32), V((8, width), F32), V((4, 8, width), F32),
        V((ring, 8, 128), F32), V((ring, 8, 128), F32), V((8, 128), F32),
        V((2, 8, 128), F32), V((4 + ring, 8, 128), F32),
        D((6 + 2 * PARTS,)), D((2, 1 + 2 * PARTS)), D((2, 1 + 2 * PARTS)),
        D((3, 2, PARTS)), D((3, 2, PARTS, ring)),
        D((2, 3)), D((2, 3)), D((3 * ring + 3,)), D((3 * ring + 3,)),
    ]
    mixed, input_grad, gradients, sums, squares = pl.pallas_call(
        functools.partial(fused_kernel, ring),
        out_shape=[
            V((rows, width), BF16),
            V((rows, width), F32),
            V((3, 2, PARTS, ring, 128, 128), BF16),
            V((ring, 8, 128), F32),
            V((8, 128), F32),
        ],
        in_specs=[hbm, hbm] + [vmem] * 8 + [hbm] * 4 + [vmem] * 4,
        out_specs=[vmem] * 5,
        scratch_shapes=scratch,
        compiler_params=pltpu.CompilerParams(
            collective_id=0, has_side_effects=True, vmem_limit_bytes=VMEM_LIMIT
        ),
        name="layer",
    )(
        tokens, cotangent,
        *(v.reshape(1, -1) for v in (gain_attn, bias_attn, gain_mlp, bias_mlp, out_bias, down_bias)),
        qkv_bias, up_bias.reshape(1, -1),
        qkv_weight, out_weight, up_weight, down_weight, cos_a, sin_a, cos_b, sin_b,
    )
    elements = rows * width * ring * lax.axis_size("tensor")
    return closing(
        mixed, input_grad, gradients, sums, squares, elements, down_weight, up_weight, qkv_weight, out_weight
    )


def closing_kernel(
    elements,
    mixed, igrad, GB, SUMS, SQUARES,
    mixed_o, igrad_o, ga_o, ba_o, gm_o, bm_o, gq_o, bqkv_o, go_o, bo_o, gu_o, bup_o, gd_o, bd_o, stats_o,
    SD, SU, SQ, SO, sems, msem,
):
    copies = [
        pltpu.make_async_copy(mixed, mixed_o, msem.at[0]),
        pltpu.make_async_copy(igrad, igrad_o, msem.at[1]),
    ]
    for copy in copies:
        copy.start()
    for segment, stage in enumerate((SD, SU, SQ)):
        for number in range(GB.shape[3]):
            there = slice(number * 128, number * 128 + 128)
            for direction in range(2):
                for part in range(PARTS):
                    piece = GB[segment, direction, part, number].astype(F32)
                    if segment == 2 and part == 3:
                        SO[direction * 128 : direction * 128 + 128, there] = piece
                    else:
                        column = direction * (384 if segment == 2 else 512) + part * 128
                        stage[there, column : column + 128] = piece
            rows = pl.ds(number * 128, 128)
            copy = pltpu.make_async_copy(
                stage.at[rows], (gd_o, gu_o, gq_o)[segment].at[rows], sems.at[segment, number]
            )
            copy.start()
            copies.append(copy)
    copies.append(pltpu.make_async_copy(SO, go_o, msem.at[2]))
    copies[-1].start()
    for row, out in ((0, ga_o), (1, ba_o), (2, gm_o), (3, bm_o), (4, bo_o), (4, bd_o), (6, bup_o)):
        for place in range(SUMS.shape[1]):
            out[:, place * 128 : (place + 1) * 128] = SUMS[row, place : place + 1, :]
    for place in range(bqkv_o.shape[0] // 128):
        bqkv_o[place * 128 : (place + 1) * 128] = SUMS[7, place, :]
    stats_o[...] = jnp.sqrt(SQUARES[0, : stats_o.shape[0]] * (1.0 / elements))
    for copy in copies:
        copy.wait()


def closing(mixed, input_grad, gradients, sums, squares, elements, down_weight, up_weight, qkv_weight, out_weight):
    hbm = pl.BlockSpec(memory_space=pl.ANY)
    vmem = pl.BlockSpec(memory_space=pltpu.VMEM)

    def like(array, dtype=F32):
        return jax.ShapeDtypeStruct(array.shape, dtype)

    width = mixed.shape[1]
    row = jax.ShapeDtypeStruct((1, width), F32)
    outs = pl.pallas_call(
        functools.partial(closing_kernel, elements),
        in_specs=[vmem] * 5,
        out_specs=[
            hbm, hbm, vmem, vmem, vmem, vmem, hbm, vmem, hbm, vmem, hbm, vmem, hbm, vmem, vmem,
        ],
        out_shape=[
            like(mixed, BF16), like(input_grad), row, row, row, row,
            like(qkv_weight), jax.ShapeDtypeStruct((qkv_weight.shape[1],), F32), like(out_weight), row,
            like(up_weight), row, like(down_weight), row, jax.ShapeDtypeStruct((3,), F32),
        ],
        scratch_shapes=[
            pltpu.VMEM(down_weight.shape, F32),
            pltpu.VMEM(up_weight.shape, F32),
            pltpu.VMEM(qkv_weight.shape, F32),
            pltpu.VMEM(out_weight.shape, F32),
            pltpu.SemaphoreType.DMA((3, gradients.shape[3])),
            pltpu.SemaphoreType.DMA((3,)),
        ],
        compiler_params=pltpu.CompilerParams(vmem_limit_bytes=24 << 20),
        name="outputs",
    )(mixed, input_grad, gradients, sums, squares)
    return tuple(out.reshape(-1) if out.shape == (1, width) else out for out in outs)


def solution(mesh):
    in_specs = (
        P(("dp", "tensor"), None),
        P(("dp", "tensor"), None),
        P(),
        P(),
        P(),
        P(),
        P(None, "tensor"),
        P("tensor"),
        P("tensor", None),
        P(),
        P(None, "tensor"),
        P("tensor"),
        P("tensor", None),
        P(),
    )
    out_specs = (
        P(("dp", "tensor"), None),
        P(("dp", "tensor"), None),
        P(),
        P(),
        P(),
        P(),
        P(None, "tensor"),
        P("tensor"),
        P("tensor", None),
        P(),
        P(None, "tensor"),
        P("tensor"),
        P("tensor", None),
        P(),
        P(),
    )
    fused = mesh.shape["tensor"] == 4 and mesh.shape["dp"] == 8
    return jax.shard_map(
        per_device_fused if fused else per_device, mesh=mesh, in_specs=in_specs, out_specs=out_specs, check_vma=False
    )
```

```python
import functools
import math

import jax
import jax.numpy as jnp
import numpy as np
from jax import lax
from jax.experimental import pallas as pl
from jax.experimental.pallas import tpu as pltpu
from jax.sharding import PartitionSpec as P

HD = 64
ROT = 16
VMEM_LIMIT = 54 << 20


epsilon = 1e-05


def angle_tables(seq_len):
    positions = jnp.arange(seq_len, dtype=jnp.float32)
    inverse = 10000.0 ** (-(jnp.arange(ROT // 2, dtype=jnp.float32) * 2.0 / ROT))
    angles = positions[:, None] * inverse[None, :]
    cosine = jnp.concatenate([jnp.cos(angles), jnp.cos(angles)], axis=-1)[:, None, :]
    sine_part = jnp.concatenate([jnp.sin(angles), jnp.sin(angles)], axis=-1)[:, None, :]
    return (cosine, sine_part)


def rotate(field_in, cosine, sine_part):
    half_rot = ROT // 2
    first_half = field_in[..., :half_rot]
    second = field_in[..., half_rot:ROT]
    turned = jnp.concatenate([-second, first_half], axis=-1)
    return jnp.concatenate(
        [field_in[..., :ROT] * cosine + turned * sine_part, field_in[..., ROT:]], axis=-1
    )


def unrotate(grad_in, cosine, sine_part):
    half_rot = ROT // 2
    head_part = grad_in[..., :ROT]
    scaled = head_part * sine_part
    turned = jnp.concatenate([scaled[..., half_rot:], -scaled[..., :half_rot]], axis=-1)
    return jnp.concatenate([head_part * cosine + turned, grad_in[..., ROT:]], axis=-1)


def normalize(raw_rows):
    average = jnp.mean(raw_rows, axis=-1, keepdims=True)
    centred = raw_rows - average
    spread = jnp.mean(centred * centred, axis=-1, keepdims=True)
    inverse_root = lax.rsqrt(spread + epsilon)
    return (centred * inverse_root, inverse_root)


def against(left, right):
    return lax.dot_general(
        left, right, (((1,), (1,)), ((), ())), preferred_element_type=jnp.float32
    )


def per_device(
    tokens,
    cotangent,
    gain_attn,
    bias_attn,
    gain_mlp,
    bias_mlp,
    qkv_weight,
    qkv_bias,
    out_weight,
    out_bias,
    up_weight,
    up_bias,
    down_weight,
    down_bias,
):
    own_rows = tokens.shape[0]
    model_width = tokens.shape[1]
    heads_here = out_weight.shape[0] // HD
    score_scale = HD ** (-0.5)
    whole_rows = lax.all_gather(tokens, "tensor", axis=0, tiled=True)
    seq_len = whole_rows.shape[0]
    normed, _ = normalize(whole_rows.astype(jnp.float32))
    attention_input = (normed * gain_attn + bias_attn).astype(jnp.bfloat16)
    feed_input = (normed * gain_mlp + bias_mlp).astype(jnp.bfloat16)
    projected = jnp.dot(attention_input, qkv_weight, preferred_element_type=jnp.float32) + qkv_bias
    projected = projected.reshape(seq_len, heads_here, 3, HD)
    cosine, sine_part = angle_tables(seq_len)
    queries = rotate(projected[:, :, 0], cosine, sine_part).astype(jnp.bfloat16)
    keys_all = rotate(projected[:, :, 1], cosine, sine_part).astype(jnp.bfloat16)
    values_all = projected[:, :, 2].astype(jnp.bfloat16)
    preact = jnp.dot(feed_input, up_weight, preferred_element_type=jnp.float32) + up_bias
    hidden = jax.nn.gelu(preact, approximate=False).astype(jnp.bfloat16)
    block_rows = min(512, seq_len)
    block_total = seq_len // block_rows
    key_positions = jnp.arange(seq_len, dtype=jnp.int32)

    def causal_mask(offset):
        return key_positions[None, :] <= (offset + jnp.arange(block_rows, dtype=jnp.int32))[:, None]

    def forward_block(number):
        offset = number * block_rows
        query_rows = lax.dynamic_slice_in_dim(queries, offset, block_rows, 0)
        scores = (
            jnp.einsum("qhd,khd->hqk", query_rows, keys_all, preferred_element_type=jnp.float32)
            * score_scale
        )
        scores = jnp.where(causal_mask(offset)[None], scores, -1e30)
        highest = jnp.max(scores, axis=-1, keepdims=True)
        weights = jnp.exp(scores - highest)
        totals = jnp.sum(weights, axis=-1, keepdims=True)
        soft_rows = (weights / totals).astype(jnp.bfloat16)
        context_rows = jnp.einsum(
            "hqk,khd->qhd", soft_rows, values_all, preferred_element_type=jnp.float32
        ).astype(jnp.bfloat16)
        log_totals = (highest + jnp.log(totals))[:, :, 0].T
        return (context_rows, log_totals)

    context_blocks, log_blocks = lax.map(forward_block, jnp.arange(block_total, dtype=jnp.int32))
    context = context_blocks.reshape(seq_len, heads_here * HD)
    log_sums = log_blocks.reshape(seq_len, heads_here)
    context_rows = context
    branch = lax.psum_scatter(
        jnp.dot(context_rows, out_weight, preferred_element_type=jnp.float32)
        + jnp.dot(hidden, down_weight, preferred_element_type=jnp.float32),
        "tensor",
        scatter_dimension=0,
        tiled=True,
    )
    branch = branch + out_bias + down_bias
    residual_out = tokens.astype(jnp.float32) + branch
    mixed_out = residual_out.astype(jnp.bfloat16)
    forward_squares = jnp.stack([jnp.sum(residual_out * residual_out), jnp.sum(branch * branch)])
    forward_totals = lax.psum(forward_squares, ("dp", "tensor"))
    upstream = lax.all_gather(cotangent, "tensor", axis=0, tiled=True)
    out_weight_grad = jnp.einsum("sa,sd->ad", context, upstream, preferred_element_type=jnp.float32)
    down_weight_grad = jnp.einsum("sf,sd->fd", hidden, upstream, preferred_element_type=jnp.float32)
    context_grad = against(upstream, out_weight).astype(jnp.bfloat16)
    hidden_grad = against(upstream, down_weight)
    normal_cdf = 0.5 * (1.0 + lax.erf(preact * 0.5**0.5))
    density = jnp.exp(-0.5 * preact * preact) * (1.0 / math.sqrt(2.0 * math.pi))
    preact_grad = (hidden_grad * (normal_cdf + preact * density)).astype(jnp.bfloat16)
    context_grad3 = context_grad.reshape(seq_len, heads_here, HD)

    def backward_block(carried, number):
        key_grad, value_grad = carried
        offset = number * block_rows
        query_rows = lax.dynamic_slice_in_dim(queries, offset, block_rows, 0)
        grad_rows = lax.dynamic_slice_in_dim(context_grad3, offset, block_rows, 0)
        log_rows = lax.dynamic_slice_in_dim(log_sums, offset, block_rows, 0).T
        scores = (
            jnp.einsum("qhd,khd->hqk", query_rows, keys_all, preferred_element_type=jnp.float32)
            * score_scale
        )
        soft_full = jnp.exp(
            jnp.where(causal_mask(offset)[None], scores - log_rows[:, :, None], -1e30)
        )
        prob_grad = jnp.einsum(
            "qhd,khd->hqk", grad_rows, values_all, preferred_element_type=jnp.float32
        )
        deltas = jnp.sum(soft_full * prob_grad, axis=-1, keepdims=True)
        score_grad = (soft_full * (prob_grad - deltas)).astype(jnp.bfloat16)
        query_grad = (
            jnp.einsum("hqk,khd->qhd", score_grad, keys_all, preferred_element_type=jnp.float32)
            * score_scale
        )
        key_grad = (
            key_grad
            + jnp.einsum("hqk,qhd->khd", score_grad, query_rows, preferred_element_type=jnp.float32)
            * score_scale
        )
        value_grad = value_grad + jnp.einsum(
            "hqk,qhd->khd",
            soft_full.astype(jnp.bfloat16),
            grad_rows,
            preferred_element_type=jnp.float32,
        )
        return ((key_grad, value_grad), query_grad)

    empty = jnp.zeros((seq_len, heads_here, HD), jnp.float32)
    (key_grad, value_grad), query_blocks = lax.scan(
        backward_block, (empty, empty), jnp.arange(block_total, dtype=jnp.int32)
    )
    query_grad = unrotate(query_blocks.reshape(seq_len, heads_here, HD), cosine, sine_part)
    key_grad = unrotate(key_grad, cosine, sine_part)
    qkv_grad = (
        jnp.stack([query_grad, key_grad, value_grad], axis=2)
        .reshape(seq_len, 3 * heads_here * HD)
        .astype(jnp.bfloat16)
    )
    qkv_weight_grad = jnp.einsum(
        "sd,sc->dc", attention_input, qkv_grad, preferred_element_type=jnp.float32
    )
    qkv_bias_grad = jnp.sum(qkv_grad, axis=0, dtype=jnp.float32)
    up_weight_grad = jnp.einsum(
        "sd,sf->df", feed_input, preact_grad, preferred_element_type=jnp.float32
    )
    up_bias_grad = jnp.sum(preact_grad, axis=0, dtype=jnp.float32)
    own_normed, own_scale = normalize(tokens.astype(jnp.float32))
    attention_back = against(qkv_grad, qkv_weight)
    feed_back = against(preact_grad, up_weight)
    gain_terms = jnp.stack(
        [
            jnp.sum(normed * attention_back, axis=0),
            jnp.sum(attention_back, axis=0),
            jnp.sum(normed * feed_back, axis=0),
            jnp.sum(feed_back, axis=0),
        ]
    )
    normed_grad = lax.psum_scatter(
        (attention_back * gain_attn + feed_back * gain_mlp).astype(jnp.bfloat16),
        "tensor",
        scatter_dimension=0,
        tiled=True,
    ).astype(jnp.float32)
    centred_term = (
        normed_grad
        - jnp.mean(normed_grad, axis=-1, keepdims=True)
        - own_normed * jnp.mean(normed_grad * own_normed, axis=-1, keepdims=True)
    )
    input_grad = own_scale * centred_term + cotangent.astype(jnp.float32)
    (
        qkv_weight_grad,
        qkv_bias_grad,
        out_weight_grad,
        up_weight_grad,
        up_bias_grad,
        down_weight_grad,
    ) = lax.psum(
        (
            qkv_weight_grad,
            qkv_bias_grad,
            out_weight_grad,
            up_weight_grad,
            up_bias_grad,
            down_weight_grad,
        ),
        "dp",
    )
    bias_rows = jnp.sum(cotangent, axis=0, dtype=jnp.float32)
    grad_square = jnp.sum(input_grad * input_grad)
    gain_totals, bias_totals, grad_total = lax.psum(
        (gain_terms, bias_rows, grad_square), ("dp", "tensor")
    )
    square_totals = jnp.concatenate([forward_totals, grad_total[None]])
    elements = own_rows * model_width * lax.axis_size("dp") * lax.axis_size("tensor")
    statistics = jnp.sqrt(square_totals / elements)
    return (
        mixed_out,
        input_grad,
        gain_totals[0],
        gain_totals[1],
        gain_totals[2],
        gain_totals[3],
        qkv_weight_grad,
        qkv_bias_grad,
        out_weight_grad,
        bias_totals,
        up_weight_grad,
        up_bias_grad,
        down_weight_grad,
        bias_totals,
        statistics,
    )


F32 = jnp.float32
BF16 = jnp.bfloat16
MESH = pl.DeviceIdType.MESH
TILE = 256
PARTS = 4
TOGETHER = (1, 4, 1)
SPLIT = (1, 1, 1)


def ring_pieces(segments):
    return sum(2 * (PARTS // TOGETHER[number] * SPLIT[number]) for number in range(segments))


def dot_nn(left, right):
    return jnp.dot(left, right, preferred_element_type=F32)


def dot_nt(left, right):
    return lax.dot_general(left, right, (((1,), (1,)), ((), ())), preferred_element_type=F32)


def dot_tn(left, right):
    return lax.dot_general(left, right, (((0,), (0,)), ((), ())), preferred_element_type=F32)


def fused_kernel(
    ring,
    tok, cot, ga, ba, gm, bm, bo, bd, bqkv, bup, wqkv_h, wout_h, wup_h, wdn_h, cos_a, sin_a, cos_b, sin_b,
    mixed, igrad, GB, SUMS, SQO,
    T, CB, AI, FI, HID, GP, PG, QG, QH, KH, VH, CGH, CTXH, CTX, DQ, DKT, DVT, COS, SIN,
    WQKV, WOUT, WUP, WDN, RSB, PSD, PSC, PART, RA, RB, SV, ES, EX, EROWS, EY, SQ, EQ, EZ,
    lsem, g_s, g_r, r_s, r_r, b_s, b_r, e_s, e_r,
):
    rows = tok.shape[0]
    width = tok.shape[1]
    seq = T.shape[0]
    heads = QH.shape[0]
    hidden_width = WUP.shape[1]
    half_rows = rows // 2
    blocks = seq // TILE
    scale = HD ** (-0.5)
    dp = lax.axis_index("dp")
    t = lax.axis_index("tensor")
    core = lax.rem(t, 2)
    x = lax.div(t, 2)
    depth = ring // 2
    y = lax.rem(dp, 2)
    z = lax.div(dp, 2)
    at = z + y * (2 * depth - 1 - 2 * z)

    def ring_device(place):
        ny = lax.div(place, depth)
        return (2 * (place + ny * (2 * depth - 1 - 2 * place)) + ny, t)

    following = ring_device(lax.rem(at + 1, ring))
    previous = ring_device(lax.rem(at + ring - 1, ring))
    onward = (following, previous)
    core_mate = (dp, t + 1 - 2 * core)
    x_block = 2 * (1 - x) + core
    x_mate = (dp, x_block)

    def remote(src, dst, send, recv, device):
        return pltpu.make_async_remote_copy(
            src_ref=src, dst_ref=dst, send_sem=send, recv_sem=recv, device_id=device, device_id_type=MESH
        )

    def gather(which, kind):
        sems = (g_s.at[5 * which + kind], g_r.at[5 * which + kind])
        own = pl.ds(t * rows, rows)
        there = pl.ds(x_block * rows, rows)
        if which == 1:
            if kind == 0:
                return remote(CB.at[:, :, own], CB.at[:, :, own], *sems, core_mate)
            if kind <= PARTS:
                return remote(CB.at[kind - 1, :, own], CB.at[kind - 1, :, own], *sems, x_mate)
            piece = CB.at[kind - 1 - PARTS, :, there]
            return remote(piece, piece, *sems, core_mate)
        if kind == 0:
            return remote(tok, T.at[own], *sems, core_mate)
        if kind <= 2:
            off = (kind - 1) * half_rows
            return remote(tok.at[pl.ds(off, half_rows)], T.at[pl.ds(t * rows + off, half_rows)], *sems, x_mate)
        part = T.at[pl.ds(x_block * rows + (kind - 3) * half_rows, half_rows)]
        return remote(part, part, *sems, core_mate)

    kinds = (5, 1 + 2 * PARTS)

    def upstream_rows(here):
        return jnp.concatenate([CB[part, direction, here, :] for direction in range(2) for part in range(PARTS)], axis=1)

    local = [
        pltpu.make_async_copy(tok, T.at[pl.ds(t * rows, rows)], lsem.at[0]),
        pltpu.make_async_copy(wqkv_h, WQKV, lsem.at[2]),
        pltpu.make_async_copy(wup_h, WUP, lsem.at[3]),
        *(
            pltpu.make_async_copy(
                cot.at[:, pl.ds(direction * 512 + part * 128, 128)],
                CB.at[part, direction, pl.ds(t * rows, rows)],
                lsem.at[6 + 2 * part + direction],
            )
            for part in range(PARTS)
            for direction in range(2)
        ),
        pltpu.make_async_copy(wdn_h, WDN, lsem.at[4]),
        pltpu.make_async_copy(wout_h, WOUT, lsem.at[5]),
    ]
    for copy in local:
        copy.start()
    barrier = pltpu.get_barrier_semaphore()
    for mate in (core_mate, x_mate, following, previous):
        pl.semaphore_signal(barrier, inc=1, device_id=mate, device_id_type=MESH)
    pl.semaphore_wait(barrier, 4)
    gather(0, 1).start()
    gather(0, 2).start()
    gather(0, 0).start()

    @pl.loop(0, seq // 32)
    def _(a):
        ca, sa = cos_a[pl.ds(a, 1), :], sin_a[pl.ds(a, 1), :]
        cb, sb = cos_b[...], sin_b[...]
        COS[pl.ds(a * 32, 32), :] = ca * cb - sa * sb
        SIN[pl.ds(a * 32, 32), :] = sa * cb + ca * sb

    SV[...] = jnp.zeros_like(SV)
    SQ[...] = jnp.zeros_like(SQ)

    @pl.loop(0, heads)
    def _(h):
        DKT[h] = jnp.zeros(DKT.shape[1:], F32)
        DVT[h] = jnp.zeros(DVT.shape[1:], F32)


    def tables(base, group, count):
        lane = lax.broadcasted_iota(jnp.int32, (count, 128), 1)
        low_lane = jnp.where(lane >= 64, lane - 64, lane)
        cosine, sine = COS[pl.ds(base, count), :], SIN[pl.ds(base, count), :]
        if group == 1:
            cosine = jnp.where(lane >= 64, cosine, 1.0)
            sine = jnp.where(lane >= 64, sine, 0.0)
        if group == 2:
            cosine = jnp.where(lane < 64, cosine, 1.0)
            sine = jnp.where(lane < 64, sine, 0.0)
        upper = jnp.where(low_lane >= ROT // 2, sine, 0.0)
        return cosine, upper, sine - upper

    def norm_rows(base, count):
        raw = T[pl.ds(base, count), :].astype(F32)
        centred = raw - jnp.mean(raw, axis=1, keepdims=True)
        inverse_root = lax.rsqrt(jnp.mean(centred * centred, axis=1, keepdims=True) + epsilon)
        return centred * inverse_root, inverse_root

    def forward_block(block, half):
        base = pl.multiple_of(block * rows + half * half_rows, half_rows)

        @pl.loop(0, half_rows // 64)
        def _(part):
            off = pl.multiple_of(base + part * 64, 64)
            normed, _ = norm_rows(off, 64)
            AI[pl.ds(off, 64), :] = (normed * ga[...] + ba[...]).astype(BF16)
            FI[pl.ds(off, 64), :] = (normed * gm[...] + bm[...]).astype(BF16)

        for group in range(3 * heads // 2):
            if group % 2 == 0:
                columns = slice(group * 128, group * 128 + 256)
                pair = dot_nn(AI[pl.ds(base, half_rows), :], WQKV[:, columns]) + bqkv[columns].reshape(1, 256)
            value = pair[:, (group % 2) * 128 : (group % 2) * 128 + 128]
            cosine, upper, lower = tables(base, group % 3, half_rows)
            turned = (
                value * cosine
                - lower * pltpu.roll(value, 128 - ROT // 2, 1)
                + upper * pltpu.roll(value, ROT // 2, 1)
            ).astype(BF16)
            first = 2 * (group // 3)
            left, left_head = ((QH, first), (VH, first), (KH, first + 1))[group % 3]
            right, right_head = ((KH, first), (QH, first + 1), (VH, first + 1))[group % 3]
            left[left_head, pl.ds(base, half_rows), :] = turned[:, :HD]
            right[right_head, pl.ds(base, half_rows), :] = turned[:, HD:]

        for part in range(hidden_width // TILE):
            columns = slice(part * TILE, (part + 1) * TILE)
            preact = dot_nn(FI[pl.ds(base, half_rows), :], WUP[:, columns]) + bup[:, columns]
            cdf = 0.5 * (1.0 + lax.erf(preact * 0.5**0.5))
            density = jnp.exp(-0.5 * preact * preact) * (1.0 / math.sqrt(2.0 * math.pi))
            HID[pl.ds(base, half_rows), columns] = (preact * cdf).astype(BF16)
            GP[pl.ds(base, half_rows), columns] = cdf + preact * density

    def cotangent_block(block):
        base = pl.multiple_of(block * rows, rows)
        upstream = upstream_rows(pl.ds(base, rows))
        grad = dot_nt(upstream, WOUT[...]).astype(BF16)
        for h in range(heads):
            CGH[h, pl.ds(base, rows), :] = grad[:, h * HD : (h + 1) * HD]

        for part in range(hidden_width // TILE):
            columns = slice(part * TILE, (part + 1) * TILE)
            back = dot_nt(upstream, WDN[columns, :])
            rounded = (back * GP[pl.ds(base, rows), columns]).astype(BF16)
            PG[pl.ds(base, rows), columns] = rounded
            SV[6:7, columns] += jnp.sum(rounded.astype(F32), axis=0, keepdims=True)

    def attention_rows(h, own):
        here = slice(own * TILE, (own + 1) * TILE)
        before = own * TILE
        reach = before + TILE
        query = QH[h, here, :]
        grad = CGH[h, here, :]
        keys = KH[h, :reach, :]
        values = VH[h, :reach, :]
        scores = dot_nt(query, keys) * scale
        row_at = lax.broadcasted_iota(jnp.int32, (TILE, TILE), 0)
        column_at = lax.broadcasted_iota(jnp.int32, (TILE, TILE), 1)
        corner = jnp.where(column_at <= row_at, scores[:, before:], -1e30)
        scores = jnp.concatenate([scores[:, :before], corner], axis=1) if own else corner
        weights = jnp.exp(scores - jnp.max(scores, axis=1, keepdims=True))
        probs = weights * (1.0 / jnp.sum(weights, axis=1, keepdims=True))
        soft = probs.astype(BF16)
        CTXH[h, here, :] = dot_nn(soft, values).astype(BF16)
        prob_grad = dot_nt(grad, values)
        delta = jnp.sum(probs * prob_grad, axis=1, keepdims=True)
        score_grad = (probs * (prob_grad - delta)).astype(BF16)
        DQ[h, here, :] = scale * dot_nn(score_grad, keys)
        DKT[h, :, :reach] += dot_nn(query.astype(F32).T.astype(BF16), score_grad)
        DVT[h, :, :reach] += dot_nn(grad.astype(F32).T.astype(BF16), soft)

    def attention_unit(unit):
        h = lax.div(unit, blocks)
        for number, own in enumerate(sorted(range(blocks), key=lambda own: min(own, blocks - 1 - own))):
            pl.when(lax.rem(unit, blocks) == number)(functools.partial(attention_rows, h, own))

    def assemble(block):
        base = pl.multiple_of(block * TILE, TILE)
        here = pl.ds(base, TILE)
        for pair in range(heads // 2):
            one, two = 2 * pair, 2 * pair + 1
            CTX[here, pair * 128 : (pair + 1) * 128] = jnp.concatenate(
                [CTXH[one, here, :], CTXH[two, here, :]], axis=1
            )
            parts = [
                (DQ[one, here, :], scale * DKT[one, :, here].T),
                (DVT[one, :, here].T, DQ[two, here, :]),
                (scale * DKT[two, :, here].T, DVT[two, :, here].T),
            ]
            for group, (left, right) in enumerate(parts):
                grad = jnp.concatenate([left, right], axis=1)
                cosine, upper, lower = tables(base, group, TILE)
                turned = (
                    grad * cosine
                    + pltpu.roll(grad * upper, 128 - ROT // 2, 1)
                    - pltpu.roll(grad * lower, ROT // 2, 1)
                ).astype(BF16)
                columns = slice((3 * pair + group) * 128, (3 * pair + group + 1) * 128)
                QG[here, columns] = turned
                SV[7:8, columns] += jnp.sum(turned.astype(F32), axis=0, keepdims=True)

    def order(step):
        flip_core = 1 - lax.div(step, 2)
        flip_x = 1 - lax.rem(step, 2)
        return 2 * lax.rem(x + flip_x, 2) + lax.rem(core + flip_core, 2)

    def to_core(which, slot):
        block = (2 * x + 1 - core) if slot == 0 else (2 * (1 - x) + 1 - core)
        return remote(
            PART.at[which, pl.ds(block * rows, rows)], RA.at[which, slot],
            b_s.at[which, slot], b_r.at[which, slot], core_mate,
        )

    def to_x(which):
        return remote(
            PART.at[which, pl.ds(x_block * rows, rows)], RB.at[which],
            b_s.at[which, 2], b_r.at[which, 2], x_mate,
        )

    def send_after(which, step):
        @pl.when(step == 0)
        def _():
            to_core(which, 1).start()

        @pl.when(step == 1)
        def _():
            to_core(which, 0).start()

    def branch_block(step):
        base = pl.multiple_of(order(step) * rows, rows)
        here = pl.ds(base, rows)

        for part in range(width // TILE):
            columns = slice(part * TILE, (part + 1) * TILE)
            PART[0, here, columns] = (
                dot_nn(CTX[here, :], WOUT[:, columns]) + dot_nn(HID[here, :], WDN[:, columns])
            ).astype(BF16)

        send_after(0, step)

    def back_block(step):
        base = pl.multiple_of(order(step) * rows, rows)
        here = pl.ds(base, rows)
        raw = T[here, :].astype(F32)
        average = jnp.mean(raw, axis=1, keepdims=True)
        spread = jnp.mean((raw - average) * (raw - average), axis=1, keepdims=True)
        inverse_root = lax.rsqrt(spread + epsilon)

        for part in range(width // TILE):
            columns = slice(part * TILE, (part + 1) * TILE)
            normed = (T[here, columns].astype(F32) - average) * inverse_root
            attention_back = dot_nt(QG[here, :], WQKV[columns, :])
            feed_back = dot_nt(PG[here, :], WUP[columns, :])
            SV[0:1, columns] += jnp.sum(normed * attention_back, axis=0, keepdims=True)
            SV[1:2, columns] += jnp.sum(attention_back, axis=0, keepdims=True)
            SV[2:3, columns] += jnp.sum(normed * feed_back, axis=0, keepdims=True)
            SV[3:4, columns] += jnp.sum(feed_back, axis=0, keepdims=True)
            PART[1, here, columns] = (attention_back * ga[:, columns] + feed_back * gm[:, columns]).astype(BF16)

        send_after(1, step)

    def chip_sum(which):
        to_core(which, 1).wait_recv()
        there = pl.ds(pl.multiple_of(x_block * rows, rows), rows)
        PART[which, there, :] = (PART[which, there, :].astype(F32) + RA[which, 1].astype(F32)).astype(BF16)
        to_x(which).start()

    def finish_start():
        for which in range(2):
            to_core(which, 0).wait_recv()
            to_x(which).wait_recv()
    def total(which, off):
        return (
            PART[which, pl.ds(pl.multiple_of(t * rows + off, 32), 32), :].astype(F32)
            + RA[which, 0, pl.ds(off, 32), :].astype(F32)
            + RB[which, pl.ds(off, 32), :].astype(F32)
        )

    def square(value):
        return jnp.sum(jnp.sum(value * value, axis=1, keepdims=True), axis=0, keepdims=True)

    def finish_part(number):
        off = pl.multiple_of(number * 32, 32)
        here = pl.ds(pl.multiple_of(t * rows + off, 32), 32)
        branch = total(0, off) + bo[...] + bd[...]
        residual = T[here, :].astype(F32) + branch
        mixed[pl.ds(off, 32), :] = residual.astype(BF16)
        normed, inverse_root = norm_rows(t * rows + off, 32)
        grad = total(1, off)
        grad = inverse_root * (
            grad
            - jnp.mean(grad, axis=1, keepdims=True)
            - normed * jnp.mean(grad * normed, axis=1, keepdims=True)
        ) + upstream_rows(here).astype(F32)
        igrad[pl.ds(off, 32), :] = grad
        spot = lax.broadcasted_iota(jnp.int32, SQ.shape, 1)
        for place, value in enumerate((residual, branch, grad)):
            SQ[...] += jnp.where(spot == place, square(value), 0.0)

    members = (4, ring, ring, 4, ring)

    def share(stage, offset):
        over_tensor = stage in (0, 3)
        mate = (dp, lax.rem(t + offset, 4)) if over_tensor else (lax.rem(dp + offset, ring), t)
        src, dst = (
            lambda: (ES, EX.at[t]),
            lambda: (EROWS.at[lax.rem(dp + offset, ring)], EY.at[dp]),
            lambda: (SUMS.at[dp], SUMS.at[dp]),
            lambda: (EQ.at[0], EZ.at[t]),
            lambda: (EQ.at[1], EZ.at[4 + dp]),
        )[stage]()
        return remote(src, dst, e_s.at[stage], e_r.at[stage], mate)

    def share_start(stage):
        for offset in range(1, members[stage]):
            share(stage, offset).start()

    def share_all(stage):
        ref, first = ((EX, 0), (EY, 0), (SUMS, 0), (EZ, 0), (EZ, 4))[stage]
        whole = ref.at[pl.ds(first, members[stage] - 1)]
        return remote(whole, whole, e_s.at[stage], e_r.at[stage], core_mate)

    def share_wait(stage):
        share_all(stage).wait_recv()

    def added(ref, first, count):
        total = ref[first]
        for number in range(1, count):
            total = total + ref[first + number]
        return total

    def share_tensor():
        ES[...] = SV[...]
        EX[t] = SV[...]
        share_start(0)

    def share_rows():
        share_wait(0)
        row = lax.broadcasted_iota(jnp.int32, SV.shape, 0)
        total = jnp.where(row < 5, added(EX, 0, 4), SV[...])
        for place in range(ring):
            EROWS[:, place, :] = total[:, place * 128 : (place + 1) * 128]
        EY[dp] = EROWS[dp]
        share_start(1)

    def share_gather():
        share_wait(1)
        SUMS[dp] = added(EY, 0, ring)
        share_start(2)

    def share_squares():
        EQ[0] = SQ[...]
        EZ[t] = SQ[...]
        share_start(3)

    def share_squares_dp():
        share_wait(3)
        total = added(EZ, 0, 4)
        EQ[1] = total
        EZ[4 + dp] = total
        share_start(4)

    def share_end():
        share_wait(2)
        share_wait(4)
        SQO[...] = added(EZ, 4, ring)

    def chunk(direction, step):
        return lax.rem(at + ring - step, ring) if direction == 0 else lax.rem(at + step, ring)

    def gathered(direction, step):
        return lax.rem(at + 1 + ring - step, ring) if direction == 0 else lax.rem(at + ring - 1 + step, ring)

    def left_of(segment, direction, step):
        columns = pl.ds(pl.multiple_of(chunk(direction, step) * 128, 128), 128)
        return (HID, FI, AI)[segment][:, columns]

    def own_piece(step, part):
        for direction in range(2):
            PSD[lax.rem(step, PARTS), direction, :, part * 128 : (part + 1) * 128] = dot_tn(
                left_of(0, direction, step), CB[part, direction]
            )

    def own_down(step):
        for direction in range(2):
            right = jnp.concatenate([CB[part, direction] for part in range(PARTS)], axis=1)
            PSD[lax.rem(step, PARTS), direction] = dot_tn(left_of(0, direction, step), right)

    def own_partial(segment, step):
        for direction in range(2):
            left = left_of(segment, direction, step)
            if segment == 1:
                PSC[direction] = dot_tn(left, PG[:, direction * 512 : (direction + 1) * 512])
            else:
                number = chunk(direction, step)
                PSC[direction, :, 0:384] = dot_tn(left, QG[:, direction * 384 : (direction + 1) * 384])
                PSC[direction, :, 384:512] = dot_tn(
                    CTX[:, direction * 128 : (direction + 1) * 128], CB[lax.rem(number, PARTS), lax.div(number, PARTS)]
                )

    def parts_of(segment, piece):
        return pl.ds(piece // SPLIT[segment] * TOGETHER[segment], TOGETHER[segment])

    def rows_of(segment, piece):
        count = 128 // SPLIT[segment]
        return slice(piece % SPLIT[segment] * count, (piece % SPLIT[segment] + 1) * count)

    def sems_of(segment, direction, piece, step):
        number = ring_pieces(segment) + direction * (PARTS // TOGETHER[segment] * SPLIT[segment]) + piece
        return r_s.at[number], r_r.at[number * ring + lax.rem(step, ring)]

    def scatter(segment, direction, piece, step):
        parts, here = parts_of(segment, piece), rows_of(segment, piece)
        return remote(
            RSB.at[segment, direction, parts, step, here], RSB.at[segment, direction, parts, step + 1, here],
            *sems_of(segment, direction, piece, step), onward[direction],
        )

    def collect(segment, direction, piece, step):
        block = GB.at[segment, direction, parts_of(segment, piece), gathered(direction, step), rows_of(segment, piece)]
        return remote(
            block, block, *sems_of(segment, direction, piece, ring - 1 + step), onward[direction]
        )

    turns = ring - 1

    def during(condition, work):
        pl.when(condition)(work)

    def pieces(segment, parts=None):
        parts = range(PARTS // TOGETHER[segment] * SPLIT[segment]) if parts is None else parts
        return [(piece, direction) for piece in parts for direction in range(2)]

    def members_of(segment, piece):
        first = piece // SPLIT[segment] * TOGETHER[segment]
        return range(first, first + TOGETHER[segment])

    def term(segment, direction, part, step, here):
        columns = slice(part * 128, (part + 1) * 128)
        if segment == 0:
            return PSD[lax.rem(step, PARTS), direction, here, columns]
        return PSC[direction, here, columns]

    def sent(segment, direction, piece):
        scatter(segment, direction, piece, 0).wait_send()

    def ring_open(segment, parts=None):
        for piece, direction in pieces(segment, parts):
            here = rows_of(segment, piece)
            for part in members_of(segment, piece):
                RSB[segment, direction, part, 0, here] = term(segment, direction, part, 0, here).astype(BF16)
            scatter(segment, direction, piece, 0).start()

    def ring_scatter(segment, step, parts=None):
        for piece, direction in pieces(segment, parts):
            here = rows_of(segment, piece)
            scatter(segment, direction, piece, step - 1).wait_recv()
            for part in members_of(segment, piece):
                RSB[segment, direction, part, step, here] = (
                    RSB[segment, direction, part, step, here].astype(F32) + term(segment, direction, part, step, here)
                ).astype(BF16)
            sent(segment, direction, piece)
            scatter(segment, direction, piece, step).start()

    def ring_turn(segment, parts=None):
        last = ring - 1
        for piece, direction in pieces(segment, parts):
            here = rows_of(segment, piece)
            scatter(segment, direction, piece, last - 1).wait_recv()
            for part in members_of(segment, piece):
                GB[segment, direction, part, gathered(direction, 0), here] = (
                    RSB[segment, direction, part, last, here].astype(F32) + term(segment, direction, part, last, here)
                ).astype(BF16)
            sent(segment, direction, piece)
            collect(segment, direction, piece, 0).start()

    def ring_collect(segment, step, parts=None):
        for piece, direction in pieces(segment, parts):
            collect(segment, direction, piece, step - 1).wait_recv()
            sent(segment, direction, piece)
            collect(segment, direction, piece, step).start()

    def ring_close(segment, parts=None):
        for piece, direction in pieces(segment, parts):
            collect(segment, direction, piece, ring - 2).wait_recv()
            sent(segment, direction, piece)

    def down_terms(slot):
        during((slot >= PARTS) & (slot <= turns), lambda: own_down(slot))
        for part in range(PARTS):
            event = slot - part
            during((event > 0) & (event < PARTS), lambda: own_piece(event, part))

    def down_slot(slot):
        for part in range(PARTS):
            event = slot - part
            during(event < turns, lambda: ring_scatter(0, event, (part,)))
            during(event == turns, lambda: ring_turn(0, (part,)))
            during((event > turns) & (event < 2 * turns), lambda: ring_collect(0, event - turns, (part,)))
            during(event == 2 * turns, lambda: ring_close(0, (part,)))
        down_terms(slot + 1)

    for copy in local[:3]:
        copy.wait()

    def place_of(step):
        return 2 * lax.rem(x + lax.div(step, 2), 2) + lax.rem(core + lax.rem(step, 2), 2)

    @pl.loop(0, 8)
    def _(step):
        @pl.when(step == 1)
        def _():
            for copy in local[3:]:
                copy.wait()
            for kind in range(PARTS + 1):
                gather(1, kind).start()

        @pl.when(step == 2)
        def _():
            gather(0, 0).wait_recv()

        for half in range(2):

            @pl.when(step == 4 + 2 * half)
            def _():
                gather(0, 1 + half).wait_recv()
                gather(0, 3 + half).start()

            @pl.when(step == 5 + 2 * half)
            def _():
                gather(0, 3 + half).wait_recv()

        late = lax.div(step, 4)
        block = place_of(2 * late + jnp.where(late == 1, lax.rem(step, 2), lax.div(step, 2)))
        forward_block(block, jnp.where(late == 1, lax.div(step - 4, 2), lax.rem(step, 2)))

        @pl.when(step == 5)
        def _():
            cotangent_block(place_of(0))

    gather(1, 0).wait_recv()
    for slot in range(PARTS):
        gather(1, 1 + slot).wait_recv()
        gather(1, 1 + PARTS + slot).start()
        for part in range(slot):
            ring_scatter(0, slot - part, (part,))
        gather(1, 1 + PARTS + slot).wait_recv()
        own_piece(0, slot)
        ring_open(0, (slot,))
        if slot == PARTS - 1:
            down_terms(PARTS)
        else:
            for part in range(slot + 1):
                own_piece(slot + 1 - part, part)
        if slot == 0:
            cotangent_block(place_of(1))

    cotangent_block(place_of(2))
    down_slot(4)
    cotangent_block(place_of(3))
    own_partial(1, 0)
    ring_open(1)

    def advance(segment, step):
        @pl.when(step <= turns)
        def _():
            own_partial(segment, step)

        during(step < turns, lambda: ring_scatter(segment, step))
        during(step == turns, lambda: ring_turn(segment))
        during(step > turns, lambda: ring_collect(segment, step - turns))

    units = heads * blocks

    @pl.loop(0, 12)
    def _(half):
        slot = 5 + lax.div(half, 2)
        during(lax.rem(half, 2) == 0, lambda: down_slot(slot))
        during(lax.rem(half, 2) == 1, lambda: advance(1, slot - 4))
        first = 3 * lax.div(half, 2) + 2 * lax.rem(half, 2)

        @pl.loop(jnp.minimum(first, units), jnp.minimum(first + 2 - lax.rem(half, 2), units))
        def _(unit):
            attention_unit(unit)

    @pl.loop(0, blocks)
    def _(block):
        during(block == 0, lambda: down_slot(11))
        during(block == 2, lambda: advance(1, turns))
        assemble(block)

    own_partial(2, 0)
    ring_open(2)
    SV[4:5, :] = jnp.sum(upstream_rows(pl.ds(t * rows, rows)).astype(F32), axis=0, keepdims=True)

    @pl.loop(0, 12)
    def _(half):
        slot = 12 + lax.div(half, 2)
        during(half == 2, lambda: chip_sum(0))
        during(half == 4, lambda: chip_sum(1))
        during(half == 5, share_tensor)
        during(lax.rem(half, 2) == 0, lambda: down_slot(slot))

        @pl.when(lax.rem(half, 2) == 1)
        def _():
            ring_collect(1, slot - 11)
            own_partial(2, slot - 11)
            ring_scatter(2, slot - 11)

        @pl.when(half < 2)
        def _():
            @pl.loop(2 * half, 2 * half + 2)
            def _(number):
                branch_block(number)

        @pl.when((half >= 2) & (half < 4))
        def _():
            @pl.loop(2 * half - 4, 2 * half - 2)
            def _(number):
                back_block(number)

        during(half == 8, finish_start)

        @pl.when(half >= 8)
        def _():
            @pl.loop(2 * half - 16, 2 * half - 14)
            def _(number):
                finish_part(number)

    ring_close(1)

    def advance_last(step, parts):
        during(step == turns, lambda: ring_turn(2, parts))
        during(step > turns, lambda: ring_collect(2, step - turns, parts))

    own_partial(2, turns)

    @pl.loop(turns, 2 * turns)
    def _(step):
        for side in range(2):
            count = PARTS * SPLIT[2] // 2
            advance_last(step, range(side * count, (side + 1) * count))

        during(step == 7, share_rows)
        during(step == 10, share_gather)
        during(step == 8, share_squares)
        during(step == 11, share_squares_dp)

    ring_close(2)
    share_end()

    for which in range(2):
        for kind in range(kinds[which]):
            gather(which, kind).wait_send()
        for slot in range(2):
            to_core(which, slot).wait_send()
        to_x(which).wait_send()
    for stage in range(5):
        share_all(stage).wait_send()


def angle_parts(seq_len):
    inverse = 10000.0 ** (-(np.arange(ROT // 2) * 2.0 / ROT))
    per_lane = np.zeros((128,))
    for start in (0, ROT // 2, HD, HD + ROT // 2):
        per_lane[start : start + ROT // 2] = inverse
    coarse = (np.arange(seq_len // 32) * 32.0)[:, None] * per_lane[None, :]
    fine = np.arange(32.0)[:, None] * per_lane[None, :]
    return [f(a).astype(np.float32) for a in (coarse, fine) for f in (np.cos, np.sin)]


def per_device_fused(
    tokens, cotangent, gain_attn, bias_attn, gain_mlp, bias_mlp, qkv_weight, qkv_bias,
    out_weight, out_bias, up_weight, up_bias, down_weight, down_bias,
):
    rows, width = tokens.shape
    ring = lax.axis_size("dp")
    seq = rows * lax.axis_size("tensor")
    heads = out_weight.shape[0] // HD
    hidden_width = up_weight.shape[1]
    qkv_width = qkv_weight.shape[1]
    cos_a, sin_a, cos_b, sin_b = angle_parts(seq)
    vmem = pl.BlockSpec(memory_space=pltpu.VMEM)
    hbm = pl.BlockSpec(memory_space=pl.ANY)
    V = pltpu.VMEM
    D = pltpu.SemaphoreType.DMA
    scratch = [
        V((seq, width), BF16), V((PARTS, 2, seq, 128), BF16), V((seq, width), BF16), V((seq, width), BF16),
        V((seq, hidden_width), BF16), V((seq, hidden_width), F32), V((seq, hidden_width), BF16),
        V((seq, qkv_width), BF16),
        V((heads, seq, HD), BF16), V((heads, seq, HD), BF16), V((heads, seq, HD), BF16),
        V((heads, seq, HD), BF16), V((heads, seq, HD), BF16), V((seq, heads * HD), BF16),
        V((heads, seq, HD), F32), V((heads, HD, seq), F32), V((heads, HD, seq), F32),
        V((seq, 128), F32), V((seq, 128), F32),
        V(qkv_weight.shape, BF16), V(out_weight.shape, BF16), V(up_weight.shape, BF16), V(down_weight.shape, BF16),
        V((3, 2, PARTS, ring, 128, 128), BF16), V((PARTS, 2, 128, 512), F32), V((2, 128, 512), F32),
        V((2, seq, width), BF16), V((2, 2, rows, width), BF16), V((2, rows, width), BF16),
        V((8, width), F32), V((8, width), F32), V((4, 8, width), F32),
        V((ring, 8, 128), F32), V((ring, 8, 128), F32), V((8, 128), F32),
        V((2, 8, 128), F32), V((4 + ring, 8, 128), F32),
        D((6 + 2 * PARTS,)), D((6 + 2 * PARTS,)), D((6 + 2 * PARTS,)),
        D((ring_pieces(3),)), D((ring_pieces(3) * ring,)),
        D((2, 3)), D((2, 3)), D((5,)), D((5,)),
    ]
    mixed, input_grad, gradients, sums, squares = pl.pallas_call(
        functools.partial(fused_kernel, ring),
        out_shape=[
            V((rows, width), BF16),
            V((rows, width), F32),
            V((3, 2, PARTS, ring, 128, 128), BF16),
            V((ring, 8, 128), F32),
            V((8, 128), F32),
        ],
        in_specs=[hbm, hbm] + [vmem] * 8 + [hbm] * 4 + [vmem] * 4,
        out_specs=[vmem] * 5,
        scratch_shapes=scratch,
        compiler_params=pltpu.CompilerParams(
            collective_id=0, has_side_effects=True, vmem_limit_bytes=VMEM_LIMIT
        ),
        name="layer",
    )(
        tokens, cotangent,
        *(v.reshape(1, -1) for v in (gain_attn, bias_attn, gain_mlp, bias_mlp, out_bias, down_bias)),
        qkv_bias, up_bias.reshape(1, -1),
        qkv_weight, out_weight, up_weight, down_weight, cos_a, sin_a, cos_b, sin_b,
    )
    elements = rows * width * ring * lax.axis_size("tensor")
    return closing(
        mixed, input_grad, gradients, sums, squares, elements, down_weight, up_weight, qkv_weight, out_weight
    )


def closing_kernel(
    elements,
    mixed, igrad, GB, SUMS, SQUARES,
    mixed_o, igrad_o, ga_o, ba_o, gm_o, bm_o, gq_o, bqkv_o, go_o, bo_o, gu_o, bup_o, gd_o, bd_o, stats_o,
    SD, SU, SQ, SO, sems, msem,
):
    copies = [
        pltpu.make_async_copy(mixed, mixed_o, msem.at[0]),
        pltpu.make_async_copy(igrad, igrad_o, msem.at[1]),
    ]
    for copy in copies:
        copy.start()
    for segment, stage in enumerate((SD, SU, SQ)):
        for number in range(GB.shape[3]):
            there = slice(number * 128, number * 128 + 128)
            for direction in range(2):
                for part in range(PARTS):
                    piece = GB[segment, direction, part, number].astype(F32)
                    if segment == 2 and part == 3:
                        SO[direction * 128 : direction * 128 + 128, there] = piece
                    else:
                        column = direction * (384 if segment == 2 else 512) + part * 128
                        stage[there, column : column + 128] = piece
            rows = pl.ds(number * 128, 128)
            copy = pltpu.make_async_copy(
                stage.at[rows], (gd_o, gu_o, gq_o)[segment].at[rows], sems.at[segment, number]
            )
            copy.start()
            copies.append(copy)
    copies.append(pltpu.make_async_copy(SO, go_o, msem.at[2]))
    copies[-1].start()
    for row, out in ((0, ga_o), (1, ba_o), (2, gm_o), (3, bm_o), (4, bo_o), (4, bd_o), (6, bup_o)):
        for place in range(SUMS.shape[1]):
            out[:, place * 128 : (place + 1) * 128] = SUMS[row, place : place + 1, :]
    for place in range(bqkv_o.shape[0] // 128):
        bqkv_o[place * 128 : (place + 1) * 128] = SUMS[7, place, :]
    stats_o[...] = jnp.sqrt(SQUARES[0, : stats_o.shape[0]] * (1.0 / elements))
    for copy in copies:
        copy.wait()


def closing(mixed, input_grad, gradients, sums, squares, elements, down_weight, up_weight, qkv_weight, out_weight):
    hbm = pl.BlockSpec(memory_space=pl.ANY)
    vmem = pl.BlockSpec(memory_space=pltpu.VMEM)

    def like(array, dtype=F32):
        return jax.ShapeDtypeStruct(array.shape, dtype)

    width = mixed.shape[1]
    row = jax.ShapeDtypeStruct((1, width), F32)
    outs = pl.pallas_call(
        functools.partial(closing_kernel, elements),
        in_specs=[vmem] * 5,
        out_specs=[
            hbm, hbm, vmem, vmem, vmem, vmem, hbm, vmem, hbm, vmem, hbm, vmem, hbm, vmem, vmem,
        ],
        out_shape=[
            like(mixed, BF16), like(input_grad), row, row, row, row,
            like(qkv_weight), jax.ShapeDtypeStruct((qkv_weight.shape[1],), F32), like(out_weight), row,
            like(up_weight), row, like(down_weight), row, jax.ShapeDtypeStruct((3,), F32),
        ],
        scratch_shapes=[
            pltpu.VMEM(down_weight.shape, F32),
            pltpu.VMEM(up_weight.shape, F32),
            pltpu.VMEM(qkv_weight.shape, F32),
            pltpu.VMEM(out_weight.shape, F32),
            pltpu.SemaphoreType.DMA((3, gradients.shape[3])),
            pltpu.SemaphoreType.DMA((3,)),
        ],
        compiler_params=pltpu.CompilerParams(vmem_limit_bytes=24 << 20),
        name="outputs",
    )(mixed, input_grad, gradients, sums, squares)
    return tuple(out.reshape(-1) if out.shape == (1, width) else out for out in outs)


def solution(mesh):
    in_specs = (
        P(("dp", "tensor"), None),
        P(("dp", "tensor"), None),
        P(),
        P(),
        P(),
        P(),
        P(None, "tensor"),
        P("tensor"),
        P("tensor", None),
        P(),
        P(None, "tensor"),
        P("tensor"),
        P("tensor", None),
        P(),
    )
    out_specs = (
        P(("dp", "tensor"), None),
        P(("dp", "tensor"), None),
        P(),
        P(),
        P(),
        P(),
        P(None, "tensor"),
        P("tensor"),
        P("tensor", None),
        P(),
        P(None, "tensor"),
        P("tensor"),
        P("tensor", None),
        P(),
        P(),
    )
    fused = mesh.shape["tensor"] == 4 and mesh.shape["dp"] == 8
    return jax.shard_map(
        per_device_fused if fused else per_device, mesh=mesh, in_specs=in_specs, out_specs=out_specs, check_vma=False
    )
```

```python
import functools
import math

import jax
import jax.numpy as jnp
import numpy as np
from jax import lax
from jax.experimental import pallas as pl
from jax.experimental.pallas import tpu as pltpu
from jax.sharding import PartitionSpec as P

HD = 64
ROT = 16
VMEM_LIMIT = 54 << 20


epsilon = 1e-05


def angle_tables(seq_len):
    positions = jnp.arange(seq_len, dtype=jnp.float32)
    inverse = 10000.0 ** (-(jnp.arange(ROT // 2, dtype=jnp.float32) * 2.0 / ROT))
    angles = positions[:, None] * inverse[None, :]
    cosine = jnp.concatenate([jnp.cos(angles), jnp.cos(angles)], axis=-1)[:, None, :]
    sine_part = jnp.concatenate([jnp.sin(angles), jnp.sin(angles)], axis=-1)[:, None, :]
    return (cosine, sine_part)


def rotate(field_in, cosine, sine_part):
    half_rot = ROT // 2
    first_half = field_in[..., :half_rot]
    second = field_in[..., half_rot:ROT]
    turned = jnp.concatenate([-second, first_half], axis=-1)
    return jnp.concatenate(
        [field_in[..., :ROT] * cosine + turned * sine_part, field_in[..., ROT:]], axis=-1
    )


def unrotate(grad_in, cosine, sine_part):
    half_rot = ROT // 2
    head_part = grad_in[..., :ROT]
    scaled = head_part * sine_part
    turned = jnp.concatenate([scaled[..., half_rot:], -scaled[..., :half_rot]], axis=-1)
    return jnp.concatenate([head_part * cosine + turned, grad_in[..., ROT:]], axis=-1)


def normalize(raw_rows):
    average = jnp.mean(raw_rows, axis=-1, keepdims=True)
    centred = raw_rows - average
    spread = jnp.mean(centred * centred, axis=-1, keepdims=True)
    inverse_root = lax.rsqrt(spread + epsilon)
    return (centred * inverse_root, inverse_root)


def against(left, right):
    return lax.dot_general(
        left, right, (((1,), (1,)), ((), ())), preferred_element_type=jnp.float32
    )


def per_device(
    tokens,
    cotangent,
    gain_attn,
    bias_attn,
    gain_mlp,
    bias_mlp,
    qkv_weight,
    qkv_bias,
    out_weight,
    out_bias,
    up_weight,
    up_bias,
    down_weight,
    down_bias,
):
    own_rows = tokens.shape[0]
    model_width = tokens.shape[1]
    heads_here = out_weight.shape[0] // HD
    score_scale = HD ** (-0.5)
    whole_rows = lax.all_gather(tokens, "tensor", axis=0, tiled=True)
    seq_len = whole_rows.shape[0]
    normed, _ = normalize(whole_rows.astype(jnp.float32))
    attention_input = (normed * gain_attn + bias_attn).astype(jnp.bfloat16)
    feed_input = (normed * gain_mlp + bias_mlp).astype(jnp.bfloat16)
    projected = jnp.dot(attention_input, qkv_weight, preferred_element_type=jnp.float32) + qkv_bias
    projected = projected.reshape(seq_len, heads_here, 3, HD)
    cosine, sine_part = angle_tables(seq_len)
    queries = rotate(projected[:, :, 0], cosine, sine_part).astype(jnp.bfloat16)
    keys_all = rotate(projected[:, :, 1], cosine, sine_part).astype(jnp.bfloat16)
    values_all = projected[:, :, 2].astype(jnp.bfloat16)
    preact = jnp.dot(feed_input, up_weight, preferred_element_type=jnp.float32) + up_bias
    hidden = jax.nn.gelu(preact, approximate=False).astype(jnp.bfloat16)
    block_rows = min(512, seq_len)
    block_total = seq_len // block_rows
    key_positions = jnp.arange(seq_len, dtype=jnp.int32)

    def causal_mask(offset):
        return key_positions[None, :] <= (offset + jnp.arange(block_rows, dtype=jnp.int32))[:, None]

    def forward_block(number):
        offset = number * block_rows
        query_rows = lax.dynamic_slice_in_dim(queries, offset, block_rows, 0)
        scores = (
            jnp.einsum("qhd,khd->hqk", query_rows, keys_all, preferred_element_type=jnp.float32)
            * score_scale
        )
        scores = jnp.where(causal_mask(offset)[None], scores, -1e30)
        highest = jnp.max(scores, axis=-1, keepdims=True)
        weights = jnp.exp(scores - highest)
        totals = jnp.sum(weights, axis=-1, keepdims=True)
        soft_rows = (weights / totals).astype(jnp.bfloat16)
        context_rows = jnp.einsum(
            "hqk,khd->qhd", soft_rows, values_all, preferred_element_type=jnp.float32
        ).astype(jnp.bfloat16)
        log_totals = (highest + jnp.log(totals))[:, :, 0].T
        return (context_rows, log_totals)

    context_blocks, log_blocks = lax.map(forward_block, jnp.arange(block_total, dtype=jnp.int32))
    context = context_blocks.reshape(seq_len, heads_here * HD)
    log_sums = log_blocks.reshape(seq_len, heads_here)
    context_rows = context
    branch = lax.psum_scatter(
        jnp.dot(context_rows, out_weight, preferred_element_type=jnp.float32)
        + jnp.dot(hidden, down_weight, preferred_element_type=jnp.float32),
        "tensor",
        scatter_dimension=0,
        tiled=True,
    )
    branch = branch + out_bias + down_bias
    residual_out = tokens.astype(jnp.float32) + branch
    mixed_out = residual_out.astype(jnp.bfloat16)
    forward_squares = jnp.stack([jnp.sum(residual_out * residual_out), jnp.sum(branch * branch)])
    forward_totals = lax.psum(forward_squares, ("dp", "tensor"))
    upstream = lax.all_gather(cotangent, "tensor", axis=0, tiled=True)
    out_weight_grad = jnp.einsum("sa,sd->ad", context, upstream, preferred_element_type=jnp.float32)
    down_weight_grad = jnp.einsum("sf,sd->fd", hidden, upstream, preferred_element_type=jnp.float32)
    context_grad = against(upstream, out_weight).astype(jnp.bfloat16)
    hidden_grad = against(upstream, down_weight)
    normal_cdf = 0.5 * (1.0 + lax.erf(preact * 0.5**0.5))
    density = jnp.exp(-0.5 * preact * preact) * (1.0 / math.sqrt(2.0 * math.pi))
    preact_grad = (hidden_grad * (normal_cdf + preact * density)).astype(jnp.bfloat16)
    context_grad3 = context_grad.reshape(seq_len, heads_here, HD)

    def backward_block(carried, number):
        key_grad, value_grad = carried
        offset = number * block_rows
        query_rows = lax.dynamic_slice_in_dim(queries, offset, block_rows, 0)
        grad_rows = lax.dynamic_slice_in_dim(context_grad3, offset, block_rows, 0)
        log_rows = lax.dynamic_slice_in_dim(log_sums, offset, block_rows, 0).T
        scores = (
            jnp.einsum("qhd,khd->hqk", query_rows, keys_all, preferred_element_type=jnp.float32)
            * score_scale
        )
        soft_full = jnp.exp(
            jnp.where(causal_mask(offset)[None], scores - log_rows[:, :, None], -1e30)
        )
        prob_grad = jnp.einsum(
            "qhd,khd->hqk", grad_rows, values_all, preferred_element_type=jnp.float32
        )
        deltas = jnp.sum(soft_full * prob_grad, axis=-1, keepdims=True)
        score_grad = (soft_full * (prob_grad - deltas)).astype(jnp.bfloat16)
        query_grad = (
            jnp.einsum("hqk,khd->qhd", score_grad, keys_all, preferred_element_type=jnp.float32)
            * score_scale
        )
        key_grad = (
            key_grad
            + jnp.einsum("hqk,qhd->khd", score_grad, query_rows, preferred_element_type=jnp.float32)
            * score_scale
        )
        value_grad = value_grad + jnp.einsum(
            "hqk,qhd->khd",
            soft_full.astype(jnp.bfloat16),
            grad_rows,
            preferred_element_type=jnp.float32,
        )
        return ((key_grad, value_grad), query_grad)

    empty = jnp.zeros((seq_len, heads_here, HD), jnp.float32)
    (key_grad, value_grad), query_blocks = lax.scan(
        backward_block, (empty, empty), jnp.arange(block_total, dtype=jnp.int32)
    )
    query_grad = unrotate(query_blocks.reshape(seq_len, heads_here, HD), cosine, sine_part)
    key_grad = unrotate(key_grad, cosine, sine_part)
    qkv_grad = (
        jnp.stack([query_grad, key_grad, value_grad], axis=2)
        .reshape(seq_len, 3 * heads_here * HD)
        .astype(jnp.bfloat16)
    )
    qkv_weight_grad = jnp.einsum(
        "sd,sc->dc", attention_input, qkv_grad, preferred_element_type=jnp.float32
    )
    qkv_bias_grad = jnp.sum(qkv_grad, axis=0, dtype=jnp.float32)
    up_weight_grad = jnp.einsum(
        "sd,sf->df", feed_input, preact_grad, preferred_element_type=jnp.float32
    )
    up_bias_grad = jnp.sum(preact_grad, axis=0, dtype=jnp.float32)
    own_normed, own_scale = normalize(tokens.astype(jnp.float32))
    attention_back = against(qkv_grad, qkv_weight)
    feed_back = against(preact_grad, up_weight)
    gain_terms = jnp.stack(
        [
            jnp.sum(normed * attention_back, axis=0),
            jnp.sum(attention_back, axis=0),
            jnp.sum(normed * feed_back, axis=0),
            jnp.sum(feed_back, axis=0),
        ]
    )
    normed_grad = lax.psum_scatter(
        (attention_back * gain_attn + feed_back * gain_mlp).astype(jnp.bfloat16),
        "tensor",
        scatter_dimension=0,
        tiled=True,
    ).astype(jnp.float32)
    centred_term = (
        normed_grad
        - jnp.mean(normed_grad, axis=-1, keepdims=True)
        - own_normed * jnp.mean(normed_grad * own_normed, axis=-1, keepdims=True)
    )
    input_grad = own_scale * centred_term + cotangent.astype(jnp.float32)
    (
        qkv_weight_grad,
        qkv_bias_grad,
        out_weight_grad,
        up_weight_grad,
        up_bias_grad,
        down_weight_grad,
    ) = lax.psum(
        (
            qkv_weight_grad,
            qkv_bias_grad,
            out_weight_grad,
            up_weight_grad,
            up_bias_grad,
            down_weight_grad,
        ),
        "dp",
    )
    bias_rows = jnp.sum(cotangent, axis=0, dtype=jnp.float32)
    grad_square = jnp.sum(input_grad * input_grad)
    gain_totals, bias_totals, grad_total = lax.psum(
        (gain_terms, bias_rows, grad_square), ("dp", "tensor")
    )
    square_totals = jnp.concatenate([forward_totals, grad_total[None]])
    elements = own_rows * model_width * lax.axis_size("dp") * lax.axis_size("tensor")
    statistics = jnp.sqrt(square_totals / elements)
    return (
        mixed_out,
        input_grad,
        gain_totals[0],
        gain_totals[1],
        gain_totals[2],
        gain_totals[3],
        qkv_weight_grad,
        qkv_bias_grad,
        out_weight_grad,
        bias_totals,
        up_weight_grad,
        up_bias_grad,
        down_weight_grad,
        bias_totals,
        statistics,
    )


F32 = jnp.float32
BF16 = jnp.bfloat16
MESH = pl.DeviceIdType.MESH
TILE = 256
PARTS = 4
TOGETHER = (1, 4, 1)
SPLIT = (1, 1, 1)


def ring_pieces(segments):
    return sum(2 * (PARTS // TOGETHER[number] * SPLIT[number]) for number in range(segments))


def dot_nn(left, right):
    return jnp.dot(left, right, preferred_element_type=F32)


def dot_nt(left, right):
    return lax.dot_general(left, right, (((1,), (1,)), ((), ())), preferred_element_type=F32)


def dot_tn(left, right):
    return lax.dot_general(left, right, (((0,), (0,)), ((), ())), preferred_element_type=F32)


def fused_kernel(
    ring,
    tok, cot, ga, ba, gm, bm, bo, bd, bqkv, bup, wqkv_h, wout_h, wup_h, wdn_h, cos_a, sin_a, cos_b, sin_b,
    mixed, igrad, GB, SUMS, SQO,
    T, CB, AI, FI, HID, GP, PG, QG, QH, KH, VH, CGH, CTXH, CTX, DQ, DKT, DVT, COS, SIN,
    WQKV, WOUT, WUP, WDN, RSB, PSD, PSC, PART, RA, RB, SV, ES, EX, EROWS, EY, SQ, EQ, EZ,
    lsem, g_s, g_r, r_s, r_r, b_s, b_r, e_s, e_r,
):
    rows = tok.shape[0]
    width = tok.shape[1]
    seq = T.shape[0]
    heads = QH.shape[0]
    hidden_width = WUP.shape[1]
    half_rows = rows // 2
    blocks = seq // TILE
    scale = HD ** (-0.5)
    dp = lax.axis_index("dp")
    t = lax.axis_index("tensor")
    core = lax.rem(t, 2)
    x = lax.div(t, 2)
    depth = ring // 2
    y = lax.rem(dp, 2)
    z = lax.div(dp, 2)
    at = z + y * (2 * depth - 1 - 2 * z)

    def ring_device(place):
        ny = lax.div(place, depth)
        return (2 * (place + ny * (2 * depth - 1 - 2 * place)) + ny, t)

    following = ring_device(lax.rem(at + 1, ring))
    previous = ring_device(lax.rem(at + ring - 1, ring))
    onward = (following, previous)
    core_mate = (dp, t + 1 - 2 * core)
    x_block = 2 * (1 - x) + core
    x_mate = (dp, x_block)

    def remote(src, dst, send, recv, device):
        return pltpu.make_async_remote_copy(
            src_ref=src, dst_ref=dst, send_sem=send, recv_sem=recv, device_id=device, device_id_type=MESH
        )

    def gather(which, kind):
        sems = (g_s.at[5 * which + kind], g_r.at[5 * which + kind])
        own = pl.ds(t * rows, rows)
        there = pl.ds(x_block * rows, rows)
        if which == 1:
            if kind == 0:
                return remote(CB.at[:, :, own], CB.at[:, :, own], *sems, core_mate)
            if kind <= PARTS:
                return remote(CB.at[kind - 1, :, own], CB.at[kind - 1, :, own], *sems, x_mate)
            piece = CB.at[kind - 1 - PARTS, :, there]
            return remote(piece, piece, *sems, core_mate)
        if kind == 0:
            return remote(tok, T.at[own], *sems, core_mate)
        if kind <= 2:
            off = (kind - 1) * half_rows
            return remote(tok.at[pl.ds(off, half_rows)], T.at[pl.ds(t * rows + off, half_rows)], *sems, x_mate)
        part = T.at[pl.ds(x_block * rows + (kind - 3) * half_rows, half_rows)]
        return remote(part, part, *sems, core_mate)

    kinds = (5, 1 + 2 * PARTS)

    def upstream_rows(here):
        return jnp.concatenate([CB[part, direction, here, :] for direction in range(2) for part in range(PARTS)], axis=1)

    local = [
        pltpu.make_async_copy(tok, T.at[pl.ds(t * rows, rows)], lsem.at[0]),
        pltpu.make_async_copy(wqkv_h, WQKV, lsem.at[2]),
        pltpu.make_async_copy(wup_h, WUP, lsem.at[3]),
        *(
            pltpu.make_async_copy(
                cot.at[:, pl.ds(direction * 512 + part * 128, 128)],
                CB.at[part, direction, pl.ds(t * rows, rows)],
                lsem.at[6 + 2 * part + direction],
            )
            for part in range(PARTS)
            for direction in range(2)
        ),
        pltpu.make_async_copy(wdn_h, WDN, lsem.at[4]),
        pltpu.make_async_copy(wout_h, WOUT, lsem.at[5]),
    ]
    for copy in local:
        copy.start()
    barrier = pltpu.get_barrier_semaphore()
    for mate in (core_mate, x_mate, following, previous):
        pl.semaphore_signal(barrier, inc=1, device_id=mate, device_id_type=MESH)
    pl.semaphore_wait(barrier, 4)
    gather(0, 1).start()
    gather(0, 2).start()
    gather(0, 0).start()

    @pl.loop(0, seq // 32)
    def _(a):
        ca, sa = cos_a[pl.ds(a, 1), :], sin_a[pl.ds(a, 1), :]
        cb, sb = cos_b[...], sin_b[...]
        COS[pl.ds(a * 32, 32), :] = ca * cb - sa * sb
        SIN[pl.ds(a * 32, 32), :] = sa * cb + ca * sb

    SV[...] = jnp.zeros_like(SV)
    SQ[...] = jnp.zeros_like(SQ)

    @pl.loop(0, heads)
    def _(h):
        DKT[h] = jnp.zeros(DKT.shape[1:], F32)
        DVT[h] = jnp.zeros(DVT.shape[1:], F32)


    def tables(base, group, count):
        lane = lax.broadcasted_iota(jnp.int32, (count, 128), 1)
        low_lane = jnp.where(lane >= 64, lane - 64, lane)
        cosine, sine = COS[pl.ds(base, count), :], SIN[pl.ds(base, count), :]
        if group == 1:
            cosine = jnp.where(lane >= 64, cosine, 1.0)
            sine = jnp.where(lane >= 64, sine, 0.0)
        if group == 2:
            cosine = jnp.where(lane < 64, cosine, 1.0)
            sine = jnp.where(lane < 64, sine, 0.0)
        upper = jnp.where(low_lane >= ROT // 2, sine, 0.0)
        return cosine, upper, sine - upper

    def norm_rows(base, count):
        raw = T[pl.ds(base, count), :].astype(F32)
        centred = raw - jnp.mean(raw, axis=1, keepdims=True)
        inverse_root = lax.rsqrt(jnp.mean(centred * centred, axis=1, keepdims=True) + epsilon)
        return centred * inverse_root, inverse_root

    def forward_block(block, half):
        base = pl.multiple_of(block * rows + half * half_rows, half_rows)

        @pl.loop(0, half_rows // 64)
        def _(part):
            off = pl.multiple_of(base + part * 64, 64)
            normed, _ = norm_rows(off, 64)
            AI[pl.ds(off, 64), :] = (normed * ga[...] + ba[...]).astype(BF16)
            FI[pl.ds(off, 64), :] = (normed * gm[...] + bm[...]).astype(BF16)

        for group in range(3 * heads // 2):
            if group % 2 == 0:
                columns = slice(group * 128, group * 128 + 256)
                pair = dot_nn(AI[pl.ds(base, half_rows), :], WQKV[:, columns]) + bqkv[columns].reshape(1, 256)
            value = pair[:, (group % 2) * 128 : (group % 2) * 128 + 128]
            cosine, upper, lower = tables(base, group % 3, half_rows)
            turned = (
                value * cosine
                - lower * pltpu.roll(value, 128 - ROT // 2, 1)
                + upper * pltpu.roll(value, ROT // 2, 1)
            ).astype(BF16)
            first = 2 * (group // 3)
            left, left_head = ((QH, first), (VH, first), (KH, first + 1))[group % 3]
            right, right_head = ((KH, first), (QH, first + 1), (VH, first + 1))[group % 3]
            left[left_head, pl.ds(base, half_rows), :] = turned[:, :HD]
            right[right_head, pl.ds(base, half_rows), :] = turned[:, HD:]

        for part in range(hidden_width // TILE):
            columns = slice(part * TILE, (part + 1) * TILE)
            preact = dot_nn(FI[pl.ds(base, half_rows), :], WUP[:, columns]) + bup[:, columns]
            cdf = 0.5 * (1.0 + lax.erf(preact * 0.5**0.5))
            density = jnp.exp(-0.5 * preact * preact) * (1.0 / math.sqrt(2.0 * math.pi))
            HID[pl.ds(base, half_rows), columns] = (preact * cdf).astype(BF16)
            GP[pl.ds(base, half_rows), columns] = cdf + preact * density

    def cotangent_block(block):
        base = pl.multiple_of(block * rows, rows)
        upstream = upstream_rows(pl.ds(base, rows))
        grad = dot_nt(upstream, WOUT[...]).astype(BF16)
        for h in range(heads):
            CGH[h, pl.ds(base, rows), :] = grad[:, h * HD : (h + 1) * HD]

        for part in range(hidden_width // TILE):
            columns = slice(part * TILE, (part + 1) * TILE)
            back = dot_nt(upstream, WDN[columns, :])
            rounded = (back * GP[pl.ds(base, rows), columns]).astype(BF16)
            PG[pl.ds(base, rows), columns] = rounded
            SV[6:7, columns] += jnp.sum(rounded.astype(F32), axis=0, keepdims=True)

    def attention_rows(h, own):
        here = slice(own * TILE, (own + 1) * TILE)
        before = own * TILE
        reach = before + TILE
        query = QH[h, here, :]
        grad = CGH[h, here, :]
        keys = KH[h, :reach, :]
        values = VH[h, :reach, :]
        scores = dot_nt(query, keys) * scale
        row_at = lax.broadcasted_iota(jnp.int32, (TILE, TILE), 0)
        column_at = lax.broadcasted_iota(jnp.int32, (TILE, TILE), 1)
        corner = jnp.where(column_at <= row_at, scores[:, before:], -1e30)
        scores = jnp.concatenate([scores[:, :before], corner], axis=1) if own else corner
        weights = jnp.exp(scores - jnp.max(scores, axis=1, keepdims=True))
        probs = weights * (1.0 / jnp.sum(weights, axis=1, keepdims=True))
        soft = probs.astype(BF16)
        CTXH[h, here, :] = dot_nn(soft, values).astype(BF16)
        prob_grad = dot_nt(grad, values)
        delta = jnp.sum(probs * prob_grad, axis=1, keepdims=True)
        score_grad = (probs * (prob_grad - delta)).astype(BF16)
        DQ[h, here, :] = scale * dot_nn(score_grad, keys)
        DKT[h, :, :reach] += dot_nn(query.astype(F32).T.astype(BF16), score_grad)
        DVT[h, :, :reach] += dot_nn(grad.astype(F32).T.astype(BF16), soft)

    def attention_unit(unit):
        h = lax.div(unit, blocks)
        for number, own in enumerate(sorted(range(blocks), key=lambda own: min(own, blocks - 1 - own))):
            pl.when(lax.rem(unit, blocks) == number)(functools.partial(attention_rows, h, own))

    def assemble(block):
        base = pl.multiple_of(block * TILE, TILE)
        here = pl.ds(base, TILE)
        for pair in range(heads // 2):
            one, two = 2 * pair, 2 * pair + 1
            CTX[here, pair * 128 : (pair + 1) * 128] = jnp.concatenate(
                [CTXH[one, here, :], CTXH[two, here, :]], axis=1
            )
            parts = [
                (DQ[one, here, :], scale * DKT[one, :, here].T),
                (DVT[one, :, here].T, DQ[two, here, :]),
                (scale * DKT[two, :, here].T, DVT[two, :, here].T),
            ]
            for group, (left, right) in enumerate(parts):
                grad = jnp.concatenate([left, right], axis=1)
                cosine, upper, lower = tables(base, group, TILE)
                turned = (
                    grad * cosine
                    + pltpu.roll(grad * upper, 128 - ROT // 2, 1)
                    - pltpu.roll(grad * lower, ROT // 2, 1)
                ).astype(BF16)
                columns = slice((3 * pair + group) * 128, (3 * pair + group + 1) * 128)
                QG[here, columns] = turned
                SV[7:8, columns] += jnp.sum(turned.astype(F32), axis=0, keepdims=True)

    def order(step):
        flip_core = 1 - lax.div(step, 2)
        flip_x = 1 - lax.rem(step, 2)
        return 2 * lax.rem(x + flip_x, 2) + lax.rem(core + flip_core, 2)

    def to_core(which, slot):
        block = (2 * x + 1 - core) if slot == 0 else (2 * (1 - x) + 1 - core)
        return remote(
            PART.at[which, pl.ds(block * rows, rows)], RA.at[which, slot],
            b_s.at[which, slot], b_r.at[which, slot], core_mate,
        )

    def to_x(which):
        return remote(
            PART.at[which, pl.ds(x_block * rows, rows)], RB.at[which],
            b_s.at[which, 2], b_r.at[which, 2], x_mate,
        )

    def send_after(which, step):
        @pl.when(step == 0)
        def _():
            to_core(which, 1).start()

        @pl.when(step == 1)
        def _():
            to_core(which, 0).start()

    def branch_block(step):
        base = pl.multiple_of(order(step) * rows, rows)
        here = pl.ds(base, rows)

        for part in range(width // TILE):
            columns = slice(part * TILE, (part + 1) * TILE)
            PART[0, here, columns] = (
                dot_nn(CTX[here, :], WOUT[:, columns]) + dot_nn(HID[here, :], WDN[:, columns])
            ).astype(BF16)

        send_after(0, step)

    def back_block(step):
        base = pl.multiple_of(order(step) * rows, rows)
        here = pl.ds(base, rows)
        raw = T[here, :].astype(F32)
        average = jnp.mean(raw, axis=1, keepdims=True)
        spread = jnp.mean((raw - average) * (raw - average), axis=1, keepdims=True)
        inverse_root = lax.rsqrt(spread + epsilon)

        for part in range(width // TILE):
            columns = slice(part * TILE, (part + 1) * TILE)
            normed = (T[here, columns].astype(F32) - average) * inverse_root
            attention_back = dot_nt(QG[here, :], WQKV[columns, :])
            feed_back = dot_nt(PG[here, :], WUP[columns, :])
            SV[0:1, columns] += jnp.sum(normed * attention_back, axis=0, keepdims=True)
            SV[1:2, columns] += jnp.sum(attention_back, axis=0, keepdims=True)
            SV[2:3, columns] += jnp.sum(normed * feed_back, axis=0, keepdims=True)
            SV[3:4, columns] += jnp.sum(feed_back, axis=0, keepdims=True)
            PART[1, here, columns] = (attention_back * ga[:, columns] + feed_back * gm[:, columns]).astype(BF16)

        send_after(1, step)

    def chip_sum(which):
        to_core(which, 1).wait_recv()
        there = pl.ds(pl.multiple_of(x_block * rows, rows), rows)
        PART[which, there, :] = (PART[which, there, :].astype(F32) + RA[which, 1].astype(F32)).astype(BF16)
        to_x(which).start()

    def finish_start():
        for which in range(2):
            to_core(which, 0).wait_recv()
            to_x(which).wait_recv()
    def total(which, off):
        return (
            PART[which, pl.ds(pl.multiple_of(t * rows + off, 32), 32), :].astype(F32)
            + RA[which, 0, pl.ds(off, 32), :].astype(F32)
            + RB[which, pl.ds(off, 32), :].astype(F32)
        )

    def square(value):
        return jnp.sum(jnp.sum(value * value, axis=1, keepdims=True), axis=0, keepdims=True)

    def finish_part(number):
        off = pl.multiple_of(number * 32, 32)
        here = pl.ds(pl.multiple_of(t * rows + off, 32), 32)
        branch = total(0, off) + bo[...] + bd[...]
        residual = T[here, :].astype(F32) + branch
        mixed[pl.ds(off, 32), :] = residual.astype(BF16)
        normed, inverse_root = norm_rows(t * rows + off, 32)
        grad = total(1, off)
        grad = inverse_root * (
            grad
            - jnp.mean(grad, axis=1, keepdims=True)
            - normed * jnp.mean(grad * normed, axis=1, keepdims=True)
        ) + upstream_rows(here).astype(F32)
        igrad[pl.ds(off, 32), :] = grad
        spot = lax.broadcasted_iota(jnp.int32, SQ.shape, 1)
        for place, value in enumerate((residual, branch, grad)):
            SQ[...] += jnp.where(spot == place, square(value), 0.0)

    members = (4, ring, ring, 4, ring)

    def share(stage, offset):
        over_tensor = stage in (0, 3)
        mate = (dp, lax.rem(t + offset, 4)) if over_tensor else (lax.rem(dp + offset, ring), t)
        src, dst = (
            lambda: (ES, EX.at[t]),
            lambda: (EROWS.at[lax.rem(dp + offset, ring)], EY.at[dp]),
            lambda: (SUMS.at[dp], SUMS.at[dp]),
            lambda: (EQ.at[0], EZ.at[t]),
            lambda: (EQ.at[1], EZ.at[4 + dp]),
        )[stage]()
        return remote(src, dst, e_s.at[stage], e_r.at[stage], mate)

    def share_start(stage):
        for offset in range(1, members[stage]):
            share(stage, offset).start()

    def share_all(stage):
        ref, first = ((EX, 0), (EY, 0), (SUMS, 0), (EZ, 0), (EZ, 4))[stage]
        whole = ref.at[pl.ds(first, members[stage] - 1)]
        return remote(whole, whole, e_s.at[stage], e_r.at[stage], core_mate)

    def share_wait(stage):
        share_all(stage).wait_recv()

    def added(ref, first, count):
        total = ref[first]
        for number in range(1, count):
            total = total + ref[first + number]
        return total

    def share_tensor():
        ES[...] = SV[...]
        EX[t] = SV[...]
        share_start(0)

    def share_rows():
        share_wait(0)
        row = lax.broadcasted_iota(jnp.int32, SV.shape, 0)
        total = jnp.where(row < 5, added(EX, 0, 4), SV[...])
        for place in range(ring):
            EROWS[:, place, :] = total[:, place * 128 : (place + 1) * 128]
        EY[dp] = EROWS[dp]
        share_start(1)

    def share_gather():
        share_wait(1)
        SUMS[dp] = added(EY, 0, ring)
        share_start(2)

    def share_squares():
        EQ[0] = SQ[...]
        EZ[t] = SQ[...]
        share_start(3)

    def share_squares_dp():
        share_wait(3)
        total = added(EZ, 0, 4)
        EQ[1] = total
        EZ[4 + dp] = total
        share_start(4)

    def share_end():
        share_wait(2)
        share_wait(4)
        SQO[...] = added(EZ, 4, ring)

    def chunk(direction, step):
        return lax.rem(at + ring - step, ring) if direction == 0 else lax.rem(at + step, ring)

    def gathered(direction, step):
        return lax.rem(at + 1 + ring - step, ring) if direction == 0 else lax.rem(at + ring - 1 + step, ring)

    def left_of(segment, direction, step):
        columns = pl.ds(pl.multiple_of(chunk(direction, step) * 128, 128), 128)
        return (HID, FI, AI)[segment][:, columns]

    def own_piece(step, part):
        for direction in range(2):
            PSD[lax.rem(step, PARTS), direction, :, part * 128 : (part + 1) * 128] = dot_tn(
                left_of(0, direction, step), CB[part, direction]
            )

    def own_down(step):
        for direction in range(2):
            right = jnp.concatenate([CB[part, direction] for part in range(PARTS)], axis=1)
            PSD[lax.rem(step, PARTS), direction] = dot_tn(left_of(0, direction, step), right)

    def own_partial(segment, step):
        for direction in range(2):
            left = left_of(segment, direction, step)
            if segment == 1:
                PSC[direction] = dot_tn(left, PG[:, direction * 512 : (direction + 1) * 512])
            else:
                number = chunk(direction, step)
                PSC[direction, :, 0:384] = dot_tn(left, QG[:, direction * 384 : (direction + 1) * 384])
                PSC[direction, :, 384:512] = dot_tn(
                    CTX[:, direction * 128 : (direction + 1) * 128], CB[lax.rem(number, PARTS), lax.div(number, PARTS)]
                )

    def parts_of(segment, piece):
        return pl.ds(piece // SPLIT[segment] * TOGETHER[segment], TOGETHER[segment])

    def rows_of(segment, piece):
        count = 128 // SPLIT[segment]
        return slice(piece % SPLIT[segment] * count, (piece % SPLIT[segment] + 1) * count)

    def sems_of(segment, direction, piece, step):
        number = ring_pieces(segment) + direction * (PARTS // TOGETHER[segment] * SPLIT[segment]) + piece
        return r_s.at[number], r_r.at[number * ring + lax.rem(step, ring)]

    def scatter(segment, direction, piece, step):
        parts, here = parts_of(segment, piece), rows_of(segment, piece)
        return remote(
            RSB.at[segment, direction, parts, step, here], RSB.at[segment, direction, parts, step + 1, here],
            *sems_of(segment, direction, piece, step), onward[direction],
        )

    def collect(segment, direction, piece, step):
        block = GB.at[segment, direction, parts_of(segment, piece), gathered(direction, step), rows_of(segment, piece)]
        return remote(
            block, block, *sems_of(segment, direction, piece, ring - 1 + step), onward[direction]
        )

    turns = ring - 1

    def during(condition, work):
        pl.when(condition)(work)

    def pieces(segment, parts=None):
        parts = range(PARTS // TOGETHER[segment] * SPLIT[segment]) if parts is None else parts
        return [(piece, direction) for piece in parts for direction in range(2)]

    def members_of(segment, piece):
        first = piece // SPLIT[segment] * TOGETHER[segment]
        return range(first, first + TOGETHER[segment])

    def term(segment, direction, part, step, here):
        columns = slice(part * 128, (part + 1) * 128)
        if segment == 0:
            return PSD[lax.rem(step, PARTS), direction, here, columns]
        return PSC[direction, here, columns]

    def sent(segment, direction, piece):
        scatter(segment, direction, piece, 0).wait_send()

    def ring_open(segment, parts=None):
        for piece, direction in pieces(segment, parts):
            here = rows_of(segment, piece)
            for part in members_of(segment, piece):
                RSB[segment, direction, part, 0, here] = term(segment, direction, part, 0, here).astype(BF16)
            scatter(segment, direction, piece, 0).start()

    def ring_scatter(segment, step, parts=None):
        for piece, direction in pieces(segment, parts):
            here = rows_of(segment, piece)
            scatter(segment, direction, piece, step - 1).wait_recv()
            for part in members_of(segment, piece):
                RSB[segment, direction, part, step, here] = (
                    RSB[segment, direction, part, step, here].astype(F32) + term(segment, direction, part, step, here)
                ).astype(BF16)
            sent(segment, direction, piece)
            scatter(segment, direction, piece, step).start()

    def ring_turn(segment, parts=None):
        last = ring - 1
        for piece, direction in pieces(segment, parts):
            here = rows_of(segment, piece)
            scatter(segment, direction, piece, last - 1).wait_recv()
            for part in members_of(segment, piece):
                GB[segment, direction, part, gathered(direction, 0), here] = (
                    RSB[segment, direction, part, last, here].astype(F32) + term(segment, direction, part, last, here)
                ).astype(BF16)
            sent(segment, direction, piece)
            collect(segment, direction, piece, 0).start()

    def ring_collect(segment, step, parts=None):
        for piece, direction in pieces(segment, parts):
            collect(segment, direction, piece, step - 1).wait_recv()
            sent(segment, direction, piece)
            collect(segment, direction, piece, step).start()

    def ring_close(segment, parts=None):
        for piece, direction in pieces(segment, parts):
            collect(segment, direction, piece, ring - 2).wait_recv()
            sent(segment, direction, piece)

    def down_terms(slot):
        during((slot >= PARTS) & (slot <= turns), lambda: own_down(slot))
        for part in range(PARTS):
            event = slot - part
            during((event > 0) & (event < PARTS), lambda: own_piece(event, part))

    def down_slot(slot):
        for part in range(PARTS):
            event = slot - part
            during(event < turns, lambda: ring_scatter(0, event, (part,)))
            during(event == turns, lambda: ring_turn(0, (part,)))
            during((event > turns) & (event < 2 * turns), lambda: ring_collect(0, event - turns, (part,)))
            during(event == 2 * turns, lambda: ring_close(0, (part,)))
        down_terms(slot + 1)

    for copy in local[:3]:
        copy.wait()

    def place_of(step):
        return 2 * lax.rem(x + lax.div(step, 2), 2) + lax.rem(core + lax.rem(step, 2), 2)

    @pl.loop(0, 8)
    def _(step):
        @pl.when(step == 1)
        def _():
            for copy in local[3:]:
                copy.wait()
            for kind in range(PARTS + 1):
                gather(1, kind).start()

        @pl.when(step == 2)
        def _():
            gather(0, 0).wait_recv()

        for half in range(2):

            @pl.when(step == 4 + 2 * half)
            def _():
                gather(0, 1 + half).wait_recv()
                gather(0, 3 + half).start()

            @pl.when(step == 5 + 2 * half)
            def _():
                gather(0, 3 + half).wait_recv()

        late = lax.div(step, 4)
        block = place_of(2 * late + jnp.where(late == 1, lax.rem(step, 2), lax.div(step, 2)))
        forward_block(block, jnp.where(late == 1, lax.div(step - 4, 2), lax.rem(step, 2)))

        @pl.when(step == 5)
        def _():
            cotangent_block(place_of(0))

    gather(1, 0).wait_recv()
    for slot in range(PARTS):
        gather(1, 1 + slot).wait_recv()
        gather(1, 1 + PARTS + slot).start()
        for part in range(slot):
            ring_scatter(0, slot - part, (part,))
        gather(1, 1 + PARTS + slot).wait_recv()
        both = dot_tn(left_of(0, 0, 0), jnp.concatenate([CB[slot, 0], CB[slot, 1]], axis=1))
        for direction in range(2):
            PSD[0, direction, :, slot * 128 : (slot + 1) * 128] = both[:, direction * 128 : (direction + 1) * 128]
        ring_open(0, (slot,))
        if slot == PARTS - 1:
            down_terms(PARTS)
        else:
            for part in range(slot + 1):
                own_piece(slot + 1 - part, part)
        if slot == 0:
            cotangent_block(place_of(1))

    cotangent_block(place_of(2))
    down_slot(4)
    cotangent_block(place_of(3))
    own_partial(1, 0)
    ring_open(1)

    def advance(segment, step):
        @pl.when(step <= turns)
        def _():
            own_partial(segment, step)

        during(step < turns, lambda: ring_scatter(segment, step))
        during(step == turns, lambda: ring_turn(segment))
        during(step > turns, lambda: ring_collect(segment, step - turns))

    units = heads * blocks

    @pl.loop(0, 12)
    def _(half):
        slot = 5 + lax.div(half, 2)
        during(lax.rem(half, 2) == 0, lambda: down_slot(slot))
        during(lax.rem(half, 2) == 1, lambda: advance(1, slot - 4))
        first = 3 * lax.div(half, 2) + 2 * lax.rem(half, 2)

        @pl.loop(jnp.minimum(first, units), jnp.minimum(first + 2 - lax.rem(half, 2), units))
        def _(unit):
            attention_unit(unit)

    @pl.loop(0, blocks)
    def _(block):
        during(block == 0, lambda: down_slot(11))
        during(block == 2, lambda: advance(1, turns))
        assemble(block)

    own_partial(2, 0)
    ring_open(2)
    SV[4:5, :] = jnp.sum(upstream_rows(pl.ds(t * rows, rows)).astype(F32), axis=0, keepdims=True)

    @pl.loop(0, 12)
    def _(half):
        slot = 12 + lax.div(half, 2)
        during(half == 2, lambda: chip_sum(0))
        during(half == 4, lambda: chip_sum(1))
        during(half == 5, share_tensor)
        during(lax.rem(half, 2) == 0, lambda: down_slot(slot))

        @pl.when(lax.rem(half, 2) == 1)
        def _():
            ring_collect(1, slot - 11)
            own_partial(2, slot - 11)
            ring_scatter(2, slot - 11)

        @pl.when(half < 2)
        def _():
            @pl.loop(2 * half, 2 * half + 2)
            def _(number):
                branch_block(number)

        @pl.when((half >= 2) & (half < 4))
        def _():
            @pl.loop(2 * half - 4, 2 * half - 2)
            def _(number):
                back_block(number)

        during(half == 8, finish_start)

        @pl.when(half >= 8)
        def _():
            @pl.loop(2 * half - 16, 2 * half - 14)
            def _(number):
                finish_part(number)

    ring_close(1)

    def advance_last(step, parts):
        during(step == turns, lambda: ring_turn(2, parts))
        during(step > turns, lambda: ring_collect(2, step - turns, parts))

    own_partial(2, turns)

    @pl.loop(turns, 2 * turns)
    def _(step):
        for side in range(2):
            count = PARTS * SPLIT[2] // 2
            advance_last(step, range(side * count, (side + 1) * count))

        during(step == 7, share_rows)
        during(step == 10, share_gather)
        during(step == 8, share_squares)
        during(step == 11, share_squares_dp)

    ring_close(2)
    share_end()

    for which in range(2):
        for kind in range(kinds[which]):
            gather(which, kind).wait_send()
        for slot in range(2):
            to_core(which, slot).wait_send()
        to_x(which).wait_send()
    for stage in range(5):
        share_all(stage).wait_send()


def angle_parts(seq_len):
    inverse = 10000.0 ** (-(np.arange(ROT // 2) * 2.0 / ROT))
    per_lane = np.zeros((128,))
    for start in (0, ROT // 2, HD, HD + ROT // 2):
        per_lane[start : start + ROT // 2] = inverse
    coarse = (np.arange(seq_len // 32) * 32.0)[:, None] * per_lane[None, :]
    fine = np.arange(32.0)[:, None] * per_lane[None, :]
    return [f(a).astype(np.float32) for a in (coarse, fine) for f in (np.cos, np.sin)]


def per_device_fused(
    tokens, cotangent, gain_attn, bias_attn, gain_mlp, bias_mlp, qkv_weight, qkv_bias,
    out_weight, out_bias, up_weight, up_bias, down_weight, down_bias,
):
    rows, width = tokens.shape
    ring = lax.axis_size("dp")
    seq = rows * lax.axis_size("tensor")
    heads = out_weight.shape[0] // HD
    hidden_width = up_weight.shape[1]
    qkv_width = qkv_weight.shape[1]
    cos_a, sin_a, cos_b, sin_b = angle_parts(seq)
    vmem = pl.BlockSpec(memory_space=pltpu.VMEM)
    hbm = pl.BlockSpec(memory_space=pl.ANY)
    V = pltpu.VMEM
    D = pltpu.SemaphoreType.DMA
    scratch = [
        V((seq, width), BF16), V((PARTS, 2, seq, 128), BF16), V((seq, width), BF16), V((seq, width), BF16),
        V((seq, hidden_width), BF16), V((seq, hidden_width), F32), V((seq, hidden_width), BF16),
        V((seq, qkv_width), BF16),
        V((heads, seq, HD), BF16), V((heads, seq, HD), BF16), V((heads, seq, HD), BF16),
        V((heads, seq, HD), BF16), V((heads, seq, HD), BF16), V((seq, heads * HD), BF16),
        V((heads, seq, HD), F32), V((heads, HD, seq), F32), V((heads, HD, seq), F32),
        V((seq, 128), F32), V((seq, 128), F32),
        V(qkv_weight.shape, BF16), V(out_weight.shape, BF16), V(up_weight.shape, BF16), V(down_weight.shape, BF16),
        V((3, 2, PARTS, ring, 128, 128), BF16), V((PARTS, 2, 128, 512), F32), V((2, 128, 512), F32),
        V((2, seq, width), BF16), V((2, 2, rows, width), BF16), V((2, rows, width), BF16),
        V((8, width), F32), V((8, width), F32), V((4, 8, width), F32),
        V((ring, 8, 128), F32), V((ring, 8, 128), F32), V((8, 128), F32),
        V((2, 8, 128), F32), V((4 + ring, 8, 128), F32),
        D((6 + 2 * PARTS,)), D((6 + 2 * PARTS,)), D((6 + 2 * PARTS,)),
        D((ring_pieces(3),)), D((ring_pieces(3) * ring,)),
        D((2, 3)), D((2, 3)), D((5,)), D((5,)),
    ]
    mixed, input_grad, gradients, sums, squares = pl.pallas_call(
        functools.partial(fused_kernel, ring),
        out_shape=[
            V((rows, width), BF16),
            V((rows, width), F32),
            V((3, 2, PARTS, ring, 128, 128), BF16),
            V((ring, 8, 128), F32),
            V((8, 128), F32),
        ],
        in_specs=[hbm, hbm] + [vmem] * 8 + [hbm] * 4 + [vmem] * 4,
        out_specs=[vmem] * 5,
        scratch_shapes=scratch,
        compiler_params=pltpu.CompilerParams(
            collective_id=0, has_side_effects=True, vmem_limit_bytes=VMEM_LIMIT
        ),
        name="layer",
    )(
        tokens, cotangent,
        *(v.reshape(1, -1) for v in (gain_attn, bias_attn, gain_mlp, bias_mlp, out_bias, down_bias)),
        qkv_bias, up_bias.reshape(1, -1),
        qkv_weight, out_weight, up_weight, down_weight, cos_a, sin_a, cos_b, sin_b,
    )
    elements = rows * width * ring * lax.axis_size("tensor")
    return closing(
        mixed, input_grad, gradients, sums, squares, elements, down_weight, up_weight, qkv_weight, out_weight
    )


def closing_kernel(
    elements,
    mixed, igrad, GB, SUMS, SQUARES,
    mixed_o, igrad_o, ga_o, ba_o, gm_o, bm_o, gq_o, bqkv_o, go_o, bo_o, gu_o, bup_o, gd_o, bd_o, stats_o,
    SD, SU, SQ, SO, sems, msem,
):
    copies = [
        pltpu.make_async_copy(mixed, mixed_o, msem.at[0]),
        pltpu.make_async_copy(igrad, igrad_o, msem.at[1]),
    ]
    for copy in copies:
        copy.start()
    for segment, stage in enumerate((SD, SU, SQ)):
        for number in range(GB.shape[3]):
            there = slice(number * 128, number * 128 + 128)
            for direction in range(2):
                for part in range(PARTS):
                    piece = GB[segment, direction, part, number].astype(F32)
                    if segment == 2 and part == 3:
                        SO[direction * 128 : direction * 128 + 128, there] = piece
                    else:
                        column = direction * (384 if segment == 2 else 512) + part * 128
                        stage[there, column : column + 128] = piece
            rows = pl.ds(number * 128, 128)
            copy = pltpu.make_async_copy(
                stage.at[rows], (gd_o, gu_o, gq_o)[segment].at[rows], sems.at[segment, number]
            )
            copy.start()
            copies.append(copy)
    copies.append(pltpu.make_async_copy(SO, go_o, msem.at[2]))
    copies[-1].start()
    for row, out in ((0, ga_o), (1, ba_o), (2, gm_o), (3, bm_o), (4, bo_o), (4, bd_o), (6, bup_o)):
        for place in range(SUMS.shape[1]):
            out[:, place * 128 : (place + 1) * 128] = SUMS[row, place : place + 1, :]
    for place in range(bqkv_o.shape[0] // 128):
        bqkv_o[place * 128 : (place + 1) * 128] = SUMS[7, place, :]
    stats_o[...] = jnp.sqrt(SQUARES[0, : stats_o.shape[0]] * (1.0 / elements))
    for copy in copies:
        copy.wait()


def closing(mixed, input_grad, gradients, sums, squares, elements, down_weight, up_weight, qkv_weight, out_weight):
    hbm = pl.BlockSpec(memory_space=pl.ANY)
    vmem = pl.BlockSpec(memory_space=pltpu.VMEM)

    def like(array, dtype=F32):
        return jax.ShapeDtypeStruct(array.shape, dtype)

    width = mixed.shape[1]
    row = jax.ShapeDtypeStruct((1, width), F32)
    outs = pl.pallas_call(
        functools.partial(closing_kernel, elements),
        in_specs=[vmem] * 5,
        out_specs=[
            hbm, hbm, vmem, vmem, vmem, vmem, hbm, vmem, hbm, vmem, hbm, vmem, hbm, vmem, vmem,
        ],
        out_shape=[
            like(mixed, BF16), like(input_grad), row, row, row, row,
            like(qkv_weight), jax.ShapeDtypeStruct((qkv_weight.shape[1],), F32), like(out_weight), row,
            like(up_weight), row, like(down_weight), row, jax.ShapeDtypeStruct((3,), F32),
        ],
        scratch_shapes=[
            pltpu.VMEM(down_weight.shape, F32),
            pltpu.VMEM(up_weight.shape, F32),
            pltpu.VMEM(qkv_weight.shape, F32),
            pltpu.VMEM(out_weight.shape, F32),
            pltpu.SemaphoreType.DMA((3, gradients.shape[3])),
            pltpu.SemaphoreType.DMA((3,)),
        ],
        compiler_params=pltpu.CompilerParams(vmem_limit_bytes=24 << 20),
        name="outputs",
    )(mixed, input_grad, gradients, sums, squares)
    return tuple(out.reshape(-1) if out.shape == (1, width) else out for out in outs)


def solution(mesh):
    in_specs = (
        P(("dp", "tensor"), None),
        P(("dp", "tensor"), None),
        P(),
        P(),
        P(),
        P(),
        P(None, "tensor"),
        P("tensor"),
        P("tensor", None),
        P(),
        P(None, "tensor"),
        P("tensor"),
        P("tensor", None),
        P(),
    )
    out_specs = (
        P(("dp", "tensor"), None),
        P(("dp", "tensor"), None),
        P(),
        P(),
        P(),
        P(),
        P(None, "tensor"),
        P("tensor"),
        P("tensor", None),
        P(),
        P(None, "tensor"),
        P("tensor"),
        P("tensor", None),
        P(),
        P(),
    )
    fused = mesh.shape["tensor"] == 4 and mesh.shape["dp"] == 8
    return jax.shard_map(
        per_device_fused if fused else per_device, mesh=mesh, in_specs=in_specs, out_specs=out_specs, check_vma=False
    )
```

```python
import functools
import math

import jax
import jax.numpy as jnp
import numpy as np
from jax import lax
from jax.experimental import pallas as pl
from jax.experimental.pallas import tpu as pltpu
from jax.sharding import PartitionSpec as P

HD = 64
ROT = 16
VMEM_LIMIT = 54 << 20


epsilon = 1e-05


def angle_tables(seq_len):
    positions = jnp.arange(seq_len, dtype=jnp.float32)
    inverse = 10000.0 ** (-(jnp.arange(ROT // 2, dtype=jnp.float32) * 2.0 / ROT))
    angles = positions[:, None] * inverse[None, :]
    cosine = jnp.concatenate([jnp.cos(angles), jnp.cos(angles)], axis=-1)[:, None, :]
    sine_part = jnp.concatenate([jnp.sin(angles), jnp.sin(angles)], axis=-1)[:, None, :]
    return (cosine, sine_part)


def rotate(field_in, cosine, sine_part):
    half_rot = ROT // 2
    first_half = field_in[..., :half_rot]
    second = field_in[..., half_rot:ROT]
    turned = jnp.concatenate([-second, first_half], axis=-1)
    return jnp.concatenate(
        [field_in[..., :ROT] * cosine + turned * sine_part, field_in[..., ROT:]], axis=-1
    )


def unrotate(grad_in, cosine, sine_part):
    half_rot = ROT // 2
    head_part = grad_in[..., :ROT]
    scaled = head_part * sine_part
    turned = jnp.concatenate([scaled[..., half_rot:], -scaled[..., :half_rot]], axis=-1)
    return jnp.concatenate([head_part * cosine + turned, grad_in[..., ROT:]], axis=-1)


def normalize(raw_rows):
    average = jnp.mean(raw_rows, axis=-1, keepdims=True)
    centred = raw_rows - average
    spread = jnp.mean(centred * centred, axis=-1, keepdims=True)
    inverse_root = lax.rsqrt(spread + epsilon)
    return (centred * inverse_root, inverse_root)


def against(left, right):
    return lax.dot_general(
        left, right, (((1,), (1,)), ((), ())), preferred_element_type=jnp.float32
    )


def per_device(
    tokens,
    cotangent,
    gain_attn,
    bias_attn,
    gain_mlp,
    bias_mlp,
    qkv_weight,
    qkv_bias,
    out_weight,
    out_bias,
    up_weight,
    up_bias,
    down_weight,
    down_bias,
):
    own_rows = tokens.shape[0]
    model_width = tokens.shape[1]
    heads_here = out_weight.shape[0] // HD
    score_scale = HD ** (-0.5)
    whole_rows = lax.all_gather(tokens, "tensor", axis=0, tiled=True)
    seq_len = whole_rows.shape[0]
    normed, _ = normalize(whole_rows.astype(jnp.float32))
    attention_input = (normed * gain_attn + bias_attn).astype(jnp.bfloat16)
    feed_input = (normed * gain_mlp + bias_mlp).astype(jnp.bfloat16)
    projected = jnp.dot(attention_input, qkv_weight, preferred_element_type=jnp.float32) + qkv_bias
    projected = projected.reshape(seq_len, heads_here, 3, HD)
    cosine, sine_part = angle_tables(seq_len)
    queries = rotate(projected[:, :, 0], cosine, sine_part).astype(jnp.bfloat16)
    keys_all = rotate(projected[:, :, 1], cosine, sine_part).astype(jnp.bfloat16)
    values_all = projected[:, :, 2].astype(jnp.bfloat16)
    preact = jnp.dot(feed_input, up_weight, preferred_element_type=jnp.float32) + up_bias
    hidden = jax.nn.gelu(preact, approximate=False).astype(jnp.bfloat16)
    block_rows = min(512, seq_len)
    block_total = seq_len // block_rows
    key_positions = jnp.arange(seq_len, dtype=jnp.int32)

    def causal_mask(offset):
        return key_positions[None, :] <= (offset + jnp.arange(block_rows, dtype=jnp.int32))[:, None]

    def forward_block(number):
        offset = number * block_rows
        query_rows = lax.dynamic_slice_in_dim(queries, offset, block_rows, 0)
        scores = (
            jnp.einsum("qhd,khd->hqk", query_rows, keys_all, preferred_element_type=jnp.float32)
            * score_scale
        )
        scores = jnp.where(causal_mask(offset)[None], scores, -1e30)
        highest = jnp.max(scores, axis=-1, keepdims=True)
        weights = jnp.exp(scores - highest)
        totals = jnp.sum(weights, axis=-1, keepdims=True)
        soft_rows = (weights / totals).astype(jnp.bfloat16)
        context_rows = jnp.einsum(
            "hqk,khd->qhd", soft_rows, values_all, preferred_element_type=jnp.float32
        ).astype(jnp.bfloat16)
        log_totals = (highest + jnp.log(totals))[:, :, 0].T
        return (context_rows, log_totals)

    context_blocks, log_blocks = lax.map(forward_block, jnp.arange(block_total, dtype=jnp.int32))
    context = context_blocks.reshape(seq_len, heads_here * HD)
    log_sums = log_blocks.reshape(seq_len, heads_here)
    context_rows = context
    branch = lax.psum_scatter(
        jnp.dot(context_rows, out_weight, preferred_element_type=jnp.float32)
        + jnp.dot(hidden, down_weight, preferred_element_type=jnp.float32),
        "tensor",
        scatter_dimension=0,
        tiled=True,
    )
    branch = branch + out_bias + down_bias
    residual_out = tokens.astype(jnp.float32) + branch
    mixed_out = residual_out.astype(jnp.bfloat16)
    forward_squares = jnp.stack([jnp.sum(residual_out * residual_out), jnp.sum(branch * branch)])
    forward_totals = lax.psum(forward_squares, ("dp", "tensor"))
    upstream = lax.all_gather(cotangent, "tensor", axis=0, tiled=True)
    out_weight_grad = jnp.einsum("sa,sd->ad", context, upstream, preferred_element_type=jnp.float32)
    down_weight_grad = jnp.einsum("sf,sd->fd", hidden, upstream, preferred_element_type=jnp.float32)
    context_grad = against(upstream, out_weight).astype(jnp.bfloat16)
    hidden_grad = against(upstream, down_weight)
    normal_cdf = 0.5 * (1.0 + lax.erf(preact * 0.5**0.5))
    density = jnp.exp(-0.5 * preact * preact) * (1.0 / math.sqrt(2.0 * math.pi))
    preact_grad = (hidden_grad * (normal_cdf + preact * density)).astype(jnp.bfloat16)
    context_grad3 = context_grad.reshape(seq_len, heads_here, HD)

    def backward_block(carried, number):
        key_grad, value_grad = carried
        offset = number * block_rows
        query_rows = lax.dynamic_slice_in_dim(queries, offset, block_rows, 0)
        grad_rows = lax.dynamic_slice_in_dim(context_grad3, offset, block_rows, 0)
        log_rows = lax.dynamic_slice_in_dim(log_sums, offset, block_rows, 0).T
        scores = (
            jnp.einsum("qhd,khd->hqk", query_rows, keys_all, preferred_element_type=jnp.float32)
            * score_scale
        )
        soft_full = jnp.exp(
            jnp.where(causal_mask(offset)[None], scores - log_rows[:, :, None], -1e30)
        )
        prob_grad = jnp.einsum(
            "qhd,khd->hqk", grad_rows, values_all, preferred_element_type=jnp.float32
        )
        deltas = jnp.sum(soft_full * prob_grad, axis=-1, keepdims=True)
        score_grad = (soft_full * (prob_grad - deltas)).astype(jnp.bfloat16)
        query_grad = (
            jnp.einsum("hqk,khd->qhd", score_grad, keys_all, preferred_element_type=jnp.float32)
            * score_scale
        )
        key_grad = (
            key_grad
            + jnp.einsum("hqk,qhd->khd", score_grad, query_rows, preferred_element_type=jnp.float32)
            * score_scale
        )
        value_grad = value_grad + jnp.einsum(
            "hqk,qhd->khd",
            soft_full.astype(jnp.bfloat16),
            grad_rows,
            preferred_element_type=jnp.float32,
        )
        return ((key_grad, value_grad), query_grad)

    empty = jnp.zeros((seq_len, heads_here, HD), jnp.float32)
    (key_grad, value_grad), query_blocks = lax.scan(
        backward_block, (empty, empty), jnp.arange(block_total, dtype=jnp.int32)
    )
    query_grad = unrotate(query_blocks.reshape(seq_len, heads_here, HD), cosine, sine_part)
    key_grad = unrotate(key_grad, cosine, sine_part)
    qkv_grad = (
        jnp.stack([query_grad, key_grad, value_grad], axis=2)
        .reshape(seq_len, 3 * heads_here * HD)
        .astype(jnp.bfloat16)
    )
    qkv_weight_grad = jnp.einsum(
        "sd,sc->dc", attention_input, qkv_grad, preferred_element_type=jnp.float32
    )
    qkv_bias_grad = jnp.sum(qkv_grad, axis=0, dtype=jnp.float32)
    up_weight_grad = jnp.einsum(
        "sd,sf->df", feed_input, preact_grad, preferred_element_type=jnp.float32
    )
    up_bias_grad = jnp.sum(preact_grad, axis=0, dtype=jnp.float32)
    own_normed, own_scale = normalize(tokens.astype(jnp.float32))
    attention_back = against(qkv_grad, qkv_weight)
    feed_back = against(preact_grad, up_weight)
    gain_terms = jnp.stack(
        [
            jnp.sum(normed * attention_back, axis=0),
            jnp.sum(attention_back, axis=0),
            jnp.sum(normed * feed_back, axis=0),
            jnp.sum(feed_back, axis=0),
        ]
    )
    normed_grad = lax.psum_scatter(
        (attention_back * gain_attn + feed_back * gain_mlp).astype(jnp.bfloat16),
        "tensor",
        scatter_dimension=0,
        tiled=True,
    ).astype(jnp.float32)
    centred_term = (
        normed_grad
        - jnp.mean(normed_grad, axis=-1, keepdims=True)
        - own_normed * jnp.mean(normed_grad * own_normed, axis=-1, keepdims=True)
    )
    input_grad = own_scale * centred_term + cotangent.astype(jnp.float32)
    (
        qkv_weight_grad,
        qkv_bias_grad,
        out_weight_grad,
        up_weight_grad,
        up_bias_grad,
        down_weight_grad,
    ) = lax.psum(
        (
            qkv_weight_grad,
            qkv_bias_grad,
            out_weight_grad,
            up_weight_grad,
            up_bias_grad,
            down_weight_grad,
        ),
        "dp",
    )
    bias_rows = jnp.sum(cotangent, axis=0, dtype=jnp.float32)
    grad_square = jnp.sum(input_grad * input_grad)
    gain_totals, bias_totals, grad_total = lax.psum(
        (gain_terms, bias_rows, grad_square), ("dp", "tensor")
    )
    square_totals = jnp.concatenate([forward_totals, grad_total[None]])
    elements = own_rows * model_width * lax.axis_size("dp") * lax.axis_size("tensor")
    statistics = jnp.sqrt(square_totals / elements)
    return (
        mixed_out,
        input_grad,
        gain_totals[0],
        gain_totals[1],
        gain_totals[2],
        gain_totals[3],
        qkv_weight_grad,
        qkv_bias_grad,
        out_weight_grad,
        bias_totals,
        up_weight_grad,
        up_bias_grad,
        down_weight_grad,
        bias_totals,
        statistics,
    )


F32 = jnp.float32
BF16 = jnp.bfloat16
MESH = pl.DeviceIdType.MESH
TILE = 256
PARTS = 4
TOGETHER = (1, 4, 1)
SPLIT = (1, 1, 1)


def ring_pieces(segments):
    return sum(2 * (PARTS // TOGETHER[number] * SPLIT[number]) for number in range(segments))


def dot_nn(left, right):
    return jnp.dot(left, right, preferred_element_type=F32)


def dot_nt(left, right):
    return lax.dot_general(left, right, (((1,), (1,)), ((), ())), preferred_element_type=F32)


def dot_tn(left, right):
    return lax.dot_general(left, right, (((0,), (0,)), ((), ())), preferred_element_type=F32)


def fused_kernel(
    ring,
    tok, cot, ga, ba, gm, bm, bo, bd, bqkv, bup, wqkv_h, wout_h, wup_h, wdn_h, cos_a, sin_a, cos_b, sin_b,
    mixed, igrad, GB, SUMS, SQO,
    T, CB, AI, FI, HID, GP, PG, QG, QH, KH, VH, CGH, CTXH, CTX, DQ, DKT, DVT, COS, SIN,
    WQKV, WOUT, WUP, WDN, RSB, PSD, PSC, PART, RA, RB, SV, ES, EX, EROWS, EY, SQ, EQ, EZ,
    lsem, g_s, g_r, r_s, r_r, b_s, b_r, e_s, e_r,
):
    rows = tok.shape[0]
    width = tok.shape[1]
    seq = T.shape[0]
    heads = QH.shape[0]
    hidden_width = WUP.shape[1]
    half_rows = rows // 2
    blocks = seq // TILE
    scale = HD ** (-0.5)
    dp = lax.axis_index("dp")
    t = lax.axis_index("tensor")
    core = lax.rem(t, 2)
    x = lax.div(t, 2)
    depth = ring // 2
    y = lax.rem(dp, 2)
    z = lax.div(dp, 2)
    at = z + y * (2 * depth - 1 - 2 * z)

    def ring_device(place):
        ny = lax.div(place, depth)
        return (2 * (place + ny * (2 * depth - 1 - 2 * place)) + ny, t)

    following = ring_device(lax.rem(at + 1, ring))
    previous = ring_device(lax.rem(at + ring - 1, ring))
    onward = (following, previous)
    core_mate = (dp, t + 1 - 2 * core)
    x_block = 2 * (1 - x) + core
    x_mate = (dp, x_block)

    def remote(src, dst, send, recv, device):
        return pltpu.make_async_remote_copy(
            src_ref=src, dst_ref=dst, send_sem=send, recv_sem=recv, device_id=device, device_id_type=MESH
        )

    def gather(which, kind):
        sems = (g_s.at[5 * which + kind], g_r.at[5 * which + kind])
        own = pl.ds(t * rows, rows)
        there = pl.ds(x_block * rows, rows)
        if which == 1:
            if kind == 0:
                return remote(CB.at[:, :, own], CB.at[:, :, own], *sems, core_mate)
            if kind <= PARTS:
                return remote(CB.at[kind - 1, :, own], CB.at[kind - 1, :, own], *sems, x_mate)
            piece = CB.at[kind - 1 - PARTS, :, there]
            return remote(piece, piece, *sems, core_mate)
        if kind == 0:
            return remote(tok, T.at[own], *sems, core_mate)
        if kind <= 2:
            off = (kind - 1) * half_rows
            return remote(tok.at[pl.ds(off, half_rows)], T.at[pl.ds(t * rows + off, half_rows)], *sems, x_mate)
        part = T.at[pl.ds(x_block * rows + (kind - 3) * half_rows, half_rows)]
        return remote(part, part, *sems, core_mate)

    kinds = (5, 1 + 2 * PARTS)

    def upstream_rows(here):
        return jnp.concatenate([CB[part, direction, here, :] for direction in range(2) for part in range(PARTS)], axis=1)

    local = [
        pltpu.make_async_copy(tok, T.at[pl.ds(t * rows, rows)], lsem.at[0]),
        pltpu.make_async_copy(wqkv_h, WQKV, lsem.at[2]),
        pltpu.make_async_copy(wup_h, WUP, lsem.at[3]),
        *(
            pltpu.make_async_copy(
                cot.at[:, pl.ds(direction * 512 + part * 128, 128)],
                CB.at[part, direction, pl.ds(t * rows, rows)],
                lsem.at[6 + 2 * part + direction],
            )
            for part in range(PARTS)
            for direction in range(2)
        ),
        pltpu.make_async_copy(wdn_h, WDN, lsem.at[4]),
        pltpu.make_async_copy(wout_h, WOUT, lsem.at[5]),
    ]
    barrier = pltpu.get_barrier_semaphore()
    for mate in (core_mate, x_mate, following, previous):
        pl.semaphore_signal(barrier, inc=1, device_id=mate, device_id_type=MESH)
    for copy in local:
        copy.start()
    pl.semaphore_wait(barrier, 4)
    gather(0, 1).start()
    gather(0, 2).start()
    gather(0, 0).start()

    @pl.loop(0, seq // 32)
    def _(a):
        ca, sa = cos_a[pl.ds(a, 1), :], sin_a[pl.ds(a, 1), :]
        cb, sb = cos_b[...], sin_b[...]
        COS[pl.ds(a * 32, 32), :] = ca * cb - sa * sb
        SIN[pl.ds(a * 32, 32), :] = sa * cb + ca * sb

    SV[...] = jnp.zeros_like(SV)
    SQ[...] = jnp.zeros_like(SQ)

    @pl.loop(0, heads)
    def _(h):
        DKT[h] = jnp.zeros(DKT.shape[1:], F32)
        DVT[h] = jnp.zeros(DVT.shape[1:], F32)


    def tables(base, group, count):
        lane = lax.broadcasted_iota(jnp.int32, (count, 128), 1)
        low_lane = jnp.where(lane >= 64, lane - 64, lane)
        cosine, sine = COS[pl.ds(base, count), :], SIN[pl.ds(base, count), :]
        if group == 1:
            cosine = jnp.where(lane >= 64, cosine, 1.0)
            sine = jnp.where(lane >= 64, sine, 0.0)
        if group == 2:
            cosine = jnp.where(lane < 64, cosine, 1.0)
            sine = jnp.where(lane < 64, sine, 0.0)
        upper = jnp.where(low_lane >= ROT // 2, sine, 0.0)
        return cosine, upper, sine - upper

    def norm_rows(base, count):
        raw = T[pl.ds(base, count), :].astype(F32)
        centred = raw - jnp.mean(raw, axis=1, keepdims=True)
        inverse_root = lax.rsqrt(jnp.mean(centred * centred, axis=1, keepdims=True) + epsilon)
        return centred * inverse_root, inverse_root

    def forward_block(block, half):
        base = pl.multiple_of(block * rows + half * half_rows, half_rows)

        @pl.loop(0, half_rows // 64)
        def _(part):
            off = pl.multiple_of(base + part * 64, 64)
            normed, _ = norm_rows(off, 64)
            AI[pl.ds(off, 64), :] = (normed * ga[...] + ba[...]).astype(BF16)
            FI[pl.ds(off, 64), :] = (normed * gm[...] + bm[...]).astype(BF16)

        for group in range(3 * heads // 2):
            if group % 2 == 0:
                columns = slice(group * 128, group * 128 + 256)
                pair = dot_nn(AI[pl.ds(base, half_rows), :], WQKV[:, columns]) + bqkv[columns].reshape(1, 256)
            value = pair[:, (group % 2) * 128 : (group % 2) * 128 + 128]
            cosine, upper, lower = tables(base, group % 3, half_rows)
            turned = (
                value * cosine
                - lower * pltpu.roll(value, 128 - ROT // 2, 1)
                + upper * pltpu.roll(value, ROT // 2, 1)
            ).astype(BF16)
            first = 2 * (group // 3)
            left, left_head = ((QH, first), (VH, first), (KH, first + 1))[group % 3]
            right, right_head = ((KH, first), (QH, first + 1), (VH, first + 1))[group % 3]
            left[left_head, pl.ds(base, half_rows), :] = turned[:, :HD]
            right[right_head, pl.ds(base, half_rows), :] = turned[:, HD:]

        for part in range(hidden_width // TILE):
            columns = slice(part * TILE, (part + 1) * TILE)
            preact = dot_nn(FI[pl.ds(base, half_rows), :], WUP[:, columns]) + bup[:, columns]
            cdf = 0.5 * (1.0 + lax.erf(preact * 0.5**0.5))
            density = jnp.exp(-0.5 * preact * preact) * (1.0 / math.sqrt(2.0 * math.pi))
            HID[pl.ds(base, half_rows), columns] = (preact * cdf).astype(BF16)
            GP[pl.ds(base, half_rows), columns] = cdf + preact * density

    def cotangent_block(block):
        base = pl.multiple_of(block * rows, rows)
        upstream = upstream_rows(pl.ds(base, rows))
        grad = dot_nt(upstream, WOUT[...]).astype(BF16)
        for h in range(heads):
            CGH[h, pl.ds(base, rows), :] = grad[:, h * HD : (h + 1) * HD]

        for part in range(hidden_width // TILE):
            columns = slice(part * TILE, (part + 1) * TILE)
            back = dot_nt(upstream, WDN[columns, :])
            rounded = (back * GP[pl.ds(base, rows), columns]).astype(BF16)
            PG[pl.ds(base, rows), columns] = rounded
            SV[6:7, columns] += jnp.sum(rounded.astype(F32), axis=0, keepdims=True)

    def attention_rows(h, own):
        here = slice(own * TILE, (own + 1) * TILE)
        before = own * TILE
        reach = before + TILE
        query = QH[h, here, :]
        grad = CGH[h, here, :]
        keys = KH[h, :reach, :]
        values = VH[h, :reach, :]
        scores = dot_nt(query, keys) * scale
        row_at = lax.broadcasted_iota(jnp.int32, (TILE, TILE), 0)
        column_at = lax.broadcasted_iota(jnp.int32, (TILE, TILE), 1)
        corner = jnp.where(column_at <= row_at, scores[:, before:], -1e30)
        scores = jnp.concatenate([scores[:, :before], corner], axis=1) if own else corner
        weights = jnp.exp(scores - jnp.max(scores, axis=1, keepdims=True))
        probs = weights * (1.0 / jnp.sum(weights, axis=1, keepdims=True))
        soft = probs.astype(BF16)
        CTXH[h, here, :] = dot_nn(soft, values).astype(BF16)
        prob_grad = dot_nt(grad, values)
        delta = jnp.sum(probs * prob_grad, axis=1, keepdims=True)
        score_grad = (probs * (prob_grad - delta)).astype(BF16)
        DQ[h, here, :] = scale * dot_nn(score_grad, keys)
        DKT[h, :, :reach] += dot_nn(query.astype(F32).T.astype(BF16), score_grad)
        DVT[h, :, :reach] += dot_nn(grad.astype(F32).T.astype(BF16), soft)

    def attention_unit(unit):
        h = lax.div(unit, blocks)
        for number, own in enumerate(sorted(range(blocks), key=lambda own: min(own, blocks - 1 - own))):
            pl.when(lax.rem(unit, blocks) == number)(functools.partial(attention_rows, h, own))

    def assemble(block):
        base = pl.multiple_of(block * TILE, TILE)
        here = pl.ds(base, TILE)
        for pair in range(heads // 2):
            one, two = 2 * pair, 2 * pair + 1
            CTX[here, pair * 128 : (pair + 1) * 128] = jnp.concatenate(
                [CTXH[one, here, :], CTXH[two, here, :]], axis=1
            )
            parts = [
                (DQ[one, here, :], scale * DKT[one, :, here].T),
                (DVT[one, :, here].T, DQ[two, here, :]),
                (scale * DKT[two, :, here].T, DVT[two, :, here].T),
            ]
            for group, (left, right) in enumerate(parts):
                grad = jnp.concatenate([left, right], axis=1)
                cosine, upper, lower = tables(base, group, TILE)
                turned = (
                    grad * cosine
                    + pltpu.roll(grad * upper, 128 - ROT // 2, 1)
                    - pltpu.roll(grad * lower, ROT // 2, 1)
                ).astype(BF16)
                columns = slice((3 * pair + group) * 128, (3 * pair + group + 1) * 128)
                QG[here, columns] = turned
                SV[7:8, columns] += jnp.sum(turned.astype(F32), axis=0, keepdims=True)

    def order(step):
        flip_core = 1 - lax.div(step, 2)
        flip_x = 1 - lax.rem(step, 2)
        return 2 * lax.rem(x + flip_x, 2) + lax.rem(core + flip_core, 2)

    def to_core(which, slot):
        block = (2 * x + 1 - core) if slot == 0 else (2 * (1 - x) + 1 - core)
        return remote(
            PART.at[which, pl.ds(block * rows, rows)], RA.at[which, slot],
            b_s.at[which, slot], b_r.at[which, slot], core_mate,
        )

    def to_x(which):
        return remote(
            PART.at[which, pl.ds(x_block * rows, rows)], RB.at[which],
            b_s.at[which, 2], b_r.at[which, 2], x_mate,
        )

    def send_after(which, step):
        @pl.when(step == 0)
        def _():
            to_core(which, 1).start()

        @pl.when(step == 1)
        def _():
            to_core(which, 0).start()

    def branch_block(step):
        base = pl.multiple_of(order(step) * rows, rows)
        here = pl.ds(base, rows)

        for part in range(width // TILE):
            columns = slice(part * TILE, (part + 1) * TILE)
            PART[0, here, columns] = (
                dot_nn(CTX[here, :], WOUT[:, columns]) + dot_nn(HID[here, :], WDN[:, columns])
            ).astype(BF16)

        send_after(0, step)

    def back_block(step):
        base = pl.multiple_of(order(step) * rows, rows)
        here = pl.ds(base, rows)
        raw = T[here, :].astype(F32)
        average = jnp.mean(raw, axis=1, keepdims=True)
        spread = jnp.mean((raw - average) * (raw - average), axis=1, keepdims=True)
        inverse_root = lax.rsqrt(spread + epsilon)

        for part in range(width // TILE):
            columns = slice(part * TILE, (part + 1) * TILE)
            normed = (T[here, columns].astype(F32) - average) * inverse_root
            attention_back = dot_nt(QG[here, :], WQKV[columns, :])
            feed_back = dot_nt(PG[here, :], WUP[columns, :])
            SV[0:1, columns] += jnp.sum(normed * attention_back, axis=0, keepdims=True)
            SV[1:2, columns] += jnp.sum(attention_back, axis=0, keepdims=True)
            SV[2:3, columns] += jnp.sum(normed * feed_back, axis=0, keepdims=True)
            SV[3:4, columns] += jnp.sum(feed_back, axis=0, keepdims=True)
            PART[1, here, columns] = (attention_back * ga[:, columns] + feed_back * gm[:, columns]).astype(BF16)

        send_after(1, step)

    def chip_sum(which):
        to_core(which, 1).wait_recv()
        there = pl.ds(pl.multiple_of(x_block * rows, rows), rows)
        PART[which, there, :] = (PART[which, there, :].astype(F32) + RA[which, 1].astype(F32)).astype(BF16)
        to_x(which).start()

    def finish_start():
        for which in range(2):
            to_core(which, 0).wait_recv()
            to_x(which).wait_recv()
    def total(which, off):
        return (
            PART[which, pl.ds(pl.multiple_of(t * rows + off, 32), 32), :].astype(F32)
            + RA[which, 0, pl.ds(off, 32), :].astype(F32)
            + RB[which, pl.ds(off, 32), :].astype(F32)
        )

    def square(value):
        return jnp.sum(jnp.sum(value * value, axis=1, keepdims=True), axis=0, keepdims=True)

    def finish_part(number):
        off = pl.multiple_of(number * 32, 32)
        here = pl.ds(pl.multiple_of(t * rows + off, 32), 32)
        branch = total(0, off) + bo[...] + bd[...]
        residual = T[here, :].astype(F32) + branch
        mixed[pl.ds(off, 32), :] = residual.astype(BF16)
        normed, inverse_root = norm_rows(t * rows + off, 32)
        grad = total(1, off)
        grad = inverse_root * (
            grad
            - jnp.mean(grad, axis=1, keepdims=True)
            - normed * jnp.mean(grad * normed, axis=1, keepdims=True)
        ) + upstream_rows(here).astype(F32)
        igrad[pl.ds(off, 32), :] = grad
        spot = lax.broadcasted_iota(jnp.int32, SQ.shape, 1)
        for place, value in enumerate((residual, branch, grad)):
            SQ[...] += jnp.where(spot == place, square(value), 0.0)

    members = (4, ring, ring, 4, ring)

    def share(stage, offset):
        over_tensor = stage in (0, 3)
        mate = (dp, lax.rem(t + offset, 4)) if over_tensor else (lax.rem(dp + offset, ring), t)
        src, dst = (
            lambda: (ES, EX.at[t]),
            lambda: (EROWS.at[lax.rem(dp + offset, ring)], EY.at[dp]),
            lambda: (SUMS.at[dp], SUMS.at[dp]),
            lambda: (EQ.at[0], EZ.at[t]),
            lambda: (EQ.at[1], EZ.at[4 + dp]),
        )[stage]()
        return remote(src, dst, e_s.at[stage], e_r.at[stage], mate)

    def share_start(stage):
        for offset in range(1, members[stage]):
            share(stage, offset).start()

    def share_all(stage):
        ref, first = ((EX, 0), (EY, 0), (SUMS, 0), (EZ, 0), (EZ, 4))[stage]
        whole = ref.at[pl.ds(first, members[stage] - 1)]
        return remote(whole, whole, e_s.at[stage], e_r.at[stage], core_mate)

    def share_wait(stage):
        share_all(stage).wait_recv()

    def added(ref, first, count):
        total = ref[first]
        for number in range(1, count):
            total = total + ref[first + number]
        return total

    def share_tensor():
        ES[...] = SV[...]
        EX[t] = SV[...]
        share_start(0)

    def share_rows():
        share_wait(0)
        row = lax.broadcasted_iota(jnp.int32, SV.shape, 0)
        total = jnp.where(row < 5, added(EX, 0, 4), SV[...])
        for place in range(ring):
            EROWS[:, place, :] = total[:, place * 128 : (place + 1) * 128]
        EY[dp] = EROWS[dp]
        share_start(1)

    def share_gather():
        share_wait(1)
        SUMS[dp] = added(EY, 0, ring)
        share_start(2)

    def share_squares():
        EQ[0] = SQ[...]
        EZ[t] = SQ[...]
        share_start(3)

    def share_squares_dp():
        share_wait(3)
        total = added(EZ, 0, 4)
        EQ[1] = total
        EZ[4 + dp] = total
        share_start(4)

    def share_end():
        share_wait(2)
        share_wait(4)
        SQO[...] = added(EZ, 4, ring)

    def chunk(direction, step):
        return lax.rem(at + ring - step, ring) if direction == 0 else lax.rem(at + step, ring)

    def gathered(direction, step):
        return lax.rem(at + 1 + ring - step, ring) if direction == 0 else lax.rem(at + ring - 1 + step, ring)

    def left_of(segment, direction, step):
        columns = pl.ds(pl.multiple_of(chunk(direction, step) * 128, 128), 128)
        return (HID, FI, AI)[segment][:, columns]

    def own_piece(step, part):
        for direction in range(2):
            PSD[lax.rem(step, PARTS), direction, :, part * 128 : (part + 1) * 128] = dot_tn(
                left_of(0, direction, step), CB[part, direction]
            )

    def own_down(step):
        for direction in range(2):
            right = jnp.concatenate([CB[part, direction] for part in range(PARTS)], axis=1)
            PSD[lax.rem(step, PARTS), direction] = dot_tn(left_of(0, direction, step), right)

    def own_partial(segment, step):
        for direction in range(2):
            left = left_of(segment, direction, step)
            if segment == 1:
                PSC[direction] = dot_tn(left, PG[:, direction * 512 : (direction + 1) * 512])
            else:
                number = chunk(direction, step)
                PSC[direction, :, 0:384] = dot_tn(left, QG[:, direction * 384 : (direction + 1) * 384])
                PSC[direction, :, 384:512] = dot_tn(
                    CTX[:, direction * 128 : (direction + 1) * 128], CB[lax.rem(number, PARTS), lax.div(number, PARTS)]
                )

    def parts_of(segment, piece):
        return pl.ds(piece // SPLIT[segment] * TOGETHER[segment], TOGETHER[segment])

    def rows_of(segment, piece):
        count = 128 // SPLIT[segment]
        return slice(piece % SPLIT[segment] * count, (piece % SPLIT[segment] + 1) * count)

    def sems_of(segment, direction, piece, step):
        number = ring_pieces(segment) + direction * (PARTS // TOGETHER[segment] * SPLIT[segment]) + piece
        return r_s.at[number], r_r.at[number * ring + lax.rem(step, ring)]

    def scatter(segment, direction, piece, step):
        parts, here = parts_of(segment, piece), rows_of(segment, piece)
        return remote(
            RSB.at[segment, direction, parts, step, here], RSB.at[segment, direction, parts, step + 1, here],
            *sems_of(segment, direction, piece, step), onward[direction],
        )

    def collect(segment, direction, piece, step):
        block = GB.at[segment, direction, parts_of(segment, piece), gathered(direction, step), rows_of(segment, piece)]
        return remote(
            block, block, *sems_of(segment, direction, piece, ring - 1 + step), onward[direction]
        )

    turns = ring - 1

    def during(condition, work):
        pl.when(condition)(work)

    def pieces(segment, parts=None):
        parts = range(PARTS // TOGETHER[segment] * SPLIT[segment]) if parts is None else parts
        return [(piece, direction) for piece in parts for direction in range(2)]

    def members_of(segment, piece):
        first = piece // SPLIT[segment] * TOGETHER[segment]
        return range(first, first + TOGETHER[segment])

    def term(segment, direction, part, step, here):
        columns = slice(part * 128, (part + 1) * 128)
        if segment == 0:
            return PSD[lax.rem(step, PARTS), direction, here, columns]
        return PSC[direction, here, columns]

    def sent(segment, direction, piece):
        scatter(segment, direction, piece, 0).wait_send()

    def ring_open(segment, parts=None):
        for piece, direction in pieces(segment, parts):
            here = rows_of(segment, piece)
            for part in members_of(segment, piece):
                RSB[segment, direction, part, 0, here] = term(segment, direction, part, 0, here).astype(BF16)
            scatter(segment, direction, piece, 0).start()

    def ring_scatter(segment, step, parts=None):
        for piece, direction in pieces(segment, parts):
            here = rows_of(segment, piece)
            scatter(segment, direction, piece, step - 1).wait_recv()
            for part in members_of(segment, piece):
                RSB[segment, direction, part, step, here] = (
                    RSB[segment, direction, part, step, here].astype(F32) + term(segment, direction, part, step, here)
                ).astype(BF16)
            sent(segment, direction, piece)
            scatter(segment, direction, piece, step).start()

    def ring_turn(segment, parts=None):
        last = ring - 1
        for piece, direction in pieces(segment, parts):
            here = rows_of(segment, piece)
            scatter(segment, direction, piece, last - 1).wait_recv()
            for part in members_of(segment, piece):
                GB[segment, direction, part, gathered(direction, 0), here] = (
                    RSB[segment, direction, part, last, here].astype(F32) + term(segment, direction, part, last, here)
                ).astype(BF16)
            sent(segment, direction, piece)
            collect(segment, direction, piece, 0).start()

    def ring_collect(segment, step, parts=None):
        for piece, direction in pieces(segment, parts):
            collect(segment, direction, piece, step - 1).wait_recv()
            sent(segment, direction, piece)
            collect(segment, direction, piece, step).start()

    def ring_close(segment, parts=None):
        for piece, direction in pieces(segment, parts):
            collect(segment, direction, piece, ring - 2).wait_recv()
            sent(segment, direction, piece)

    def down_terms(slot):
        during((slot >= PARTS) & (slot <= turns), lambda: own_down(slot))
        for part in range(PARTS):
            event = slot - part
            during((event > 0) & (event < PARTS), lambda: own_piece(event, part))

    def down_slot(slot):
        for part in range(PARTS):
            event = slot - part
            during(event < turns, lambda: ring_scatter(0, event, (part,)))
            during(event == turns, lambda: ring_turn(0, (part,)))
            during((event > turns) & (event < 2 * turns), lambda: ring_collect(0, event - turns, (part,)))
            during(event == 2 * turns, lambda: ring_close(0, (part,)))
        down_terms(slot + 1)

    for copy in local[:3]:
        copy.wait()

    def place_of(step):
        return 2 * lax.rem(x + lax.div(step, 2), 2) + lax.rem(core + lax.rem(step, 2), 2)

    @pl.loop(0, 8)
    def _(step):
        @pl.when(step == 1)
        def _():
            for copy in local[3:]:
                copy.wait()
            for kind in range(PARTS + 1):
                gather(1, kind).start()

        @pl.when(step == 2)
        def _():
            gather(0, 0).wait_recv()

        for half in range(2):

            @pl.when(step == 4 + 2 * half)
            def _():
                gather(0, 1 + half).wait_recv()
                gather(0, 3 + half).start()

            @pl.when(step == 5 + 2 * half)
            def _():
                gather(0, 3 + half).wait_recv()

        late = lax.div(step, 4)
        block = place_of(2 * late + jnp.where(late == 1, lax.rem(step, 2), lax.div(step, 2)))
        forward_block(block, jnp.where(late == 1, lax.div(step - 4, 2), lax.rem(step, 2)))

        @pl.when(step == 5)
        def _():
            cotangent_block(place_of(0))

    gather(1, 0).wait_recv()
    for slot in range(PARTS):
        gather(1, 1 + slot).wait_recv()
        gather(1, 1 + PARTS + slot).start()
        for part in range(slot):
            ring_scatter(0, slot - part, (part,))
        gather(1, 1 + PARTS + slot).wait_recv()
        both = dot_tn(left_of(0, 0, 0), jnp.concatenate([CB[slot, 0], CB[slot, 1]], axis=1))
        for direction in range(2):
            PSD[0, direction, :, slot * 128 : (slot + 1) * 128] = both[:, direction * 128 : (direction + 1) * 128]
        ring_open(0, (slot,))
        if slot == PARTS - 1:
            down_terms(PARTS)
        else:
            for part in range(slot + 1):
                own_piece(slot + 1 - part, part)
        if slot == 0:
            cotangent_block(place_of(1))

    cotangent_block(place_of(2))
    down_slot(4)
    cotangent_block(place_of(3))
    own_partial(1, 0)
    ring_open(1)

    def advance(segment, step):
        @pl.when(step <= turns)
        def _():
            own_partial(segment, step)

        during(step < turns, lambda: ring_scatter(segment, step))
        during(step == turns, lambda: ring_turn(segment))
        during(step > turns, lambda: ring_collect(segment, step - turns))

    units = heads * blocks

    @pl.loop(0, 12)
    def _(half):
        slot = 5 + lax.div(half, 2)
        during(lax.rem(half, 2) == 0, lambda: down_slot(slot))
        during(lax.rem(half, 2) == 1, lambda: advance(1, slot - 4))
        first = 3 * lax.div(half, 2) + 2 * lax.rem(half, 2)

        @pl.loop(jnp.minimum(first, units), jnp.minimum(first + 2 - lax.rem(half, 2), units))
        def _(unit):
            attention_unit(unit)

    @pl.loop(0, blocks)
    def _(block):
        during(block == 0, lambda: down_slot(11))
        during(block == 2, lambda: advance(1, turns))
        assemble(block)

    own_partial(2, 0)
    ring_open(2)
    SV[4:5, :] = jnp.sum(upstream_rows(pl.ds(t * rows, rows)).astype(F32), axis=0, keepdims=True)

    @pl.loop(0, 12)
    def _(half):
        slot = 12 + lax.div(half, 2)
        during(half == 2, lambda: chip_sum(0))
        during(half == 4, lambda: chip_sum(1))
        during(half == 5, share_tensor)
        during(lax.rem(half, 2) == 0, lambda: down_slot(slot))

        @pl.when(lax.rem(half, 2) == 1)
        def _():
            ring_collect(1, slot - 11)
            own_partial(2, slot - 11)
            ring_scatter(2, slot - 11)

        @pl.when(half < 2)
        def _():
            @pl.loop(2 * half, 2 * half + 2)
            def _(number):
                branch_block(number)

        @pl.when((half >= 2) & (half < 4))
        def _():
            @pl.loop(2 * half - 4, 2 * half - 2)
            def _(number):
                back_block(number)

        during(half == 8, finish_start)

        @pl.when(half >= 8)
        def _():
            @pl.loop(2 * half - 16, 2 * half - 14)
            def _(number):
                finish_part(number)

    ring_close(1)

    def advance_last(step, parts):
        during(step == turns, lambda: ring_turn(2, parts))
        during(step > turns, lambda: ring_collect(2, step - turns, parts))

    own_partial(2, turns)

    @pl.loop(turns, 2 * turns)
    def _(step):
        for side in range(2):
            count = PARTS * SPLIT[2] // 2
            advance_last(step, range(side * count, (side + 1) * count))

        during(step == 7, share_rows)
        during(step == 10, share_gather)
        during(step == 8, share_squares)
        during(step == 11, share_squares_dp)

    ring_close(2)
    share_end()

    for which in range(2):
        for kind in range(kinds[which]):
            gather(which, kind).wait_send()
        for slot in range(2):
            to_core(which, slot).wait_send()
        to_x(which).wait_send()
    for stage in range(5):
        share_all(stage).wait_send()


def angle_parts(seq_len):
    inverse = 10000.0 ** (-(np.arange(ROT // 2) * 2.0 / ROT))
    per_lane = np.zeros((128,))
    for start in (0, ROT // 2, HD, HD + ROT // 2):
        per_lane[start : start + ROT // 2] = inverse
    coarse = (np.arange(seq_len // 32) * 32.0)[:, None] * per_lane[None, :]
    fine = np.arange(32.0)[:, None] * per_lane[None, :]
    return [f(a).astype(np.float32) for a in (coarse, fine) for f in (np.cos, np.sin)]


def per_device_fused(
    tokens, cotangent, gain_attn, bias_attn, gain_mlp, bias_mlp, qkv_weight, qkv_bias,
    out_weight, out_bias, up_weight, up_bias, down_weight, down_bias,
):
    rows, width = tokens.shape
    ring = lax.axis_size("dp")
    seq = rows * lax.axis_size("tensor")
    heads = out_weight.shape[0] // HD
    hidden_width = up_weight.shape[1]
    qkv_width = qkv_weight.shape[1]
    cos_a, sin_a, cos_b, sin_b = angle_parts(seq)
    vmem = pl.BlockSpec(memory_space=pltpu.VMEM)
    hbm = pl.BlockSpec(memory_space=pl.ANY)
    V = pltpu.VMEM
    D = pltpu.SemaphoreType.DMA
    scratch = [
        V((seq, width), BF16), V((PARTS, 2, seq, 128), BF16), V((seq, width), BF16), V((seq, width), BF16),
        V((seq, hidden_width), BF16), V((seq, hidden_width), F32), V((seq, hidden_width), BF16),
        V((seq, qkv_width), BF16),
        V((heads, seq, HD), BF16), V((heads, seq, HD), BF16), V((heads, seq, HD), BF16),
        V((heads, seq, HD), BF16), V((heads, seq, HD), BF16), V((seq, heads * HD), BF16),
        V((heads, seq, HD), F32), V((heads, HD, seq), F32), V((heads, HD, seq), F32),
        V((seq, 128), F32), V((seq, 128), F32),
        V(qkv_weight.shape, BF16), V(out_weight.shape, BF16), V(up_weight.shape, BF16), V(down_weight.shape, BF16),
        V((3, 2, PARTS, ring, 128, 128), BF16), V((PARTS, 2, 128, 512), F32), V((2, 128, 512), F32),
        V((2, seq, width), BF16), V((2, 2, rows, width), BF16), V((2, rows, width), BF16),
        V((8, width), F32), V((8, width), F32), V((4, 8, width), F32),
        V((ring, 8, 128), F32), V((ring, 8, 128), F32), V((8, 128), F32),
        V((2, 8, 128), F32), V((4 + ring, 8, 128), F32),
        D((6 + 2 * PARTS,)), D((6 + 2 * PARTS,)), D((6 + 2 * PARTS,)),
        D((ring_pieces(3),)), D((ring_pieces(3) * ring,)),
        D((2, 3)), D((2, 3)), D((5,)), D((5,)),
    ]
    mixed, input_grad, gradients, sums, squares = pl.pallas_call(
        functools.partial(fused_kernel, ring),
        out_shape=[
            V((rows, width), BF16),
            V((rows, width), F32),
            V((3, 2, PARTS, ring, 128, 128), BF16),
            V((ring, 8, 128), F32),
            V((8, 128), F32),
        ],
        in_specs=[hbm, hbm] + [vmem] * 8 + [hbm] * 4 + [vmem] * 4,
        out_specs=[vmem] * 5,
        scratch_shapes=scratch,
        compiler_params=pltpu.CompilerParams(
            collective_id=0, has_side_effects=True, vmem_limit_bytes=VMEM_LIMIT
        ),
        name="layer",
    )(
        tokens, cotangent,
        *(v.reshape(1, -1) for v in (gain_attn, bias_attn, gain_mlp, bias_mlp, out_bias, down_bias)),
        qkv_bias, up_bias.reshape(1, -1),
        qkv_weight, out_weight, up_weight, down_weight, cos_a, sin_a, cos_b, sin_b,
    )
    elements = rows * width * ring * lax.axis_size("tensor")
    return closing(
        mixed, input_grad, gradients, sums, squares, elements, down_weight, up_weight, qkv_weight, out_weight
    )


def closing_kernel(
    elements,
    mixed, igrad, GB, SUMS, SQUARES,
    mixed_o, igrad_o, ga_o, ba_o, gm_o, bm_o, gq_o, bqkv_o, go_o, bo_o, gu_o, bup_o, gd_o, bd_o, stats_o,
    SD, SU, SQ, SO, sems, msem,
):
    copies = [
        pltpu.make_async_copy(mixed, mixed_o, msem.at[0]),
        pltpu.make_async_copy(igrad, igrad_o, msem.at[1]),
    ]
    for copy in copies:
        copy.start()
    for segment, stage in enumerate((SD, SU, SQ)):
        for number in range(GB.shape[3]):
            there = slice(number * 128, number * 128 + 128)
            for direction in range(2):
                for part in range(PARTS):
                    piece = GB[segment, direction, part, number].astype(F32)
                    if segment == 2 and part == 3:
                        SO[direction * 128 : direction * 128 + 128, there] = piece
                    else:
                        column = direction * (384 if segment == 2 else 512) + part * 128
                        stage[there, column : column + 128] = piece
            rows = pl.ds(number * 128, 128)
            copy = pltpu.make_async_copy(
                stage.at[rows], (gd_o, gu_o, gq_o)[segment].at[rows], sems.at[segment, number]
            )
            copy.start()
            copies.append(copy)
    copies.append(pltpu.make_async_copy(SO, go_o, msem.at[2]))
    copies[-1].start()
    for row, out in ((0, ga_o), (1, ba_o), (2, gm_o), (3, bm_o), (4, bo_o), (4, bd_o), (6, bup_o)):
        for place in range(SUMS.shape[1]):
            out[:, place * 128 : (place + 1) * 128] = SUMS[row, place : place + 1, :]
    for place in range(bqkv_o.shape[0] // 128):
        bqkv_o[place * 128 : (place + 1) * 128] = SUMS[7, place, :]
    stats_o[...] = jnp.sqrt(SQUARES[0, : stats_o.shape[0]] * (1.0 / elements))
    for copy in copies:
        copy.wait()


def closing(mixed, input_grad, gradients, sums, squares, elements, down_weight, up_weight, qkv_weight, out_weight):
    hbm = pl.BlockSpec(memory_space=pl.ANY)
    vmem = pl.BlockSpec(memory_space=pltpu.VMEM)

    def like(array, dtype=F32):
        return jax.ShapeDtypeStruct(array.shape, dtype)

    width = mixed.shape[1]
    row = jax.ShapeDtypeStruct((1, width), F32)
    outs = pl.pallas_call(
        functools.partial(closing_kernel, elements),
        in_specs=[vmem] * 5,
        out_specs=[
            hbm, hbm, vmem, vmem, vmem, vmem, hbm, vmem, hbm, vmem, hbm, vmem, hbm, vmem, vmem,
        ],
        out_shape=[
            like(mixed, BF16), like(input_grad), row, row, row, row,
            like(qkv_weight), jax.ShapeDtypeStruct((qkv_weight.shape[1],), F32), like(out_weight), row,
            like(up_weight), row, like(down_weight), row, jax.ShapeDtypeStruct((3,), F32),
        ],
        scratch_shapes=[
            pltpu.VMEM(down_weight.shape, F32),
            pltpu.VMEM(up_weight.shape, F32),
            pltpu.VMEM(qkv_weight.shape, F32),
            pltpu.VMEM(out_weight.shape, F32),
            pltpu.SemaphoreType.DMA((3, gradients.shape[3])),
            pltpu.SemaphoreType.DMA((3,)),
        ],
        compiler_params=pltpu.CompilerParams(vmem_limit_bytes=24 << 20),
        name="outputs",
    )(mixed, input_grad, gradients, sums, squares)
    return tuple(out.reshape(-1) if out.shape == (1, width) else out for out in outs)


def solution(mesh):
    in_specs = (
        P(("dp", "tensor"), None),
        P(("dp", "tensor"), None),
        P(),
        P(),
        P(),
        P(),
        P(None, "tensor"),
        P("tensor"),
        P("tensor", None),
        P(),
        P(None, "tensor"),
        P("tensor"),
        P("tensor", None),
        P(),
    )
    out_specs = (
        P(("dp", "tensor"), None),
        P(("dp", "tensor"), None),
        P(),
        P(),
        P(),
        P(),
        P(None, "tensor"),
        P("tensor"),
        P("tensor", None),
        P(),
        P(None, "tensor"),
        P("tensor"),
        P("tensor", None),
        P(),
        P(),
    )
    fused = mesh.shape["tensor"] == 4 and mesh.shape["dp"] == 8
    return jax.shard_map(
        per_device_fused if fused else per_device, mesh=mesh, in_specs=in_specs, out_specs=out_specs, check_vma=False
    )
```
